32 devices in a mesh: dp: 2 (over x), sp: 16 (over z, y, core).
Axes of the slice: x: 2, y: 2, z: 4, core: 2. Of those that a mesh axis runs over, the one named last changes fastest.
Arguments:
- tokens: bfloat16 [32768, 768], P(('dp', 'sp')), may hold values from -6 to 6
- condition: bfloat16 [4, 768], P('dp'), may hold values from -6 to 6
- patch_mask: int32 [4, 512], P('dp'), may hold values from 0 to 1, as said below
- grad_out: bfloat16 [32768, 768], P(('dp', 'sp')), may hold values from -6 to 6
- mod_weight: bfloat16 [768, 6912], P(('dp', 'sp')), may hold values from -0.21875 to 0.21875
- mod_bias: bfloat16 [6912], P(('dp', 'sp')), may hold values from -2 to 2
- space_qkv: bfloat16 [768, 2304], P(('dp', 'sp')), may hold values from -0.21875 to 0.21875
- space_proj: bfloat16 [768, 768], P(('dp', 'sp')), may hold values from -3 to 3
- time_qkv: bfloat16 [768, 2304], P(('dp', 'sp')), may hold values from -0.21875 to 0.21875
- time_proj: bfloat16 [768, 768], P(('dp', 'sp')), may hold values from -0.875 to 0.875
- mlp_in: bfloat16 [768, 3072], P(('dp', 'sp')), may hold values from -0.21875 to 0.21875
- in_bias: bfloat16 [3072], P(('dp', 'sp')), may hold values from -3 to 3
- mlp_out: bfloat16 [3072, 768], P(('dp', 'sp')), may hold values from -0.109375 to 0.109375
- out_bias: bfloat16 [768], P(('dp', 'sp')), may hold values from -3 to 3
Outputs:
- out_tokens: bfloat16 [32768, 768], P(('dp', 'sp'))
- grad_tokens: bfloat16 [32768, 768], P(('dp', 'sp'))
- grad_condition: float32 [4, 768], P('dp')
- grad_mod_weight: float32 [768, 6912], P(('dp', 'sp'))
- grad_mod_bias: float32 [6912], P(('dp', 'sp'))
- grad_space_qkv: float32 [768, 2304], P(('dp', 'sp'))
- grad_space_proj: float32 [768, 768], P(('dp', 'sp'))
- grad_time_qkv: float32 [768, 2304], P(('dp', 'sp'))
- grad_time_proj: float32 [768, 768], P(('dp', 'sp'))
- grad_mlp_in: float32 [768, 3072], P(('dp', 'sp'))
- grad_in_bias: float32 [3072], P(('dp', 'sp'))
- grad_mlp_out: float32 [3072, 768], P(('dp', 'sp'))
- grad_out_bias: float32 [768], P(('dp', 'sp'))
The draws below stay inside these ranges and needn't reach their ends.
Inputs may be any that keep to these rules, and one draw needn't show every extreme that they name: `patch_mask`: each clip's mask is 1 on a prefix of its 512 slots and 0 after it, the same for all frames of the clip; the prefix holds a multiple of 64 slots, at least 64; some clip has padding.
All inputs are finite; a program needn't handle non-finite values.
Results may differ from the reference program's by a relative error of at most 0.018.
Values may be sent and summed in bfloat16 or wider, within the bound.
No kernel may reach another device: no remote copies, remote signals or barrier semaphores. Data moves between devices by JAX's collectives and lax.ppermute only.
A program may use at most 256 MiB of HBM per device.

```python
import jax
import jax.numpy as jnp
from jax import lax

D = 768
HEADS = 12
HEAD_DIM = 64
FF = 3072
FRAMES = 16
PATCHES = 512
CLIPS = 4
TOKENS = 32768


def draw_patch_mask(key, part):
    steps = jax.random.randint(jax.random.fold_in(key, 11), (CLIPS,), 1, 9).astype(jnp.int32)
    chosen = jax.random.randint(jax.random.fold_in(key, 12), (), 0, CLIPS).astype(jnp.int32)
    indices = jnp.arange(CLIPS, dtype=jnp.int32)
    steps = jnp.where(indices == chosen, jnp.minimum(steps, 4), steps).astype(jnp.int32)
    counts = (steps * (PATCHES // 8)).astype(jnp.int32)
    places = jnp.arange(PATCHES, dtype=jnp.int32)
    return (places[None, :] < counts[:, None]).astype(jnp.int32)


def shard_levels(own_key, dims, shards, low, top_value):
    def one(dim, shards_of):
        draws = jax.random.uniform(jax.random.fold_in(jax.random.fold_in(own_key, 6), dim), (shards_of,), jnp.float32, low / len(shards), top_value / len(shards))
        return jnp.repeat(jnp.exp(draws), dims[dim] // shards_of).reshape((-1,) + (1,) * (len(dims) - dim - 1))

    loudness = one(*shards[0])
    for cut in shards[1:]:
        loudness = loudness * one(*cut)
    return loudness


def gaussian(own_key, shape, scale, limit, cuts=(), kind=jnp.bfloat16):
    array = scale * jax.random.normal(own_key, shape, jnp.float32)
    if cuts:
        array = array * shard_levels(own_key, shape, cuts, -0.22, 0.18)
    return jnp.clip(array, -limit, limit).astype(kind)


def setup_inputs(seed: int = 0) -> dict:
    arg_keys = jax.random.split(jax.random.key(seed), 15)
    tokens = gaussian(arg_keys[0], (TOKENS, D), 1.0, 6.0, ((0, 32),))
    condition = gaussian(arg_keys[1], (CLIPS, D), 1.0, 6.0, ((0, 2),))
    patch_mask = draw_patch_mask(jax.random.fold_in(arg_keys[14], 71), 0)
    grad_out = gaussian(arg_keys[3], (TOKENS, D), 1.0, 6.0, ((0, 32),))
    mod_weight = gaussian(arg_keys[4], (D, 9 * D), D ** -0.5, 0.21875, ((0, 32),))
    mod_bias = gaussian(arg_keys[5], (9 * D,), 0.3, 2.0, ((0, 32),))
    space_qkv = gaussian(arg_keys[6], (D, 3 * D), D ** -0.5, 0.21875, ((0, 32),))
    space_proj = gaussian(arg_keys[7], (D, D), (D // 192) ** -0.5, 3.0, ((0, 32),))
    time_qkv = gaussian(arg_keys[8], (D, 3 * D), D ** -0.5, 0.21875, ((0, 32),))
    time_proj = gaussian(arg_keys[9], (D, D), (D // 16) ** -0.5, 0.875, ((0, 32),))
    mlp_in = gaussian(arg_keys[10], (D, FF), D ** -0.5, 0.21875, ((0, 32),))
    in_bias = gaussian(arg_keys[11], (FF,), 0.5, 3.0, ((0, 32),))
    mlp_out = gaussian(arg_keys[12], (FF, D), FF ** -0.5, 0.109375, ((0, 32),))
    out_bias = gaussian(arg_keys[13], (D,), 0.5, 3.0, ((0, 32),))
    return {"tokens": tokens, "condition": condition, "patch_mask": patch_mask, "grad_out": grad_out, "mod_weight": mod_weight, "mod_bias": mod_bias, "space_qkv": space_qkv, "space_proj": space_proj, "time_qkv": time_qkv, "time_proj": time_proj, "mlp_in": mlp_in, "in_bias": in_bias, "mlp_out": mlp_out, "out_bias": out_bias}


@jax.custom_vjp
def low(v):
    return lax.optimization_barrier(v.astype(jnp.bfloat16)).astype(jnp.float32)

@jax.custom_vjp
def low_back(v):
    return v

def low_keep(v):
    return (low(v), None)

def low_pass(kept, grad):
    return (grad,)

def back_keep(v):
    return (v, None)

def back_low(kept, grad):
    return (low(grad),)
low.defvjp(low_keep, low_pass)
low_back.defvjp(back_keep, back_low)
EPSILON = 1e-06
MASKED = -10000.0
HIGHEST = lax.Precision.HIGHEST

def modulated(values, shift, scale):
    average = lax.optimization_barrier(jnp.mean(values, axis=-1, keepdims=True))
    centred = values - average
    normed = centred * lax.rsqrt(lax.optimization_barrier(jnp.mean(centred * centred, axis=-1, keepdims=True)) + EPSILON)
    return normed * (1.0 + scale) + shift

def layer(clip_tokens, clip_cond, key_bias, params):
    mod_weight, mod_bias, space_qkv, space_proj, time_qkv, time_proj, mlp_in, in_bias, mlp_out, out_bias = params
    lifted = low(jax.nn.silu(clip_cond))
    mod_rows = (jnp.dot(lifted, mod_weight, precision=HIGHEST) + mod_bias).reshape(9, -1)
    space_in = low(modulated(clip_tokens, mod_rows[0], mod_rows[1]))
    projected = low_back(low(jnp.dot(space_in, space_qkv, precision=HIGHEST)))
    projected = projected.reshape(FRAMES, PATCHES, 3, HEADS, HEAD_DIM)
    scores = jnp.einsum('fqhd,fkhd->fhqk', projected[:, :, 0], projected[:, :, 1], precision=HIGHEST)
    scores = low_back(scores * 0.125 + key_bias)
    softmaxed = low(jax.nn.softmax(scores, axis=-1))
    attended = jnp.einsum('fhqk,fkhd->fqhd', softmaxed, projected[:, :, 2], precision=HIGHEST)
    attended = low_back(low(attended)).reshape(FRAMES * PATCHES, -1)
    after_space = clip_tokens + mod_rows[2] * low_back(jnp.dot(attended, space_proj, precision=HIGHEST))
    time_in = low_back(low(modulated(after_space, mod_rows[3], mod_rows[4])))
    projected = low_back(low(jnp.dot(time_in, time_qkv, precision=HIGHEST)))
    projected = projected.reshape(FRAMES, PATCHES, 3, HEADS, HEAD_DIM)
    scores = jnp.einsum('fphd,gphd->phfg', projected[:, :, 0], projected[:, :, 1], precision=HIGHEST)
    scores = low_back(scores * 0.125)
    softmaxed = low(jax.nn.softmax(scores, axis=-1))
    attended = jnp.einsum('phfg,gphd->fphd', softmaxed, projected[:, :, 2], precision=HIGHEST)
    attended = low_back(low(attended)).reshape(FRAMES * PATCHES, -1)
    after_time = after_space + mod_rows[5] * low_back(jnp.dot(attended, time_proj, precision=HIGHEST))
    mlp_act = low(modulated(after_time, mod_rows[6], mod_rows[7]))
    hidden_pre = low_back(jnp.dot(mlp_act, mlp_in, precision=HIGHEST) + in_bias)
    hidden = low(jax.nn.gelu(hidden_pre, approximate=True))
    mlp_branch = low_back(jnp.dot(hidden, mlp_out, precision=HIGHEST) + out_bias)
    return after_time + mod_rows[8] * mlp_branch

def reference(tokens, condition, patch_mask, grad_out, mod_weight, mod_bias, space_qkv, space_proj, time_qkv, time_proj, mlp_in, in_bias, mlp_out, out_bias):
    params = tuple((member.astype(jnp.float32) for member in (mod_weight, mod_bias, space_qkv, space_proj, time_qkv, time_proj, mlp_in, in_bias, mlp_out, out_bias)))
    clips = condition.shape[0]
    width = tokens.shape[1]
    flattened = tokens.astype(jnp.float32).reshape(clips, FRAMES * PATCHES, width)
    cotangent = grad_out.astype(jnp.float32).reshape(clips, FRAMES * PATCHES, width)
    key_biases = jnp.where(patch_mask == 1, 0.0, MASKED).astype(jnp.float32)

    def one_clip(totals, sample):
        clip_tokens, clip_cond, key_bias, clip_grad = sample

        def forward(inputs, cond_row, weights):
            return layer(inputs, cond_row, key_bias, weights)
        result, pullback = jax.vjp(forward, clip_tokens, clip_cond, params)
        grad_inputs, grad_cond, grad_params = pullback(clip_grad)
        totals = jax.tree.map(jnp.add, totals, grad_params)
        return (totals, (result, grad_inputs, grad_cond))
    zeros = jax.tree.map(jnp.zeros_like, params)
    totals, stacked = lax.scan(one_clip, zeros, (flattened, condition.astype(jnp.float32), key_biases, cotangent))
    results, grad_inputs, grad_conds = stacked
    out_tokens = results.reshape(-1, width).astype(jnp.bfloat16)
    grad_tokens = grad_inputs.reshape(-1, width).astype(jnp.bfloat16)
    return (out_tokens, grad_tokens, grad_conds, totals[0], totals[1], totals[2], totals[3], totals[4], totals[5], totals[6], totals[7], totals[8], totals[9])
```

```python
import functools
import math

import jax
import jax.numpy as jnp
from jax import lax
from jax.experimental import pallas as pl
from jax.experimental.pallas import tpu as pltpu
from jax.sharding import PartitionSpec as P

HEADS = 12
HEAD_DIM = 64
FRAMES = 16
EPSILON = 1e-06
MASKED = -10000.0
APART = -1e30
AXES = ("dp", "sp")
F32 = jnp.float32
BF16 = jnp.bfloat16
MIB = 1 << 20


def swap(values, mask, count):
    return lax.ppermute(values, AXES, [(i, i ^ mask) for i in range(count)])


def chip_orders(count):
    bits = [1 << i for i in range(1, count.bit_length() - 1)]
    low, high, middle = bits[0], bits[-1], bits[1:-1][::-1]
    return (middle + [high, low], middle + [low, high])


def spread(shard, order, count):
    held = shard[None]
    for mask in order:
        held = jnp.concatenate([held, swap(held, mask, count)], axis=0)
    return held


def spread_places(order, count):
    places = []
    for distance in range(count // 2):
        places.append(sum(1 << s for s, mask in enumerate(order) if distance & (mask >> 1)))
    return places


def fold_places(order, count):
    steps = len(order)
    places = []
    for distance in range(count // 2):
        places.append(
            sum(1 << (steps - 1 - s) for s, mask in enumerate(order) if distance & (mask >> 1))
        )
    return places


def fold(keep, send, order, count):
    masks = [1] + list(order)
    for step, mask in enumerate(masks):
        got = swap(send, mask, count)
        if step == len(masks) - 1:
            return keep[0].astype(F32) + got[0].astype(F32)
        half = keep.shape[0] // 2
        low = (keep[:half].astype(F32) + got[:half].astype(F32)).astype(BF16)
        high = (keep[half:].astype(F32) + got[half:].astype(F32)).astype(BF16)
        keep, send = low, high


def clip_total(row, clip_dev, count):
    mask = clip_dev // 2
    while mask:
        row = row + swap(row, mask, count)
        mask //= 2
    return row


def clip_spread(row, clip_dev, count):
    mask = clip_dev
    while mask < count:
        row = jnp.concatenate([row, swap(row, mask, count)], axis=0)
        mask *= 2
    return row


def nn(a, b):
    return jnp.dot(a, b, preferred_element_type=F32)


def nt(a, b):
    return lax.dot_general(a, b, (((1,), (1,)), ((), ())), preferred_element_type=F32)


def tn(a, b):
    return lax.dot_general(a, b, (((0,), (0,)), ((), ())), preferred_element_type=F32)


def normalise(values):
    average = jnp.mean(values, axis=-1, keepdims=True)
    centred = values - average
    inverse = lax.rsqrt(jnp.mean(centred * centred, axis=-1, keepdims=True) + EPSILON)
    return centred * inverse, inverse


def norm_back(grad_mod, normed, inverse, scale):
    grad_normed = grad_mod * (1.0 + scale)
    inner = jnp.mean(grad_normed * normed, axis=-1, keepdims=True)
    average = jnp.mean(grad_normed, axis=-1, keepdims=True)
    return inverse * (grad_normed - average - normed * inner)


def column_sum(values):
    return jnp.sum(values, axis=0, keepdims=True)


def halves():
    lane = lax.broadcasted_iota(jnp.int32, (1, 2 * HEAD_DIM), 1)
    first = (lane < HEAD_DIM).astype(F32)
    return first.astype(BF16), (1.0 - first).astype(BF16)


def turned(values):
    return jnp.transpose(values.astype(F32), (1, 0))


def pair_forward(queries, keys, values, bias):
    values_t = turned(values).astype(BF16)
    parts = []
    totals = []
    for half, mask in enumerate(halves()):
        scores = nt(keys * mask, queries) * 0.125 + bias
        largest = jnp.max(scores, axis=0, keepdims=True)
        exponent = jnp.exp(scores - largest)
        denominator = jnp.sum(exponent, axis=0, keepdims=True)
        probable = (exponent * (1.0 / denominator)).astype(BF16)
        parts.append(nn(values_t[half * HEAD_DIM : (half + 1) * HEAD_DIM], probable))
        totals.append(largest + jnp.log(denominator))
    attended = jnp.transpose(jnp.concatenate(parts, axis=0), (1, 0)).astype(BF16)
    return attended, totals


def pair_back(queries, keys, values, grad, totals, bias):
    keys_t = turned(keys).astype(BF16)
    grad_queries = []
    grad_keys = 0.0
    grad_values = 0.0
    for half, mask in enumerate(halves()):
        scores = nt(keys * mask, queries) * 0.125 + bias
        probable = jnp.exp(scores - totals[half])
        grad_probs = nt(values * mask, grad)
        inner = jnp.sum(probable * grad_probs, axis=0, keepdims=True)
        grad_scores = (probable * (grad_probs - inner)).astype(BF16)
        grad_values = grad_values + nn(probable.astype(BF16), grad * mask)
        grad_keys = grad_keys + nn(grad_scores, queries * mask)
        grad_queries.append(nn(keys_t[half * HEAD_DIM : (half + 1) * HEAD_DIM], grad_scores))
    grad_queries = jnp.transpose(jnp.concatenate(grad_queries, axis=0), (1, 0))
    return (
        (grad_queries * 0.125).astype(BF16),
        (grad_keys * 0.125).astype(BF16),
        grad_values.astype(BF16),
    )


def whole(shape):
    return pl.BlockSpec(shape, lambda *_: (0,) * len(shape), pipeline_mode=pl.Buffered(1))


def whole_out(shape):
    return pl.BlockSpec(shape, lambda *_: (0,) * len(shape))


def params(limit=56):
    return pltpu.CompilerParams(vmem_limit_bytes=limit * MIB)


def cost(flops, moved, special=0):
    return pl.CostEstimate(flops=int(flops), bytes_accessed=int(moved), transcendentals=int(special))


def assemble(pieces, orders, layout, chip, core, count):
    chips = count // 2
    rows = pieces[0][0].shape[1]
    tables = jnp.stack(
        [jnp.array(spread_places(order, count), jnp.int32)[jnp.arange(chips) ^ chip] for order in orders]
        + [jnp.full((chips,), core, jnp.int32)]
    )

    def body(table, *refs):
        ins = refs[: 2 * len(pieces)]
        outs = refs[2 * len(pieces) :]

        def put(first, second):
            for out, runs in zip(outs, layout):
                start = 0
                for piece, column, width in runs:
                    cut = slice(column, column + width)
                    joined = jnp.concatenate(
                        [
                            ins[2 * piece + first][0, :, cut].astype(F32),
                            ins[2 * piece + second][0, :, cut].astype(F32),
                        ],
                        axis=0,
                    )
                    out[:, start : start + width] = joined.astype(BF16)
                    start += width

        even = table[len(pieces), 0] == 0

        @pl.when(even)
        def _():
            put(0, 1)

        @pl.when(jnp.logical_not(even))
        def _():
            put(1, 0)

    in_specs = []
    operands = []
    for index, (own, other) in enumerate(pieces):
        for part in (own, other):
            in_specs.append(
                pl.BlockSpec((1,) + part.shape[1:], lambda i, t, index=index: (t[index, i], 0, 0))
            )
            operands.append(part)
    widths = [sum(run[2] for run in runs) for runs in layout]
    return pl.pallas_call(
        body,
        grid_spec=pltpu.PrefetchScalarGridSpec(
            num_scalar_prefetch=1,
            grid=(chips,),
            in_specs=in_specs,
            out_specs=[pl.BlockSpec((2 * rows, w), lambda i, t: (i, 0)) for w in widths],
        ),
        out_shape=[jax.ShapeDtypeStruct((count * rows, w), BF16) for w in widths],
        compiler_params=params(),
        cost_estimate=cost(0, 4 * count * rows * sum(widths)),
        name="assemble",
    )(tables, *operands)


def weight_grads(groups, order, chip, core, count, block=768):
    chips = count // 2
    length = groups[0][0].shape[0]
    depth = groups[0][0].shape[1]
    share = depth // count
    steps = [g.shape[1] // block for _, g in groups]
    starts = [sum(steps[:i]) for i in range(len(steps))]
    total = sum(steps)
    k_block = min(depth, 768)
    k_steps = depth // k_block
    pairs = k_block // (2 * share)
    table = jnp.concatenate(
        [
            jnp.array(fold_places(order, count), jnp.int32)[jnp.arange(chips) ^ chip],
            jnp.full((1,), core, jnp.int32),
        ]
    )

    def body(table, *refs):
        keep, send = refs[2 * len(groups) :]
        j = pl.program_id(0)
        k = pl.program_id(1)
        odd = table[chips] == 1
        for index in range(len(groups)):

            @pl.when(jnp.logical_and(j >= starts[index], j < starts[index] + steps[index]))
            def _():
                product = tn(refs[2 * index][...], refs[2 * index + 1][...])
                for pair in range(pairs):
                    place = table[k * pairs + pair]
                    first = product[2 * pair * share : (2 * pair + 1) * share]
                    second = product[(2 * pair + 1) * share : (2 * pair + 2) * share]
                    keep[place] = jnp.where(odd, second, first).astype(BF16)
                    send[place] = jnp.where(odd, first, second).astype(BF16)

    in_specs = []
    operands = []
    for index, (acts, grads) in enumerate(groups):
        in_specs.append(pl.BlockSpec((length, k_block), lambda j, k, t: (0, k)))
        in_specs.append(
            pl.BlockSpec(
                (length, block),
                lambda j, k, t, s=starts[index], m=steps[index]: (0, jnp.clip(j - s, 0, m - 1)),
            )
        )
        operands += [acts, grads]
    out = jax.ShapeDtypeStruct((chips, share, total * block), BF16)
    out_spec = pl.BlockSpec((chips, share, block), lambda j, k, t: (0, 0, j))
    return pl.pallas_call(
        body,
        grid_spec=pltpu.PrefetchScalarGridSpec(
            num_scalar_prefetch=1,
            grid=(total, k_steps),
            in_specs=in_specs,
            out_specs=[out_spec, out_spec],
        ),
        out_shape=[out, out],
        compiler_params=params(),
        cost_estimate=cost(2 * length * depth * total * block, 4 * depth * total * block),
        name="weight_grads",
    )(table, *operands)


def space_project(tokens, mods, weight):
    length, width = tokens.shape
    wide = weight.shape[1]
    block = 256

    def body(tokens, mods, weight, act, packed):
        normed, _ = normalise(tokens[...].astype(F32))
        value = (normed * (1.0 + mods[1:2]) + mods[0:1]).astype(BF16)
        act[...] = value
        packed[...] = nn(value, weight[...]).astype(BF16)

    return pl.pallas_call(
        body,
        grid=(length // block,),
        in_specs=[
            pl.BlockSpec((block, width), lambda i: (i, 0)),
            whole(mods.shape),
            whole(weight.shape),
        ],
        out_specs=[
            pl.BlockSpec((block, width), lambda i: (i, 0)),
            pl.BlockSpec((block, wide), lambda i: (i, 0)),
        ],
        out_shape=[
            jax.ShapeDtypeStruct((length, width), BF16),
            jax.ShapeDtypeStruct((length, wide), BF16),
        ],
        compiler_params=params(),
        cost_estimate=cost(2 * length * width * wide, 10 * MIB),
        name="space_project",
    )(tokens, mods, weight)


def space_forward(packed, tokens, mods, bias, weight, patches, peers):
    length, width = tokens.shape
    frames = length // patches
    pairs = width // 128
    spots = patches // peers

    def body(queries, keys, values, tokens, mods, bias, weight, heads, totals, branch, after, kept):
        pair = pl.program_id(1)
        attended, logs = pair_forward(queries[...], keys[...], values[...], bias[...])
        heads[...] = attended
        totals[0, 0] = jnp.concatenate(logs, axis=0)
        kept[pair] = attended

        @pl.when(pair == pairs - 1)
        def _():
            joined = jnp.concatenate([kept[p] for p in range(pairs)], axis=1)
            product = nn(joined, weight[...])
            branch[...] = product.astype(BF16)
            result = (tokens[...].astype(F32) + mods[2:3] * product).astype(BF16)
            for peer in range(peers):
                after[peer, 0] = result[peer * spots : (peer + 1) * spots]

    return pl.pallas_call(
        body,
        grid=(frames, pairs),
        in_specs=[
            pl.BlockSpec((patches, 128), lambda f, p: (f, p)),
            pl.BlockSpec((patches, 128), lambda f, p: (f, pairs + p)),
            pl.BlockSpec((patches, 128), lambda f, p: (f, 2 * pairs + p)),
            pl.BlockSpec((patches, width), lambda f, p: (f, 0)),
            whole(mods.shape),
            whole(bias.shape),
            whole(weight.shape),
        ],
        out_specs=[
            pl.BlockSpec((patches, 128), lambda f, p: (f, p)),
            pl.BlockSpec((1, 1, 2, patches), lambda f, p: (f, p, 0, 0)),
            pl.BlockSpec((patches, width), lambda f, p: (f, 0)),
            pl.BlockSpec((peers, 1, spots, width), lambda f, p: (0, f, 0, 0)),
        ],
        out_shape=[
            jax.ShapeDtypeStruct((length, width), BF16),
            jax.ShapeDtypeStruct((frames, pairs, 2, patches), F32),
            jax.ShapeDtypeStruct((length, width), BF16),
            jax.ShapeDtypeStruct((peers, frames, spots, width), BF16),
        ],
        scratch_shapes=[pltpu.VMEM((pairs, patches, 128), BF16)],
        compiler_params=params(),
        cost_estimate=cost(10e9, 10 * MIB, 6e6),
        name="space_forward",
    )(packed, packed, packed, tokens, mods, bias, weight)


def space_branch_back(grad_after, branch, mods, weight, patches):
    peers, frames, spots, width = grad_after.shape
    length = frames * patches

    def body(grad_after, branch, mods, weight, grad_branch, grad_heads, grad_gate):
        upstream = grad_after[...].reshape(patches, width).astype(F32)
        value = (upstream * mods[2:3]).astype(BF16)
        grad_branch[...] = value
        grad_heads[...] = nt(value, weight[...]).astype(BF16)

        @pl.when(pl.program_id(0) == 0)
        def _():
            grad_gate[...] = jnp.zeros_like(grad_gate)

        grad_gate[...] += column_sum(upstream * branch[...].astype(F32))

    return pl.pallas_call(
        body,
        grid=(frames,),
        in_specs=[
            pl.BlockSpec((peers, 1, spots, width), lambda f: (0, f, 0, 0)),
            pl.BlockSpec((patches, width), lambda f: (f, 0)),
            whole(mods.shape),
            whole(weight.shape),
        ],
        out_specs=[
            pl.BlockSpec((patches, width), lambda f: (f, 0)),
            pl.BlockSpec((patches, width), lambda f: (f, 0)),
            whole_out((1, width)),
        ],
        out_shape=[
            jax.ShapeDtypeStruct((length, width), BF16),
            jax.ShapeDtypeStruct((length, width), BF16),
            jax.ShapeDtypeStruct((1, width), F32),
        ],
        compiler_params=params(),
        cost_estimate=cost(2 * length * width * width, 8 * MIB),
        name="space_branch_back",
    )(grad_after, branch, mods, weight)


def space_back(packed, grad_heads, totals, bias, patches):
    length, width = grad_heads.shape
    frames = length // patches
    pairs = width // 128

    def body(queries, keys, values, grad, totals, bias, grad_q, grad_k, grad_v):
        logs = totals[0, 0]
        grad_q[...], grad_k[...], grad_v[...] = pair_back(
            queries[...], keys[...], values[...], grad[...], (logs[0:1], logs[1:2]), bias[...]
        )

    one = pl.BlockSpec((patches, 128), lambda f, p: (f, p))
    return pl.pallas_call(
        body,
        grid=(frames, pairs),
        in_specs=[
            one,
            pl.BlockSpec((patches, 128), lambda f, p: (f, pairs + p)),
            pl.BlockSpec((patches, 128), lambda f, p: (f, 2 * pairs + p)),
            one,
            pl.BlockSpec((1, 1, 2, patches), lambda f, p: (f, p, 0, 0)),
            whole(bias.shape),
        ],
        out_specs=[one, one, one],
        out_shape=[jax.ShapeDtypeStruct((length, width), BF16)] * 3,
        compiler_params=params(),
        cost_estimate=cost(20e9, 12 * MIB, 6e6),
        name="space_back",
    )(packed, packed, packed, grad_heads, totals, bias)


def space_input_back(grads, weight, tokens, grad_after, mods, patches):
    peers, frames, spots, width = grad_after.shape
    length = frames * patches

    def body(grad_q, grad_k, grad_v, weight, tokens, grad_after, mods, grad_tokens, sums):
        grad_act = nt(grad_q[...], weight[:, :width])
        grad_act += nt(grad_k[...], weight[:, width : 2 * width])
        grad_act += nt(grad_v[...], weight[:, 2 * width :])
        normed, inverse = normalise(tokens[...].astype(F32))
        upstream = grad_after[...].reshape(patches, width).astype(F32)
        grad_tokens[...] = (upstream + norm_back(grad_act, normed, inverse, mods[1:2])).astype(BF16)

        @pl.when(pl.program_id(0) == 0)
        def _():
            sums[...] = jnp.zeros_like(sums)

        sums[0:1] += column_sum(grad_act)
        sums[1:2] += column_sum(grad_act * normed)

    one = pl.BlockSpec((patches, width), lambda f: (f, 0))
    return pl.pallas_call(
        body,
        grid=(frames,),
        in_specs=[
            one,
            one,
            one,
            whole(weight.shape),
            one,
            pl.BlockSpec((peers, 1, spots, width), lambda f: (0, f, 0, 0)),
            whole(mods.shape),
        ],
        out_specs=[one, whole_out((2, width))],
        out_shape=[
            jax.ShapeDtypeStruct((length, width), BF16),
            jax.ShapeDtypeStruct((2, width), F32),
        ],
        compiler_params=params(),
        cost_estimate=cost(6 * length * width * width, 14 * MIB),
        name="space_input_back",
    )(*grads, weight, tokens, grad_after, mods)


def middle(after, grad_out, mods, first_bias, second_bias, time_in, time_out, first, second):
    frames, spots, width = after.shape
    hidden_width = first.shape[1]
    tile = 16
    block = frames * tile
    length = frames * spots
    pairs = width // 128
    chunks = hidden_width // width
    slope = math.sqrt(2.0 / math.pi)

    def body(
        after, grad_out, mods, first_bias, second_bias, time_in, time_out, first, second,
        out, grad_after, time_act, time_heads, mlp_act, hidden, grad_second, grad_pre,
        grad_branch, grad_packed, sums, bias_sums, packed, derived,
    ):
        @pl.when(pl.program_id(0) == 0)
        def _():
            sums[...] = jnp.zeros_like(sums)
            bias_sums[...] = jnp.zeros_like(bias_sums)

        row = lax.broadcasted_iota(jnp.int32, (block, block), 0)
        column = lax.broadcasted_iota(jnp.int32, (block, block), 1)
        apart = jnp.where((row & (tile - 1)) == (column & (tile - 1)), 0.0, APART)

        current = after[...].reshape(block, width).astype(F32)
        time_norm, time_inverse = normalise(current)
        act = (time_norm * (1.0 + mods[4:5]) + mods[3:4]).astype(BF16)
        time_act[...] = act
        packed[...] = nn(act, time_in[...]).astype(BF16)
        totals = []
        for pair in range(pairs):
            cut = slice(128 * pair, 128 * pair + 128)
            attended, logs = pair_forward(
                packed[:, cut],
                packed[:, width + 128 * pair : width + 128 * pair + 128],
                packed[:, 2 * width + 128 * pair : 2 * width + 128 * pair + 128],
                apart,
            )
            time_heads[:, cut] = attended
            totals.append(logs)
        time_branch = nn(time_heads[...], time_out[...])
        after_time = current + mods[5:6] * time_branch
        mlp_norm, mlp_inverse = normalise(after_time)
        act = (mlp_norm * (1.0 + mods[7:8]) + mods[6:7]).astype(BF16)
        mlp_act[...] = act
        mlp_branch = 0.0
        for chunk in range(chunks):
            cut = slice(width * chunk, width * chunk + width)
            pre = nn(act, first[:, cut]) + first_bias[:, cut]
            squared = pre * pre
            bent = jnp.tanh(slope * pre * (1.0 + 0.044715 * squared))
            half = 0.5 * (1.0 + bent)
            value = (pre * half).astype(BF16)
            hidden[:, cut] = value
            derived[:, cut] = half + 0.5 * slope * pre * (1.0 - bent * bent) * (
                1.0 + 3.0 * 0.044715 * squared
            )
            mlp_branch += nn(value, second[cut])
        mlp_branch += second_bias[...]
        out[...] = (after_time + mods[8:9] * mlp_branch).astype(BF16).reshape(frames, tile, width)

        upstream = grad_out[...].reshape(block, width).astype(F32)
        sums[5:6] += column_sum(upstream * mlp_branch)
        grad_value = (upstream * mods[8:9]).astype(BF16)
        grad_second[...] = grad_value
        bias_sums[:, hidden_width:] += column_sum(grad_value.astype(F32))
        grad_act = 0.0
        for chunk in range(chunks):
            cut = slice(width * chunk, width * chunk + width)
            value = (nt(grad_value, second[cut]) * derived[:, cut]).astype(BF16)
            grad_pre[:, cut] = value
            bias_sums[:, cut] += column_sum(value.astype(F32))
            grad_act += nt(value, first[:, cut])
        sums[3:4] += column_sum(grad_act)
        sums[4:5] += column_sum(grad_act * mlp_norm)
        upstream = upstream + norm_back(grad_act, mlp_norm, mlp_inverse, mods[7:8])

        sums[2:3] += column_sum(upstream * time_branch)
        grad_value = (upstream * mods[5:6]).astype(BF16)
        grad_branch[...] = grad_value
        grad_heads = nt(grad_value, time_out[...]).astype(BF16)
        for pair in range(pairs):
            cuts = [
                slice(part * width + 128 * pair, part * width + 128 * pair + 128)
                for part in range(3)
            ]
            parts = pair_back(
                packed[:, cuts[0]],
                packed[:, cuts[1]],
                packed[:, cuts[2]],
                grad_heads[:, cuts[0]],
                totals[pair],
                apart,
            )
            for cut, part in zip(cuts, parts):
                grad_packed[:, cut] = part
        grad_act = nt(grad_packed[...], time_in[...]).astype(BF16).astype(F32)
        sums[0:1] += column_sum(grad_act)
        sums[1:2] += column_sum(grad_act * time_norm)
        upstream = upstream + norm_back(grad_act, time_norm, time_inverse, mods[4:5])
        grad_after[...] = upstream.astype(BF16).reshape(frames, tile, width)

    moving = pl.BlockSpec((frames, tile, width), lambda i: (0, i, 0))

    def rows(columns):
        return pl.BlockSpec((block, columns), lambda i: (i, 0))

    def array(columns):
        return jax.ShapeDtypeStruct((length, columns), BF16)

    narrow, wide, triple = width, hidden_width, 3 * width
    kept = [narrow, narrow, narrow, wide, narrow, wide, narrow, triple]
    return pl.pallas_call(
        body,
        grid=(spots // tile,),
        in_specs=[moving, moving]
        + [
            whole(a.shape)
            for a in (mods, first_bias, second_bias, time_in, time_out, first, second)
        ],
        out_specs=[moving, moving]
        + [rows(c) for c in kept]
        + [whole_out((8, width)), whole_out((1, hidden_width + width))],
        out_shape=[jax.ShapeDtypeStruct(after.shape, BF16)] * 2
        + [array(c) for c in kept]
        + [
            jax.ShapeDtypeStruct((8, width), F32),
            jax.ShapeDtypeStruct((1, hidden_width + width), F32),
        ],
        scratch_shapes=[
            pltpu.VMEM((block, triple), BF16),
            pltpu.VMEM((block, hidden_width), F32),
        ],
        compiler_params=params(),
        cost_estimate=cost(45e9, 50 * MIB, 8e6),
        name="middle",
    )(after, grad_out, mods, first_bias, second_bias, time_in, time_out, first, second)


def local(
    count,
    tokens,
    condition,
    patch_mask,
    grad_out,
    mod_weight,
    mod_bias,
    space_qkv,
    space_proj,
    time_qkv,
    time_proj,
    mlp_in,
    in_bias,
    mlp_out,
    out_bias,
):
    length, width = tokens.shape
    patches = patch_mask.shape[1]
    frame_dev = length // patches
    groups = condition.shape[0]
    clip_dev = FRAMES // frame_dev
    spots = patches // clip_dev
    sp_size = lax.axis_size("sp")
    shard = mod_weight.shape[0]
    mod_width = mod_weight.shape[1]
    hidden_width = mlp_in.shape[1]
    me = lax.axis_index("dp") * sp_size + lax.axis_index("sp")
    chip = me // 2
    core = me % 2
    clip_row = lax.axis_index("sp") // clip_dev
    order_a, order_b = chip_orders(count)
    teams = [list(range(s, s + clip_dev)) for s in range(0, sp_size, clip_dev)]

    def across(values):
        return lax.all_to_all(
            values, "sp", split_axis=0, concat_axis=0, tiled=True, axis_index_groups=teams
        )

    near = jnp.stack([condition[clip_row ^ s] for s in range(groups)])
    mask = sp_size
    while mask < count:
        near = jnp.concatenate([near, swap(near, mask, count)], axis=0)
        mask *= 2
    lifted = jax.nn.silu(near.astype(F32)).astype(BF16)
    lifted_rows = lax.dynamic_slice_in_dim(lifted, me * shard, shard, 1)
    part = jnp.dot(lifted_rows, mod_weight, preferred_element_type=F32)
    own = jnp.zeros((mod_width + hidden_width + width,), F32)
    own = lax.dynamic_update_slice(own, mod_bias.astype(F32), (me * mod_bias.shape[0],))
    own = lax.dynamic_update_slice(
        own, in_bias.astype(F32), (mod_width + me * in_bias.shape[0],)
    )
    own = lax.dynamic_update_slice(
        own, out_bias.astype(F32), (mod_width + hidden_width + me * out_bias.shape[0],)
    )
    row = jnp.pad(part, ((0, 0), (0, hidden_width + width))) + own[None]
    mask = count // 2
    while mask >= clip_dev:
        half = row.shape[0] // 2
        row = row[:half] + swap(row[half:], mask, count)
        mask //= 2
    row = clip_total(row, clip_dev, count)
    mods = row[0, :mod_width].reshape(9, width)
    first_bias = row[:, mod_width : mod_width + hidden_width]
    second_bias = row[:, mod_width + hidden_width :]

    if shard % 8:
        space_full, time_full, space_out, time_out = (
            lax.all_gather(w, AXES, axis=0, tiled=True)
            for w in (space_qkv, time_qkv, space_proj, time_proj)
        )
    else:
        cut = space_qkv.shape[1] // 2
        held = [
            spread(space_qkv[:, :cut], order_a, count),
            spread(space_qkv[:, cut:], order_b, count),
        ]
        pieces = [(h, swap(h, 1, count)) for h in held]
        (space_full,) = assemble(
            pieces, (order_a, order_b), [[(0, 0, cut), (1, 0, cut)]], chip, core, count
        )
        cut = (time_qkv.shape[1] + 2 * width) // 2
        rest = time_qkv.shape[1] - cut
        held = [
            spread(time_qkv[:, :cut], order_a, count),
            spread(
                jnp.concatenate([time_qkv[:, cut:], space_proj, time_proj], axis=1), order_b, count
            ),
        ]
        pieces = [(h, swap(h, 1, count)) for h in held]
        time_full, space_out, time_out = assemble(
            pieces,
            (order_a, order_b),
            [[(0, 0, cut), (1, 0, rest)], [(1, rest, width)], [(1, rest + width, width)]],
            chip,
            core,
            count,
        )
    first_full = lax.all_gather(mlp_in, AXES, axis=0, tiled=True)
    second_full = lax.all_gather(mlp_out, AXES, axis=0, tiled=True)

    mask_row = lax.dynamic_index_in_dim(patch_mask, clip_row, 0, keepdims=False)
    key_bias = jnp.where(mask_row == 1, 0.0, MASKED).astype(F32)[:, None]
    grad_here = across(
        jnp.transpose(grad_out.reshape(frame_dev, clip_dev, spots, width), (1, 0, 2, 3))
    )
    space_act, space_packed = space_project(tokens, mods, space_full)
    space_heads, space_total, space_branch, after_space = space_forward(
        space_packed, tokens, mods, key_bias, space_out, patches, clip_dev
    )
    after_here = across(after_space)

    (
        out_here,
        grad_here,
        time_act,
        time_heads,
        mlp_act,
        hidden,
        grad_second,
        grad_pre,
        grad_time_branch,
        grad_time_packed,
        sums,
        bias_sums,
    ) = middle(
        after_here.reshape(FRAMES, spots, width),
        grad_here.reshape(FRAMES, spots, width),
        mods,
        first_bias,
        second_bias,
        time_full,
        time_out,
        first_full,
        second_full,
    )
    shape = (clip_dev, frame_dev, spots, width)
    grad_after = across(grad_here.reshape(shape))
    out_tokens = jnp.transpose(across(out_here.reshape(shape)), (1, 0, 2, 3)).reshape(length, width)

    turn_a, turn_b = order_a[::-1], order_b[::-1]
    keep, send = weight_grads([(mlp_act, grad_pre)], turn_a, chip, core, count)
    grad_mlp_in = fold(keep, send, turn_a, count)
    keep, send = weight_grads([(hidden, grad_second)], turn_b, chip, core, count)
    grad_mlp_out = fold(keep, send, turn_b, count)
    keep, send = weight_grads(
        [(time_act, grad_time_packed), (time_heads, grad_time_branch)], turn_a, chip, core, count
    )
    grad_time = fold(keep, send, turn_a, count)

    early = jnp.concatenate([sums[:6].reshape(1, -1), bias_sums], axis=1)
    early = clip_spread(clip_total(early, clip_dev, count), clip_dev, count)

    grad_space_branch, grad_space_heads, grad_gate = space_branch_back(
        grad_after, space_branch, mods, space_out, patches
    )
    keep, send = weight_grads([(space_heads, grad_space_branch)], turn_b, chip, core, count)
    grad_space_proj = fold(keep, send, turn_b, count)
    grads = space_back(space_packed, grad_space_heads, space_total, key_bias, patches)
    grad_tokens, space_sums = space_input_back(
        grads, space_full, tokens, grad_after, mods, patches
    )
    keep, send = weight_grads([(space_act, g) for g in grads], turn_b, chip, core, count)
    grad_space_qkv = fold(keep, send, turn_b, count)

    late = jnp.concatenate([space_sums.reshape(1, -1), grad_gate], axis=1)
    late = clip_spread(clip_total(late, clip_dev, count), clip_dev, count)
    grad_rows = jnp.concatenate([late, early[:, : mod_width - 3 * width]], axis=1)
    grad_mod_weight = lax.dot_general(
        lifted_rows.astype(F32),
        grad_rows,
        (((0,), (0,)), ((), ())),
        precision=lax.Precision.HIGHEST,
        preferred_element_type=F32,
    )
    totals = jnp.sum(jnp.concatenate([grad_rows, early[:, mod_width - 3 * width :]], axis=1), axis=0)
    grad_mod_bias = lax.dynamic_slice_in_dim(totals, me * mod_bias.shape[0], mod_bias.shape[0])
    grad_in_bias = lax.dynamic_slice_in_dim(
        totals, mod_width + me * in_bias.shape[0], in_bias.shape[0]
    )
    grad_out_bias = lax.dynamic_slice_in_dim(
        totals, mod_width + hidden_width + me * out_bias.shape[0], out_bias.shape[0]
    )
    grad_lifted = lax.dot_general(
        grad_rows,
        mod_weight.astype(F32),
        (((1,), (1,)), ((), ())),
        precision=lax.Precision.HIGHEST,
        preferred_element_type=F32,
    )
    mask = count // 2
    while mask >= sp_size:
        half = grad_lifted.shape[0] // 2
        grad_lifted = jnp.concatenate(
            [grad_lifted[:half], swap(grad_lifted[half:], mask, count)], axis=1
        )
        mask //= 2
    dp_size = count // sp_size
    places = []
    for distance in range(dp_size):
        places.append(
            sum(1 << (dp_size.bit_length() - 2 - s) for s in range(dp_size.bit_length() - 1)
                if distance & (1 << (s)))
        )
    grad_lifted = jnp.stack([grad_lifted[clip_row ^ s] for s in range(groups)])
    grad_lifted = grad_lifted.reshape(1, groups, dp_size, shard)
    mask = 1
    while mask < sp_size:
        grad_lifted = jnp.concatenate([grad_lifted, swap(grad_lifted, mask, count)], axis=0)
        mask *= 2
    sp_order = jnp.arange(sp_size) ^ lax.axis_index("sp")
    dp_order = jnp.array(places, jnp.int32)[jnp.arange(dp_size) ^ lax.axis_index("dp")]
    grad_lifted = grad_lifted[sp_order][:, :, dp_order]
    grad_lifted = jnp.transpose(grad_lifted, (1, 2, 0, 3)).reshape(groups, width)
    _, silu_back = jax.vjp(jax.nn.silu, condition.astype(F32))
    grad_condition = silu_back(grad_lifted)[0]

    return (
        out_tokens,
        grad_tokens,
        grad_condition,
        grad_mod_weight,
        grad_mod_bias,
        grad_space_qkv,
        grad_space_proj,
        grad_time[:, : 3 * width],
        grad_time[:, 3 * width :],
        grad_mlp_in,
        grad_in_bias,
        grad_mlp_out,
        grad_out_bias,
    )


def solution(mesh):
    count = mesh.shape["dp"] * mesh.shape["sp"]
    both = P(AXES, None)
    flat = P(AXES)
    clips = P("dp", None)
    return jax.shard_map(
        functools.partial(local, count),
        mesh=mesh,
        in_specs=(
            both, clips, clips, both, both, flat, both, both, both, both, both, flat, both, flat,
        ),
        out_specs=(
            both, both, clips, both, flat, both, both, both, both, both, flat, both, flat,
        ),
        check_vma=False,
    )
```

```python
import functools
import math

import jax
import jax.numpy as jnp
from jax import lax
from jax.experimental import pallas as pl
from jax.experimental.pallas import tpu as pltpu
from jax.sharding import PartitionSpec as P

HEADS = 12
HEAD_DIM = 64
FRAMES = 16
EPSILON = 1e-06
MASKED = -10000.0
APART = -1e30
AXES = ("dp", "sp")
F32 = jnp.float32
BF16 = jnp.bfloat16
MIB = 1 << 20


def swap(values, mask, count):
    return lax.ppermute(values, AXES, [(i, i ^ mask) for i in range(count)])


def chip_orders(count):
    bits = [1 << i for i in range(1, count.bit_length() - 1)]
    low, high, middle = bits[0], bits[-1], bits[1:-1][::-1]
    return (middle + [high, low], middle + [low, high])


def spread(shard, order, count):
    held = shard[None]
    for mask in order:
        held = jnp.concatenate([held, swap(held, mask, count)], axis=0)
    return held


def spread_places(order, count):
    places = []
    for distance in range(count // 2):
        places.append(sum(1 << s for s, mask in enumerate(order) if distance & (mask >> 1)))
    return places


def fold_places(order, count):
    steps = len(order)
    places = []
    for distance in range(count // 2):
        places.append(
            sum(1 << (steps - 1 - s) for s, mask in enumerate(order) if distance & (mask >> 1))
        )
    return places


class Fold:
    def __init__(self, shares, order, count):
        self.keep, self.send = shares
        self.masks = [1] + list(order)
        self.count = count
        self.got = swap(self.send, 1, count)

    def add(self):
        half = self.keep.shape[0] // 2
        low = self.keep[:half].astype(F32) + self.got[:half].astype(F32)
        high = self.keep[half:].astype(F32) + self.got[half:].astype(F32)
        self.keep, self.send = low.astype(BF16), high.astype(BF16)
        self.masks.pop(0)

    def go(self):
        self.got = swap(self.send, self.masks[0], self.count)

    def finish(self):
        while len(self.masks) > 1:
            self.add()
            self.go()
        return self.keep[0].astype(F32) + self.got[0].astype(F32)


def meet(values, *folds):
    values, states = lax.optimization_barrier(
        (values, [(f.keep, f.got) for f in folds])
    )
    for fold, (fold.keep, fold.got) in zip(folds, states):
        fold.add()
    values, states = lax.optimization_barrier((values, [(f.keep, f.send) for f in folds]))
    for fold, (fold.keep, fold.send) in zip(folds, states):
        fold.go()
    return values


def clip_total(row, mask, count):
    while mask:
        row = row + swap(row, mask, count)
        mask //= 2
    return row


def nn(a, b):
    return jnp.dot(a, b, preferred_element_type=F32)


def nt(a, b):
    return lax.dot_general(a, b, (((1,), (1,)), ((), ())), preferred_element_type=F32)


def tn(a, b):
    return lax.dot_general(a, b, (((0,), (0,)), ((), ())), preferred_element_type=F32)


def normalise(values):
    average = jnp.mean(values, axis=-1, keepdims=True)
    centred = values - average
    inverse = lax.rsqrt(jnp.mean(centred * centred, axis=-1, keepdims=True) + EPSILON)
    return centred * inverse, inverse


def norm_back(grad_mod, normed, inverse, scale):
    grad_normed = grad_mod * (1.0 + scale)
    inner = jnp.mean(grad_normed * normed, axis=-1, keepdims=True)
    average = jnp.mean(grad_normed, axis=-1, keepdims=True)
    return inverse * (grad_normed - average - normed * inner)


def column_sum(values):
    return jnp.sum(values, axis=0, keepdims=True)


def halves():
    lane = lax.broadcasted_iota(jnp.int32, (1, 2 * HEAD_DIM), 1)
    first = (lane < HEAD_DIM).astype(F32)
    return first.astype(BF16), (1.0 - first).astype(BF16)


def turned(values):
    return jnp.transpose(values.astype(F32), (1, 0))


def pair_forward(queries, keys, values, bias):
    values_t = turned(values).astype(BF16)
    parts = []
    totals = []
    for half, mask in enumerate(halves()):
        scores = nt(keys * mask, queries) * 0.125 + bias
        largest = jnp.max(scores, axis=0, keepdims=True)
        exponent = jnp.exp(scores - largest)
        denominator = jnp.sum(exponent, axis=0, keepdims=True)
        probable = (exponent * (1.0 / denominator)).astype(BF16)
        parts.append(nn(values_t[half * HEAD_DIM : (half + 1) * HEAD_DIM], probable))
        totals.append(largest + jnp.log(denominator))
    attended = jnp.transpose(jnp.concatenate(parts, axis=0), (1, 0)).astype(BF16)
    return attended, totals


def pair_back(queries, keys, values, grad, totals, bias):
    keys_t = turned(keys).astype(BF16)
    grad_queries = []
    grad_keys = 0.0
    grad_values = 0.0
    for half, mask in enumerate(halves()):
        scores = nt(keys * mask, queries) * 0.125 + bias
        probable = jnp.exp(scores - totals[half])
        grad_probs = nt(values * mask, grad)
        inner = jnp.sum(probable * grad_probs, axis=0, keepdims=True)
        grad_scores = (probable * (grad_probs - inner)).astype(BF16)
        grad_values = grad_values + nn(probable.astype(BF16), grad * mask)
        grad_keys = grad_keys + nn(grad_scores, queries * mask)
        grad_queries.append(nn(keys_t[half * HEAD_DIM : (half + 1) * HEAD_DIM], grad_scores))
    grad_queries = jnp.transpose(jnp.concatenate(grad_queries, axis=0), (1, 0))
    return (
        (grad_queries * 0.125).astype(BF16),
        (grad_keys * 0.125).astype(BF16),
        grad_values.astype(BF16),
    )


def whole(shape):
    return pl.BlockSpec(shape, lambda *_: (0,) * len(shape), pipeline_mode=pl.Buffered(1))


def whole_out(shape):
    return pl.BlockSpec(shape, lambda *_: (0,) * len(shape))


def params(limit=56):
    return pltpu.CompilerParams(vmem_limit_bytes=limit * MIB)


def cost(flops, moved, special=0):
    return pl.CostEstimate(flops=int(flops), bytes_accessed=int(moved), transcendentals=int(special))


def place_table(orders, chip, core, count):
    chips = count // 2
    index = jnp.arange(chips) ^ chip
    return jnp.stack(
        [jnp.array(spread_places(order, count), jnp.int32)[index] for order in orders]
        + [jnp.full((chips,), core, jnp.int32)]
    )


def build(table, row, own, other, runs):
    chips, share, _ = own.shape
    odd = table[table.shape[0] - 1, 0] == 1

    def step(i, carry):
        place = table[row, i]
        one = own[place].astype(F32)
        two = other[place].astype(F32)
        joined = jnp.concatenate(
            [jnp.where(odd, two, one), jnp.where(odd, one, two)], axis=0
        ).astype(BF16)
        rows = pl.ds(pl.multiple_of(i * 2 * share, 2 * share), 2 * share)
        for column, width, target, start in runs:
            target[rows, start : start + width] = joined[:, column : column + width]
        return carry

    lax.fori_loop(0, chips, step, 0)


def weight_grads(groups, order, chip, core, count, share, block):
    chips = count // 2
    length = groups[0][0].shape[0]
    depth = count * share
    packed = [acts.shape[1] // depth for acts, *_ in groups]
    steps = [blocks if deep == 1 else deep for deep, (_, _, _, blocks) in zip(packed, groups)]
    spans = [blocks * deep for deep, (_, _, _, blocks) in zip(packed, groups)]
    starts = [sum(steps[:i]) for i in range(len(steps))]
    offsets = [sum(spans[:i]) for i in range(len(spans))]
    resident = max(packed) > 1
    columns = sum(spans) * block
    table = jnp.concatenate(
        [
            jnp.array(fold_places(order, count), jnp.int32)[jnp.arange(chips) ^ chip],
            jnp.full((1,), core, jnp.int32),
        ]
    )

    def body(table, *refs):
        keep, send, acts_t = refs[2 * len(groups) :]
        j = pl.program_id(0)
        odd = table[chips] == 1

        def put(place, cut, first, second):
            keep[place, :, cut] = jnp.where(odd, second, first).astype(BF16)
            send[place, :, cut] = jnp.where(odd, first, second).astype(BF16)

        for index, deep in enumerate(packed):
            acts, grads = refs[2 * index : 2 * index + 2]
            here = j - starts[index]

            @pl.when(jnp.logical_and(here >= 0, here < (steps[index] if deep > 1 else 1)))
            def _():
                acts_t[...] = turned(acts[...]).astype(BF16)

            @pl.when(jnp.logical_and(here >= 0, here < steps[index]))
            def _():
                product = nn(acts_t[...], grads[...])
                if deep > 1:
                    pairs = depth // (2 * share * deep)
                    for pair in range(pairs):
                        place = table[here * pairs + pair]
                        for part in range(deep):
                            start = (2 * pair * deep + part) * share
                            first = product[start : start + share]
                            second = product[start + deep * share : start + deep * share + share]
                            at = (offsets[index] + part) * block
                            put(place, slice(at, at + block), first, second)
                else:
                    if resident:
                        at = pl.multiple_of((offsets[index] + here) * block, block)
                        cut = pl.ds(at, block)
                    else:
                        cut = slice(None)
                    for pair in range(chips):
                        start = 2 * pair * share
                        first = product[start : start + share]
                        second = product[start + share : start + 2 * share]
                        put(table[pair], cut, first, second)

    in_specs = []
    operands = []
    for start, step, deep, (acts, grads, g_first, _) in zip(starts, steps, packed, groups):
        place = lambda j, t, s=start, m=step: jnp.clip(j - s, 0, m - 1)
        if deep > 1:
            in_specs.append(pl.BlockSpec((length, depth), lambda j, t, p=place: (0, p(j, t))))
            in_specs.append(pl.BlockSpec((length, block), lambda j, t: (0, 0)))
        else:
            in_specs.append(pl.BlockSpec((length, depth), lambda j, t: (0, 0)))
            in_specs.append(
                pl.BlockSpec((length, block), lambda j, t, p=place, g=g_first: (0, g + p(j, t)))
            )
        operands += [acts, grads]
    out = jax.ShapeDtypeStruct((chips, share, columns), BF16)
    if resident:
        out_spec = whole_out(out.shape)
    else:
        out_spec = pl.BlockSpec((chips, share, block), lambda j, t: (0, 0, j))
    return pl.pallas_call(
        body,
        grid_spec=pltpu.PrefetchScalarGridSpec(
            num_scalar_prefetch=1,
            grid=(sum(steps),),
            in_specs=in_specs,
            out_specs=[out_spec, out_spec],
            scratch_shapes=[pltpu.VMEM((depth, length), BF16)],
        ),
        out_shape=[out, out],
        compiler_params=params(),
        cost_estimate=cost(2 * length * depth * columns, 4 * depth * columns),
        name="weight_grads",
    )(table, *operands)


def space_project(tokens, mods, table, held):
    length, width = tokens.shape
    depth = held[0][0].shape[0] * held[0][0].shape[1] * 2
    wide = 3 * width
    cut = held[0][0].shape[2]
    block = 256

    def body(table, tokens, mods, own_a, other_a, own_b, other_b, act, packed, weight, last):
        @pl.when(pl.program_id(0) == 0)
        def _():
            build(table, 0, own_a, other_a, [(0, cut, weight, 0)])
            build(
                table, 1, own_b, other_b, [(0, wide - cut, weight, cut), (wide - cut, width, last, 0)]
            )

        normed, _ = normalise(tokens[...].astype(F32))
        value = (normed * (1.0 + mods[1:2]) + mods[0:1]).astype(BF16)
        act[...] = value
        packed[...] = nn(value, weight[...]).astype(BF16)

    parts = [part for pair in held for part in pair]
    return pl.pallas_call(
        body,
        grid_spec=pltpu.PrefetchScalarGridSpec(
            num_scalar_prefetch=1,
            grid=(length // block,),
            in_specs=[pl.BlockSpec((block, width), lambda i, t: (i, 0)), whole(mods.shape)]
            + [whole(part.shape) for part in parts],
            out_specs=[
                pl.BlockSpec((block, width), lambda i, t: (i, 0)),
                pl.BlockSpec((block, wide), lambda i, t: (i, 0)),
                whole_out((depth, wide)),
                whole_out((depth, width)),
            ],
        ),
        out_shape=[
            jax.ShapeDtypeStruct((length, width), BF16),
            jax.ShapeDtypeStruct((length, wide), BF16),
            jax.ShapeDtypeStruct((depth, wide), BF16),
            jax.ShapeDtypeStruct((depth, width), BF16),
        ],
        compiler_params=params(),
        cost_estimate=cost(2 * length * width * wide, 16 * MIB),
        name="space_project",
    )(table, tokens, mods, *parts)


def space_forward(packed, tokens, mods, bias, weight, patches, peers):
    length, width = tokens.shape
    frames = length // patches
    pairs = width // 128
    spots = patches // peers

    def body(queries, keys, values, tokens, mods, bias, weight, heads, totals, branch, after, kept):
        pair = pl.program_id(1)
        attended, logs = pair_forward(queries[...], keys[...], values[...], bias[...])
        heads[...] = attended
        totals[0, 0] = jnp.concatenate(logs, axis=0)
        kept[pair] = attended

        @pl.when(pair == pairs - 1)
        def _():
            joined = jnp.concatenate([kept[p] for p in range(pairs)], axis=1)
            product = nn(joined, weight[...])
            branch[...] = product.astype(BF16)
            result = (tokens[...].astype(F32) + mods[2:3] * product).astype(BF16)
            for peer in range(peers):
                after[peer, 0] = result[peer * spots : (peer + 1) * spots]

    return pl.pallas_call(
        body,
        grid=(frames, pairs),
        in_specs=[
            pl.BlockSpec((patches, 128), lambda f, p: (f, p)),
            pl.BlockSpec((patches, 128), lambda f, p: (f, pairs + p)),
            pl.BlockSpec((patches, 128), lambda f, p: (f, 2 * pairs + p)),
            pl.BlockSpec((patches, width), lambda f, p: (f, 0)),
            whole(mods.shape),
            whole(bias.shape),
            whole(weight.shape),
        ],
        out_specs=[
            pl.BlockSpec((patches, 128), lambda f, p: (f, p)),
            pl.BlockSpec((1, 1, 2, patches), lambda f, p: (f, p, 0, 0)),
            pl.BlockSpec((patches, width), lambda f, p: (f, 0)),
            pl.BlockSpec((peers, 1, spots, width), lambda f, p: (0, f, 0, 0)),
        ],
        out_shape=[
            jax.ShapeDtypeStruct((length, width), BF16),
            jax.ShapeDtypeStruct((frames, pairs, 2, patches), F32),
            jax.ShapeDtypeStruct((length, width), BF16),
            jax.ShapeDtypeStruct((peers, frames, spots, width), BF16),
        ],
        scratch_shapes=[pltpu.VMEM((pairs, patches, 128), BF16)],
        compiler_params=params(),
        cost_estimate=cost(10e9, 10 * MIB, 6e6),
        name="space_forward",
    )(packed, packed, packed, tokens, mods, bias, weight)


def space_branch_back(grad_after, branch, mods, weight, patches):
    peers, frames, spots, width = grad_after.shape
    length = frames * patches

    def body(grad_after, branch, mods, weight, grad_branch, grad_heads, grad_gate):
        upstream = grad_after[...].reshape(patches, width).astype(F32)
        value = (upstream * mods[2:3]).astype(BF16)
        grad_branch[...] = value
        grad_heads[...] = nt(value, weight[...]).astype(BF16)

        @pl.when(pl.program_id(0) == 0)
        def _():
            grad_gate[...] = jnp.zeros_like(grad_gate)

        grad_gate[...] += column_sum(upstream * branch[...].astype(F32))

    return pl.pallas_call(
        body,
        grid=(frames,),
        in_specs=[
            pl.BlockSpec((peers, 1, spots, width), lambda f: (0, f, 0, 0)),
            pl.BlockSpec((patches, width), lambda f: (f, 0)),
            whole(mods.shape),
            whole(weight.shape),
        ],
        out_specs=[
            pl.BlockSpec((patches, width), lambda f: (f, 0)),
            pl.BlockSpec((patches, width), lambda f: (f, 0)),
            whole_out((1, width)),
        ],
        out_shape=[
            jax.ShapeDtypeStruct((length, width), BF16),
            jax.ShapeDtypeStruct((length, width), BF16),
            jax.ShapeDtypeStruct((1, width), F32),
        ],
        compiler_params=params(),
        cost_estimate=cost(2 * length * width * width, 8 * MIB),
        name="space_branch_back",
    )(grad_after, branch, mods, weight)


def space_back(packed, grad_heads, totals, bias, weight, tokens, grad_after, mods, patches):
    peers, frames, spots, width = grad_after.shape
    length = frames * patches
    pairs = width // 128

    def body(
        queries, keys, values, grad, totals, bias, weight, tokens, grad_after, mods,
        grad_q, grad_k, grad_v, grad_tokens, sums, kept,
    ):
        pair = pl.program_id(1)
        logs = totals[0, 0]
        parts = pair_back(
            queries[...], keys[...], values[...], grad[...], (logs[0:1], logs[1:2]), bias[...]
        )
        for index, (out, part) in enumerate(zip((grad_q, grad_k, grad_v), parts)):
            out[...] = part
            kept[index * pairs + pair] = part

        @pl.when(jnp.logical_and(pl.program_id(0) == 0, pair == 0))
        def _():
            sums[...] = jnp.zeros_like(sums)

        @pl.when(pair == pairs - 1)
        def _():
            joined = jnp.concatenate([kept[i] for i in range(3 * pairs)], axis=1)
            grad_act = nt(joined, weight[...])
            normed, inverse = normalise(tokens[...].astype(F32))
            upstream = grad_after[...].reshape(patches, width).astype(F32)
            grad_tokens[...] = (
                upstream + norm_back(grad_act, normed, inverse, mods[1:2])
            ).astype(BF16)
            sums[0:1] += column_sum(grad_act)
            sums[1:2] += column_sum(grad_act * normed)

    def taken(part):
        return pl.BlockSpec((patches, 128), lambda f, p: (f, part * pairs + p))

    one = pl.BlockSpec((patches, 128), lambda f, p: (f, p))
    full = pl.BlockSpec((patches, width), lambda f, p: (f, 0))
    flat = jax.ShapeDtypeStruct((length, width), BF16)
    return pl.pallas_call(
        body,
        grid=(frames, pairs),
        in_specs=[
            taken(0),
            taken(1),
            taken(2),
            one,
            pl.BlockSpec((1, 1, 2, patches), lambda f, p: (f, p, 0, 0)),
            whole(bias.shape),
            whole(weight.shape),
            full,
            pl.BlockSpec((peers, 1, spots, width), lambda f, p: (0, f, 0, 0)),
            whole(mods.shape),
        ],
        out_specs=[one, one, one, full, whole_out((2, width))],
        out_shape=[flat, flat, flat, flat, jax.ShapeDtypeStruct((2, width), F32)],
        scratch_shapes=[pltpu.VMEM((3 * pairs, patches, 128), BF16)],
        compiler_params=params(),
        cost_estimate=cost(24e9, 20 * MIB, 6e6),
        name="space_back",
    )(packed, packed, packed, grad_heads, totals, bias, weight, tokens, grad_after, mods)


TILE = 16


def apart_bias(block):
    row = lax.broadcasted_iota(jnp.int32, (block, block), 0)
    column = lax.broadcasted_iota(jnp.int32, (block, block), 1)
    return jnp.where((row & (TILE - 1)) == (column & (TILE - 1)), 0.0, APART)


def part_cuts(pair, width):
    return [slice(p * width + 128 * pair, p * width + 128 * pair + 128) for p in range(3)]


def time_forward(after, mods, table, own, other):
    frames, spots, width = after.shape
    depth = own.shape[0] * own.shape[1] * 2
    block = frames * TILE
    length = frames * spots
    pairs = width // 128

    def body(table, after, mods, own, other, act, packed, heads, branch, totals, time_in, time_out):
        @pl.when(pl.program_id(0) == 0)
        def _():
            build(
                table, 0, own, other, [(0, 3 * width, time_in, 0), (3 * width, width, time_out, 0)]
            )

        apart = apart_bias(block)
        normed, _ = normalise(after[...].reshape(block, width).astype(F32))
        value = (normed * (1.0 + mods[4:5]) + mods[3:4]).astype(BF16)
        act[...] = value
        packed[...] = nn(value, time_in[...]).astype(BF16)
        for pair in range(pairs):
            queries, keys, values = (packed[:, cut] for cut in part_cuts(pair, width))
            attended, logs = pair_forward(queries, keys, values, apart)
            heads[:, 128 * pair : 128 * pair + 128] = attended
            totals[0, pair] = jnp.concatenate(logs, axis=0)
        branch[...] = nn(heads[...], time_out[...])

    def rows(columns):
        return pl.BlockSpec((block, columns), lambda i, t: (i, 0))

    return pl.pallas_call(
        body,
        grid_spec=pltpu.PrefetchScalarGridSpec(
            num_scalar_prefetch=1,
            grid=(spots // TILE,),
            in_specs=[pl.BlockSpec((frames, TILE, width), lambda i, t: (0, i, 0))]
            + [whole(a.shape) for a in (mods, own, other)],
            out_specs=[
                rows(width),
                rows(3 * width),
                rows(width),
                rows(width),
                pl.BlockSpec((1, pairs, 2, block), lambda i, t: (i, 0, 0, 0)),
                whole_out((depth, 3 * width)),
                whole_out((depth, width)),
            ],
        ),
        out_shape=[
            jax.ShapeDtypeStruct((length, width), BF16),
            jax.ShapeDtypeStruct((length, 3 * width), BF16),
            jax.ShapeDtypeStruct((length, width), BF16),
            jax.ShapeDtypeStruct((length, width), F32),
            jax.ShapeDtypeStruct((spots // TILE, pairs, 2, block), F32),
            jax.ShapeDtypeStruct((depth, 3 * width), BF16),
            jax.ShapeDtypeStruct((depth, width), BF16),
        ],
        compiler_params=params(),
        cost_estimate=cost(8e9, 24 * MIB, 3e6),
        name="time_forward",
    )(table, after, mods, own, other)


def middle(
    after, grad_out, packed, time_branch, totals, mods, first_bias, second_bias, time_in, time_out,
    mlp_full, share,
):
    frames, spots, width = after.shape
    hidden_width = first_bias.shape[1]
    depth = mlp_full.shape[0]
    count = depth // share
    block = frames * TILE
    length = frames * spots
    pairs = width // 128
    chunks = hidden_width // width
    slope = math.sqrt(2.0 / math.pi)

    def body(
        after, grad_out, packed, time_branch, totals,
        mods, first_bias, second_bias, time_in, time_out, first, shares,
        out, grad_after, mlp_act, hidden, grad_second, grad_pre, grad_branch, grad_packed,
        sums, bias_sums, derived, second,
    ):
        @pl.when(pl.program_id(0) == 0)
        def _():
            def unpack(i, carry):
                piece = shares[i].astype(F32)
                parts = [piece[:, c * width : (c + 1) * width] for c in range(chunks)]
                rows = pl.ds(pl.multiple_of(i * chunks * share, chunks * share), chunks * share)
                second[rows] = jnp.concatenate(parts, axis=0).astype(BF16)
                return carry

            lax.fori_loop(0, count, unpack, 0)
            sums[...] = jnp.zeros_like(sums)
            bias_sums[...] = jnp.zeros_like(bias_sums)

        current = after[...].reshape(block, width).astype(F32)
        after_time = current + mods[5:6] * time_branch[...]
        mlp_norm, mlp_inverse = normalise(after_time)
        act = (mlp_norm * (1.0 + mods[7:8]) + mods[6:7]).astype(BF16)
        mlp_act[...] = act
        mlp_branch = 0.0
        for chunk in range(chunks):
            cut = slice(width * chunk, width * chunk + width)
            pre = nn(act, first[:, cut]) + first_bias[:, cut]
            squared = pre * pre
            bent = jnp.tanh(slope * pre * (1.0 + 0.044715 * squared))
            half = 0.5 * (1.0 + bent)
            value = (pre * half).astype(BF16)
            hidden[:, cut] = value
            derived[:, cut] = half + 0.5 * slope * pre * (1.0 - bent * bent) * (
                1.0 + 3.0 * 0.044715 * squared
            )
            mlp_branch += nn(value, second[cut])
        mlp_branch += second_bias[...]
        out[...] = (after_time + mods[8:9] * mlp_branch).astype(BF16).reshape(frames, TILE, width)

        upstream = grad_out[...].reshape(block, width).astype(F32)
        sums[5:6] += column_sum(upstream * mlp_branch)
        grad_value = (upstream * mods[8:9]).astype(BF16)
        grad_second[...] = grad_value
        bias_sums[:, hidden_width:] += column_sum(grad_value.astype(F32))
        grad_act = 0.0
        for chunk in range(chunks):
            cut = slice(width * chunk, width * chunk + width)
            value = (nt(grad_value, second[cut]) * derived[:, cut]).astype(BF16)
            grad_pre[:, cut] = value
            bias_sums[:, cut] += column_sum(value.astype(F32))
            grad_act += nt(value, first[:, cut])
        sums[3:4] += column_sum(grad_act)
        sums[4:5] += column_sum(grad_act * mlp_norm)
        upstream = upstream + norm_back(grad_act, mlp_norm, mlp_inverse, mods[7:8])

        sums[2:3] += column_sum(upstream * time_branch[...])
        grad_value = (upstream * mods[5:6]).astype(BF16)
        grad_branch[...] = grad_value
        grad_heads = nt(grad_value, time_out[...]).astype(BF16)
        apart = apart_bias(block)
        for pair in range(pairs):
            cuts = part_cuts(pair, width)
            queries, keys, values = (packed[:, cut] for cut in cuts)
            logs = totals[0, pair]
            parts = pair_back(
                queries, keys, values, grad_heads[:, cuts[0]], (logs[0:1], logs[1:2]), apart
            )
            for cut, part in zip(cuts, parts):
                grad_packed[:, cut] = part
        grad_act = nt(grad_packed[...], time_in[...]).astype(BF16).astype(F32)
        time_norm, time_inverse = normalise(current)
        sums[0:1] += column_sum(grad_act)
        sums[1:2] += column_sum(grad_act * time_norm)
        upstream = upstream + norm_back(grad_act, time_norm, time_inverse, mods[4:5])
        grad_after[...] = upstream.astype(BF16).reshape(frames, TILE, width)

    moving = pl.BlockSpec((frames, TILE, width), lambda i: (0, i, 0))

    def rows(columns):
        return pl.BlockSpec((block, columns), lambda i: (i, 0))

    def array(columns):
        return jax.ShapeDtypeStruct((length, columns), BF16)

    narrow, wide, triple = width, hidden_width, 3 * width
    kept = [narrow, wide, narrow, wide, narrow, triple]
    held = (mods, first_bias, second_bias, time_in, time_out)
    shares = mlp_full.reshape(count, share, 2 * hidden_width)
    return pl.pallas_call(
        body,
        grid=(spots // TILE,),
        in_specs=[moving, moving, rows(triple), rows(width)]
        + [pl.BlockSpec((1, pairs, 2, block), lambda i: (i, 0, 0, 0))]
        + [whole(a.shape) for a in held]
        + [
            pl.BlockSpec((depth, hidden_width), lambda i: (0, 0), pipeline_mode=pl.Buffered(1)),
            pl.BlockSpec(
                (count, share, hidden_width), lambda i: (0, 0, 1), pipeline_mode=pl.Buffered(1)
            ),
        ],
        out_specs=[moving, moving]
        + [rows(c) for c in kept]
        + [whole_out((8, width)), whole_out((1, hidden_width + width))],
        out_shape=[jax.ShapeDtypeStruct(after.shape, BF16)] * 2
        + [array(c) for c in kept]
        + [
            jax.ShapeDtypeStruct((8, width), F32),
            jax.ShapeDtypeStruct((1, hidden_width + width), F32),
        ],
        scratch_shapes=[
            pltpu.VMEM((block, hidden_width), F32),
            pltpu.VMEM((hidden_width, width), BF16),
        ],
        compiler_params=params(60),
        cost_estimate=cost(40e9, 50 * MIB, 8e6),
        name="middle",
    )(after, grad_out, packed, time_branch, totals, *held, mlp_full, shares)


def local(
    count,
    tokens,
    condition,
    patch_mask,
    grad_out,
    mod_weight,
    mod_bias,
    space_qkv,
    space_proj,
    time_qkv,
    time_proj,
    mlp_in,
    in_bias,
    mlp_out,
    out_bias,
):
    length, width = tokens.shape
    patches = patch_mask.shape[1]
    frame_dev = length // patches
    groups = condition.shape[0]
    clip_dev = FRAMES // frame_dev
    spots = patches // clip_dev
    sp_size = lax.axis_size("sp")
    shard = mod_weight.shape[0]
    mod_width = mod_weight.shape[1]
    hidden_width = mlp_in.shape[1]
    me = lax.axis_index("dp") * sp_size + lax.axis_index("sp")
    chip = me // 2
    core = me % 2
    clip_row = lax.axis_index("sp") // clip_dev
    order_a, order_b = chip_orders(count)
    teams = [list(range(s, s + clip_dev)) for s in range(0, sp_size, clip_dev)]

    def across(values):
        return lax.all_to_all(
            values, "sp", split_axis=0, concat_axis=0, tiled=True, axis_index_groups=teams
        )

    near = jnp.stack([condition[clip_row ^ s] for s in range(groups)])
    mask = sp_size
    while mask < count:
        near = jnp.concatenate([near, swap(near, mask, count)], axis=0)
        mask *= 2
    lifted = jax.nn.silu(near.astype(F32)).astype(BF16)
    lifted_rows = lax.dynamic_slice_in_dim(lifted, me * shard, shard, 1)
    part = jnp.dot(lifted_rows, mod_weight, preferred_element_type=F32)
    own = jnp.zeros((mod_width + hidden_width + width,), F32)
    own = lax.dynamic_update_slice(own, mod_bias.astype(F32), (me * mod_bias.shape[0],))
    own = lax.dynamic_update_slice(
        own, in_bias.astype(F32), (mod_width + me * in_bias.shape[0],)
    )
    own = lax.dynamic_update_slice(
        own, out_bias.astype(F32), (mod_width + hidden_width + me * out_bias.shape[0],)
    )
    row = jnp.pad(part, ((0, 0), (0, hidden_width + width))) + own[None]
    mask = count // 2
    while mask >= clip_dev:
        half = row.shape[0] // 2
        row = row[:half] + swap(row[half:], mask, count)
        mask //= 2
    row = clip_total(row, clip_dev // 2, count)
    mods = row[0, :mod_width].reshape(9, width)
    first_bias = row[:, mod_width : mod_width + hidden_width]
    second_bias = row[:, mod_width + hidden_width :]

    hidden_share = mlp_out.shape[0] // shard
    if shard % 8:
        mlp_share = 8
        full = lax.all_gather(mlp_out, AXES, axis=0, tiled=True)
        full = full.reshape(-1, hidden_share, mlp_share, width)
        full = jnp.transpose(full, (0, 2, 1, 3)).reshape(-1, hidden_width)
        mlp_full = jnp.concatenate([lax.all_gather(mlp_in, AXES, axis=0, tiled=True), full], axis=1)
    else:
        mlp_share = shard
        packed_out = [mlp_out[i * shard : (i + 1) * shard] for i in range(hidden_share)]
        mlp_full = lax.all_gather(
            jnp.concatenate([mlp_in] + packed_out, axis=1), AXES, axis=0, tiled=True
        )
    cut = (space_qkv.shape[1] + width) // 2
    wanted = [
        space_qkv[:, :cut],
        jnp.concatenate([space_qkv[:, cut:], space_proj], axis=1),
        jnp.concatenate([time_qkv, time_proj], axis=1),
    ]
    if shard % 8:
        held = []
        for part in wanted:
            full = lax.all_gather(part, AXES, axis=0, tiled=True).reshape(-1, 2, 8, part.shape[1])
            held.append((full[:, 0], full[:, 1]))
        time_held = held.pop()
        spots_held = held[0][0].shape[0]
        table = jnp.stack(
            [jnp.arange(spots_held, dtype=jnp.int32)] * 2 + [jnp.zeros((spots_held,), jnp.int32)]
        )
        time_steps = []
    else:
        time_steps = list(order_a)
        time_own = wanted[2][None]

        def time_step(value):
            nonlocal time_own
            got = swap(time_own, time_steps.pop(0), count)
            value, time_own = lax.optimization_barrier(
                (value, jnp.concatenate([time_own, got], axis=0))
            )
            return value

        one, two = wanted[0][None], wanted[1][None]
        for step, (mask_a, mask_b) in enumerate(zip(order_a, order_b)):
            if step >= 2 and len(time_steps) > 2:
                one = time_step(one)
            got = swap(one, mask_a, count), swap(two, mask_b, count)
            one = jnp.concatenate([one, got[0]], axis=0)
            two = jnp.concatenate([two, got[1]], axis=0)
        held = [(one, swap(one, 1, count)), (two, swap(two, 1, count))]
        table = place_table((order_a, order_b), chip, core, count)

    mask_row = lax.dynamic_index_in_dim(patch_mask, clip_row, 0, keepdims=False)
    key_bias = jnp.where(mask_row == 1, 0.0, MASKED).astype(F32)[:, None]
    space_act, space_packed, space_full, space_out = space_project(tokens, mods, table, held)
    if time_steps:
        space_packed = time_step(space_packed)
    space_heads, space_total, space_branch, after_space = space_forward(
        space_packed, tokens, mods, key_bias, space_out, patches, clip_dev
    )
    if time_steps:
        after_space = time_step(after_space)
    after_here = across(after_space)
    if shard % 8 == 0:
        time_held = time_own, swap(time_own, 1, count)

    shape = (clip_dev, frame_dev, spots, width)
    flat_shape = (FRAMES, spots, width)
    grad_here = jnp.transpose(grad_out.reshape(frame_dev, clip_dev, spots, width), (1, 0, 2, 3))
    after_here, time_held, grad_here = lax.optimization_barrier((after_here, time_held, grad_here))
    after_here = after_here.reshape(flat_shape)
    grad_here = across(grad_here)
    times = time_forward(after_here, mods, table, *time_held)
    times, grad_here = lax.optimization_barrier((times, grad_here))
    time_act, time_packed, time_heads, time_branch, time_total, time_full, time_out = times
    (
        out_here,
        grad_here,
        mlp_act,
        hidden,
        grad_second,
        grad_pre,
        grad_time_branch,
        grad_time_packed,
        sums,
        bias_sums,
    ) = middle(
        after_here,
        grad_here.reshape(flat_shape),
        time_packed,
        time_branch,
        time_total,
        mods,
        first_bias,
        second_bias,
        time_full,
        time_out,
        mlp_full,
        mlp_share,
    )

    turn_a, turn_b = order_a[::-1], order_b[::-1]
    turn_a[1], turn_a[2] = turn_a[2], turn_a[1]

    def reduced(groups, order):
        return weight_grads(groups, order, chip, core, count, shard, width)

    grad_after = across(grad_here.reshape(shape))
    wide = hidden_width // width
    shares = reduced([(mlp_act, grad_pre, 0, wide), (time_act, grad_time_packed, 0, 2)], turn_a)
    shares, grad_after, hidden, out_here = lax.optimization_barrier(
        (shares, grad_after, hidden, out_here)
    )
    fold_a = Fold(shares, turn_a, count)
    out_back = across(out_here.reshape(shape))
    shares = reduced(
        [
            (hidden, grad_second, 0, 1),
            (time_act, grad_time_packed, 2, 1),
            (time_heads, grad_time_branch, 0, 1),
        ],
        turn_b,
    )
    shares, out_back, grad_after = meet((shares, out_back, grad_after), fold_a)
    fold_b = Fold(shares, turn_b, count)
    grad_space_branch, grad_space_heads, grad_gate = space_branch_back(
        grad_after, space_branch, mods, space_out, patches
    )
    grad_space_branch, grad_space_heads, grad_gate = meet(
        (grad_space_branch, grad_space_heads, grad_gate), fold_b
    )
    grads = space_back(
        space_packed,
        grad_space_heads,
        space_total,
        key_bias,
        space_full,
        tokens,
        grad_after,
        mods,
        patches,
    )
    grad_q, grad_k, grad_v, grad_tokens, space_sums, out_back, grad_gate = meet(
        (*grads, out_back, grad_gate), fold_a, fold_b
    )
    out_tokens = jnp.transpose(out_back, (1, 0, 2, 3)).reshape(length, width)
    rows = jnp.concatenate(
        [space_sums.reshape(1, -1), grad_gate, sums[:6].reshape(1, -1), bias_sums], axis=1
    )
    got = swap(rows, clip_dev // 2, count)
    shares = reduced([(space_heads, grad_space_branch, 0, 1), (space_act, grad_q, 0, 1)], turn_a)
    shares, grad_k, rows, got = lax.optimization_barrier((shares, grad_k, rows, got))
    rows = rows + got
    fold_c = Fold(shares, turn_a, count)
    mask = clip_dev // 4
    if mask:
        got = swap(rows, mask, count)
    shares = reduced([(space_act, grad_k, 0, 1), (space_act, grad_v, 0, 1)], turn_b)
    shares, rows, got = meet((shares, rows, got), fold_a, fold_b, fold_c)
    fold_d = Fold(shares, turn_b, count)
    if mask:
        rows = clip_total(rows + got, mask // 2, count)
    rows = meet(rows, fold_d)
    mask = clip_dev
    folds = [fold_a, fold_b, fold_c, fold_d]
    while mask < count:
        rows = jnp.concatenate([rows, swap(rows, mask, count)], axis=0)
        rows = meet(rows, *[fold for fold in folds if len(fold.masks) > 1])
        mask *= 2
    grad_a, grad_b = fold_a.finish(), fold_b.finish()
    grad_rows = rows[:, :mod_width]
    grad_lifted = lax.dot_general(
        grad_rows,
        mod_weight.astype(F32),
        (((1,), (1,)), ((), ())),
        precision=lax.Precision.HIGHEST,
        preferred_element_type=F32,
    )
    near_clips = jnp.arange(count // clip_dev) ^ (me // clip_dev)
    grad_lifted = jnp.take(grad_lifted, near_clips, axis=0)
    grad_lifted = jnp.repeat(
        grad_lifted.reshape(count // sp_size, 1, groups * shard), sp_size, axis=1
    ).reshape(count, groups * shard)
    grad_lifted = lax.all_to_all(grad_lifted, AXES, split_axis=0, concat_axis=0, tiled=True)
    while len(fold_d.masks) > 1:
        grad_a, grad_b = meet(
            (grad_a, grad_b), *[fold for fold in (fold_c, fold_d) if len(fold.masks) > 1]
        )
    grad_c, grad_d = fold_c.finish(), fold_d.finish()
    grad_mlp_in = grad_a[:, :hidden_width]
    grad_mlp_out = jnp.concatenate(
        [grad_b[:, i * width : (i + 1) * width] for i in range(hidden_share)], axis=0
    )
    grad_time_qkv = jnp.concatenate(
        [grad_a[:, hidden_width:], grad_b[:, hidden_width : hidden_width + width]], axis=1
    )
    grad_time_proj = grad_b[:, hidden_width + width :]
    grad_space_proj = grad_c[:, :width]
    grad_space_qkv = jnp.concatenate([grad_c[:, width:], grad_d], axis=1)

    grad_mod_weight = lax.dot_general(
        lifted_rows.astype(F32),
        grad_rows,
        (((0,), (0,)), ((), ())),
        precision=lax.Precision.HIGHEST,
        preferred_element_type=F32,
    )
    totals = jnp.sum(rows, axis=0)
    grad_mod_bias = lax.dynamic_slice_in_dim(totals, me * mod_bias.shape[0], mod_bias.shape[0])
    grad_in_bias = lax.dynamic_slice_in_dim(
        totals, mod_width + me * in_bias.shape[0], in_bias.shape[0]
    )
    grad_out_bias = lax.dynamic_slice_in_dim(
        totals, mod_width + hidden_width + me * out_bias.shape[0], out_bias.shape[0]
    )
    grad_lifted = jnp.transpose(grad_lifted.reshape(count, groups, shard), (1, 0, 2))
    grad_lifted = grad_lifted.reshape(groups, width)
    _, silu_back = jax.vjp(jax.nn.silu, condition.astype(F32))
    grad_condition = silu_back(grad_lifted)[0]

    return (
        out_tokens,
        grad_tokens,
        grad_condition,
        grad_mod_weight,
        grad_mod_bias,
        grad_space_qkv,
        grad_space_proj,
        grad_time_qkv,
        grad_time_proj,
        grad_mlp_in,
        grad_in_bias,
        grad_mlp_out,
        grad_out_bias,
    )


def solution(mesh):
    count = mesh.shape["dp"] * mesh.shape["sp"]
    both = P(AXES, None)
    flat = P(AXES)
    clips = P("dp", None)
    return jax.shard_map(
        functools.partial(local, count),
        mesh=mesh,
        in_specs=(
            both, clips, clips, both, both, flat, both, both, both, both, both, flat, both, flat,
        ),
        out_specs=(
            both, both, clips, both, flat, both, both, both, both, both, flat, both, flat,
        ),
        check_vma=False,
    )
```

```python
import functools
import math

import jax
import jax.numpy as jnp
from jax import lax
from jax.experimental import pallas as pl
from jax.experimental.pallas import tpu as pltpu
from jax.sharding import PartitionSpec as P

HEADS = 12
HEAD_DIM = 64
FRAMES = 16
EPSILON = 1e-06
MASKED = -10000.0
APART = -1e30
AXES = ("dp", "sp")
F32 = jnp.float32
BF16 = jnp.bfloat16
MIB = 1 << 20


def swap(values, mask, count):
    return lax.ppermute(values, AXES, [(i, i ^ mask) for i in range(count)])


def chip_orders(count):
    bits = [1 << i for i in range(1, count.bit_length() - 1)]
    low, high, middle = bits[0], bits[-1], bits[1:-1][::-1]
    return (middle + [high, low], middle + [low, high])


def spread(shard, order, count):
    held = shard[None]
    for mask in order:
        held = jnp.concatenate([held, swap(held, mask, count)], axis=0)
    return held


def spread_places(order, count):
    places = []
    for distance in range(count // 2):
        places.append(sum(1 << s for s, mask in enumerate(order) if distance & (mask >> 1)))
    return places


def fold_places(order, count):
    steps = len(order)
    places = []
    for distance in range(count // 2):
        places.append(
            sum(1 << (steps - 1 - s) for s, mask in enumerate(order) if distance & (mask >> 1))
        )
    return places


class Fold:
    def __init__(self, shares, order, count):
        self.keep, self.send = shares
        self.masks = [1] + list(order)
        self.count = count
        self.got = swap(self.send, 1, count)

    def add(self):
        half = self.keep.shape[0] // 2
        low = self.keep[:half].astype(F32) + self.got[:half].astype(F32)
        high = self.keep[half:].astype(F32) + self.got[half:].astype(F32)
        self.keep, self.send = low.astype(BF16), high.astype(BF16)
        self.masks.pop(0)

    def go(self):
        self.got = swap(self.send, self.masks[0], self.count)

    def finish(self):
        while len(self.masks) > 1:
            self.add()
            self.go()
        return self.keep[0].astype(F32) + self.got[0].astype(F32)


def meet(values, *folds):
    values, states = lax.optimization_barrier(
        (values, [(f.keep, f.got) for f in folds])
    )
    for fold, (fold.keep, fold.got) in zip(folds, states):
        fold.add()
    values, states = lax.optimization_barrier((values, [(f.keep, f.send) for f in folds]))
    for fold, (fold.keep, fold.send) in zip(folds, states):
        fold.go()
    return values


def clip_total(row, mask, count):
    while mask:
        row = row + swap(row, mask, count)
        mask //= 2
    return row


def nn(a, b):
    return jnp.dot(a, b, preferred_element_type=F32)


def nt(a, b):
    return lax.dot_general(a, b, (((1,), (1,)), ((), ())), preferred_element_type=F32)


def tn(a, b):
    return lax.dot_general(a, b, (((0,), (0,)), ((), ())), preferred_element_type=F32)


def normalise(values):
    average = jnp.mean(values, axis=-1, keepdims=True)
    centred = values - average
    inverse = lax.rsqrt(jnp.mean(centred * centred, axis=-1, keepdims=True) + EPSILON)
    return centred * inverse, inverse


def norm_back(grad_mod, normed, inverse, scale):
    grad_normed = grad_mod * (1.0 + scale)
    inner = jnp.mean(grad_normed * normed, axis=-1, keepdims=True)
    average = jnp.mean(grad_normed, axis=-1, keepdims=True)
    return inverse * (grad_normed - average - normed * inner)


def column_sum(values):
    return jnp.sum(values, axis=0, keepdims=True)


def halves():
    lane = lax.broadcasted_iota(jnp.int32, (1, 2 * HEAD_DIM), 1)
    first = (lane < HEAD_DIM).astype(F32)
    return first.astype(BF16), (1.0 - first).astype(BF16)


def turned(values):
    return jnp.transpose(values.astype(F32), (1, 0))


def key_lanes(bias, half):
    lane = lax.broadcasted_iota(jnp.int32, (1, 2 * HEAD_DIM), 1) - (1 - half) * HEAD_DIM
    large = bias.astype(BF16).astype(F32)
    lanes = large * (lane == 0).astype(F32) + (bias - large) * (lane == 1).astype(F32)
    return lanes.astype(BF16)


def query_lanes(half):
    lane = lax.broadcasted_iota(jnp.int32, (1, 2 * HEAD_DIM), 1) - (1 - half) * HEAD_DIM
    return jnp.logical_or(lane == 0, lane == 1).astype(F32).astype(BF16)


def biased_scores(queries, keys, half, mask, lanes):
    if lanes is None:
        return nt(keys * (mask * 0.125), queries)
    return nt(keys * (mask * 0.125) + lanes[half], queries * mask + query_lanes(half))


def heads_forward(pairs, apart=None, lanes=None):
    masks = halves()

    def scores_of(item):
        queries, keys, _ = pairs[item // 2]
        return biased_scores(queries, keys, item % 2, masks[item % 2], lanes)

    coming = scores_of(0)
    results = []
    for item in range(2 * len(pairs)):
        scores = coming if apart is None else spaced(coming, apart)
        if item + 1 < 2 * len(pairs):
            coming = scores_of(item + 1)
        if item % 2 == 0:
            values_t = turned(pairs[item // 2][2]).astype(BF16)
            parts, totals = [], []
        largest = jnp.max(scores, axis=0, keepdims=True)
        exponent = jnp.exp(scores - largest)
        denominator = jnp.sum(exponent, axis=0, keepdims=True)
        half = item % 2
        attended = nn(values_t[half * HEAD_DIM : (half + 1) * HEAD_DIM], exponent.astype(BF16))
        parts.append(attended * (1.0 / denominator))
        totals.append(largest + jnp.log(denominator))
        if half == 1:
            attended = jnp.transpose(jnp.concatenate(parts, axis=0), (1, 0)).astype(BF16)
            results.append((attended, jnp.concatenate(totals, axis=0)))
    return results


def spaced(scores, apart):
    rows, lanes = apart.shape
    parts = []
    for start in range(0, scores.shape[1], lanes):
        part = scores[:, start : start + lanes].reshape(-1, rows, lanes) + apart[None]
        parts.append(part.reshape(-1, lanes))
    return jnp.concatenate(parts, axis=1)


def heads_back(pairs, apart=None, lanes=None):
    masks = halves()

    def products_of(item):
        queries, keys, values, grad, _, _ = pairs[item // 2]
        mask = masks[item % 2]
        scores = biased_scores(queries, keys, item % 2, mask, lanes)
        return scores, nt(values * mask, grad)

    coming = products_of(0)
    results = []
    for item in range(2 * len(pairs)):
        scores, grad_probs = coming
        if item + 1 < 2 * len(pairs):
            coming = products_of(item + 1)
        half = item % 2
        queries, keys, _, grad, totals, inner = pairs[item // 2]
        if half == 0:
            keys_t = turned(keys).astype(BF16)
            grad_queries, grad_keys, grad_values = [], 0.0, 0.0
        if apart is not None:
            scores = spaced(scores, apart)
        probable = jnp.exp(scores - totals[half : half + 1])
        grad_scores = (probable * (grad_probs - inner[half : half + 1])).astype(BF16)
        mask = masks[half]
        grad_values += nn(probable.astype(BF16), grad * mask)
        grad_keys += nn(grad_scores, queries * (mask * 0.125))
        grad_queries.append(nn(keys_t[half * HEAD_DIM : (half + 1) * HEAD_DIM], grad_scores))
        if half == 1:
            grad_queries = jnp.transpose(jnp.concatenate(grad_queries, axis=0), (1, 0)) * 0.125
            results.append(
                (grad_queries.astype(BF16), grad_keys.astype(BF16), grad_values.astype(BF16))
            )
    return results


def inner_sums(heads, grad_heads):
    width = heads.shape[1]
    head = lax.broadcasted_iota(jnp.int32, (16, width), 0)
    lane = lax.broadcasted_iota(jnp.int32, (16, width), 1)
    chosen = (lane // HEAD_DIM == head).astype(F32).astype(BF16)
    product = heads.astype(F32) * grad_heads.astype(F32)
    large = product.astype(BF16)
    return nt(chosen, large) + nt(chosen, (product - large.astype(F32)).astype(BF16))


def whole(shape):
    return pl.BlockSpec(shape, lambda *_: (0,) * len(shape), pipeline_mode=pl.Buffered(1))


def whole_out(shape):
    return pl.BlockSpec(shape, lambda *_: (0,) * len(shape))


def params(limit=56):
    return pltpu.CompilerParams(vmem_limit_bytes=limit * MIB)


def cost(flops, moved, special=0):
    return pl.CostEstimate(flops=int(flops) // 16, bytes_accessed=int(moved) // 16, transcendentals=0)


def place_table(orders, chip, core, count):
    chips = count // 2
    index = jnp.arange(chips) ^ chip
    return jnp.stack(
        [jnp.array(spread_places(order, count), jnp.int32)[index] for order in orders]
        + [jnp.full((chips,), core, jnp.int32)]
    )


def build(table, row, own, other, runs):
    chips, share, _ = own.shape
    odd = table[table.shape[0] - 1, 0] == 1

    def step(i, carry):
        place = table[row, i]
        one = own[place].astype(F32)
        two = other[place].astype(F32)
        joined = jnp.concatenate(
            [jnp.where(odd, two, one), jnp.where(odd, one, two)], axis=0
        ).astype(BF16)
        rows = pl.ds(pl.multiple_of(i * 2 * share, 2 * share), 2 * share)
        for column, width, target, start in runs:
            target[rows, start : start + width] = joined[:, column : column + width]
        return carry

    lax.fori_loop(0, chips, step, 0)


def weight_grads(sheets, chip, core, count, share, block, deep=None):
    chips = count // 2
    groups = [group for sheet, _ in sheets for group in sheet]
    length = groups[0][0].shape[0]
    depth = count * share
    steps = [group[3] for group in groups]
    starts = [sum(steps[:i]) for i in range(len(steps))]
    sizes = [sum(group[3] for group in sheet) for sheet, _ in sheets]
    sheet_starts = [sum(sizes[:i]) for i in range(len(sizes))]
    owners = [i for i, (sheet, _) in enumerate(sheets) for _ in sheet]
    total = sum(steps)
    extra = deep[0].shape[1] // block if deep else 0
    orders = [order for _, order in sheets] + ([deep[2]] if deep else [])
    distances = jnp.arange(chips) ^ chip
    table = jnp.concatenate(
        [jnp.array(fold_places(order, count), jnp.int32)[distances] for order in orders]
        + [jnp.full((1,), core, jnp.int32)]
    )

    def body(table, *refs):
        ins, outs = refs[: len(operands)], refs[len(operands) : -1]
        acts_t = refs[-1]
        j = pl.program_id(0)
        odd = table[chips * len(orders)] == 1
        for index, owner in enumerate(owners):
            acts, grads = ins[2 * index : 2 * index + 2]
            keep, send = outs[2 * owner : 2 * owner + 2]
            here = j - starts[index]

            @pl.when(here == 0)
            def _():
                acts_t[...] = turned(acts[...]).astype(BF16)

            @pl.when(jnp.logical_and(here >= 0, here < steps[index]))
            def _():
                product = nn(acts_t[...], grads[...])
                for pair in range(chips):
                    place = table[owner * chips + pair]
                    start = 2 * pair * share
                    first = product[start : start + share]
                    second = product[start + share : start + 2 * share]
                    keep[place] = jnp.where(odd, second, first).astype(BF16)
                    send[place] = jnp.where(odd, first, second).astype(BF16)

        if deep:
            keep, send = outs[-2:]
            rows = keep.shape[1]
            pairs = block // (2 * rows)

            @pl.when(j >= total)
            def _():
                product = tn(ins[-2][...], ins[-1][...])
                for pair in range(pairs):
                    place = table[len(sheets) * chips + (j - total) * pairs + pair]
                    start = 2 * pair * rows
                    first = product[start : start + rows]
                    second = product[start + rows : start + 2 * rows]
                    keep[place] = jnp.where(odd, second, first).astype(BF16)
                    send[place] = jnp.where(odd, first, second).astype(BF16)

    in_specs = []
    operands = []
    for start, step, (acts, grads, g_first, _) in zip(starts, steps, groups):
        in_specs.append(pl.BlockSpec((length, depth), lambda j, t: (0, 0)))
        in_specs.append(
            pl.BlockSpec(
                (length, block),
                lambda j, t, s=start, m=step, g=g_first: (0, g + jnp.clip(j - s, 0, m - 1)),
            )
        )
        operands += [acts, grads]
    out_specs = []
    out_shape = []
    for start, size in zip(sheet_starts, sizes):
        out_specs += [
            pl.BlockSpec(
                (chips, share, block),
                lambda j, t, s=start, m=size: (0, 0, jnp.clip(j - s, 0, m - 1)),
            )
        ] * 2
        out_shape += [jax.ShapeDtypeStruct((chips, share, size * block), BF16)] * 2
    if deep:
        in_specs.append(
            pl.BlockSpec((length, block), lambda j, t: (0, jnp.clip(j - total, 0, extra - 1)))
        )
        in_specs.append(pl.BlockSpec(deep[1].shape, lambda j, t: (0, 0)))
        operands += list(deep[:2])
        shape = (chips, deep[0].shape[1] // count, deep[1].shape[1])
        out_specs += [whole_out(shape)] * 2
        out_shape += [jax.ShapeDtypeStruct(shape, BF16)] * 2
    return pl.pallas_call(
        body,
        grid_spec=pltpu.PrefetchScalarGridSpec(
            num_scalar_prefetch=1,
            grid=(total + extra,),
            in_specs=in_specs,
            out_specs=out_specs,
            scratch_shapes=[pltpu.VMEM((depth, length), BF16)],
        ),
        out_shape=out_shape,
        compiler_params=params(),
        cost_estimate=cost(2 * length * depth * total * block, 4 * depth * total * block),
        name="weight_grads",
    )(table, *operands)


def space_project(tokens, mods, table, held):
    length, width = tokens.shape
    depth = held[0][0].shape[0] * held[0][0].shape[1] * 2
    wide = 3 * width
    cut = held[0][0].shape[2]
    block = 256

    def body(table, tokens, mods, own_a, other_a, own_b, other_b, act, packed, weight, last):
        @pl.when(pl.program_id(0) == 0)
        def _():
            build(table, 0, own_a, other_a, [(0, cut, weight, 0)])
            build(
                table, 1, own_b, other_b, [(0, wide - cut, weight, cut), (wide - cut, width, last, 0)]
            )

        normed, _ = normalise(tokens[...].astype(F32))
        value = (normed * (1.0 + mods[1:2]) + mods[0:1]).astype(BF16)
        act[...] = value
        packed[...] = nn(value, weight[...]).astype(BF16)

    parts = [part for pair in held for part in pair]
    return pl.pallas_call(
        body,
        grid_spec=pltpu.PrefetchScalarGridSpec(
            num_scalar_prefetch=1,
            grid=(length // block,),
            in_specs=[pl.BlockSpec((block, width), lambda i, t: (i, 0)), whole(mods.shape)]
            + [whole(part.shape) for part in parts],
            out_specs=[
                pl.BlockSpec((block, width), lambda i, t: (i, 0)),
                pl.BlockSpec((block, wide), lambda i, t: (i, 0)),
                whole_out((depth, wide)),
                whole_out((depth, width)),
            ],
        ),
        out_shape=[
            jax.ShapeDtypeStruct((length, width), BF16),
            jax.ShapeDtypeStruct((length, wide), BF16),
            jax.ShapeDtypeStruct((depth, wide), BF16),
            jax.ShapeDtypeStruct((depth, width), BF16),
        ],
        compiler_params=params(),
        cost_estimate=cost(2 * length * width * wide, 16 * MIB),
        name="space_project",
    )(table, tokens, mods, *parts)


def space_forward(packed, tokens, mods, bias, weight, patches, peers):
    length, width = tokens.shape
    frames = length // patches
    pairs = width // 128
    spots = patches // peers

    def body(packed, tokens, mods, bias, weight, heads, totals, branch, after):
        lanes = [key_lanes(bias[...], half) for half in range(2)]

        def step(pair, carry):
            at = pl.multiple_of(pair * 128, 128)
            parts = [packed[:, pl.ds(part * width + at, 128)] for part in range(3)]
            ((attended, logs),) = heads_forward([parts], lanes=lanes)
            heads[:, pl.ds(at, 128)] = attended
            totals[0, pair] = logs
            return carry

        lax.fori_loop(0, pairs, step, 0)
        product = nn(heads[...], weight[...])
        branch[...] = product.astype(BF16)
        result = (tokens[...].astype(F32) + mods[2:3] * product).astype(BF16)
        for peer in range(peers):
            after[peer, 0] = result[peer * spots : (peer + 1) * spots]

    def rows(columns):
        return pl.BlockSpec((patches, columns), lambda f: (f, 0))

    return pl.pallas_call(
        body,
        grid=(frames,),
        in_specs=[rows(3 * width), rows(width)]
        + [whole(a.shape) for a in (mods, bias, weight)],
        out_specs=[
            rows(width),
            pl.BlockSpec((1, pairs, 2, patches), lambda f: (f, 0, 0, 0)),
            rows(width),
            pl.BlockSpec((peers, 1, spots, width), lambda f: (0, f, 0, 0)),
        ],
        out_shape=[
            jax.ShapeDtypeStruct((length, width), BF16),
            jax.ShapeDtypeStruct((frames, pairs, 2, patches), F32),
            jax.ShapeDtypeStruct((length, width), BF16),
            jax.ShapeDtypeStruct((peers, frames, spots, width), BF16),
        ],
        compiler_params=params(),
        cost_estimate=cost(10e9, 10 * MIB, 6e6),
        name="space_forward",
    )(packed, tokens, mods, bias, weight)


def space_branch_back(grad_after, branch, heads, mods, weight, patches):
    peers, frames, spots, width = grad_after.shape
    length = frames * patches

    def body(grad_after, branch, heads, mods, weight, grad_branch, grad_heads, inner, grad_gate):
        upstream = grad_after[...].reshape(patches, width).astype(F32)
        value = (upstream * mods[2:3]).astype(BF16)
        grad_branch[...] = value
        grads = nt(value, weight[...]).astype(BF16)
        grad_heads[...] = grads
        rows = inner_sums(heads[...], grads)
        for pair in range(inner.shape[1]):
            inner[0, pair] = rows[2 * pair : 2 * pair + 2]

        @pl.when(pl.program_id(0) == 0)
        def _():
            grad_gate[...] = jnp.zeros_like(grad_gate)

        grad_gate[...] += column_sum(upstream * branch[...].astype(F32))

    return pl.pallas_call(
        body,
        grid=(frames,),
        in_specs=[
            pl.BlockSpec((peers, 1, spots, width), lambda f: (0, f, 0, 0)),
            pl.BlockSpec((patches, width), lambda f: (f, 0)),
            pl.BlockSpec((patches, width), lambda f: (f, 0)),
            whole(mods.shape),
            whole(weight.shape),
        ],
        out_specs=[
            pl.BlockSpec((patches, width), lambda f: (f, 0)),
            pl.BlockSpec((patches, width), lambda f: (f, 0)),
            pl.BlockSpec((1, width // 128, 2, patches), lambda f: (f, 0, 0, 0)),
            whole_out((1, width)),
        ],
        out_shape=[
            jax.ShapeDtypeStruct((length, width), BF16),
            jax.ShapeDtypeStruct((length, width), BF16),
            jax.ShapeDtypeStruct((frames, width // 128, 2, patches), F32),
            jax.ShapeDtypeStruct((1, width), F32),
        ],
        compiler_params=params(),
        cost_estimate=cost(2 * length * width * width, 8 * MIB),
        name="space_branch_back",
    )(grad_after, branch, heads, mods, weight)


def space_back(packed, grad_heads, totals, inner, bias, weight, tokens, grad_after, mods, patches):
    peers, frames, spots, width = grad_after.shape
    length = frames * patches
    pairs = width // 128

    def body(
        packed, grad_heads, totals, inner, bias, weight, tokens, grad_after, mods,
        grad_q, grad_k, grad_v, grad_tokens, sums,
    ):
        lanes = [key_lanes(bias[...], half) for half in range(2)]

        def step(pair, carry):
            at = pl.multiple_of(pair * 128, 128)
            parts = [packed[:, pl.ds(part * width + at, 128)] for part in range(3)]
            rest = [grad_heads[:, pl.ds(at, 128)], totals[0, pair], inner[0, pair]]
            (results,) = heads_back([parts + rest], lanes=lanes)
            for out, result in zip((grad_q, grad_k, grad_v), results):
                out[:, pl.ds(at, 128)] = result
            return carry

        lax.fori_loop(0, pairs, step, 0)

        @pl.when(pl.program_id(0) == 0)
        def _():
            sums[...] = jnp.zeros_like(sums)

        grad_act = nt(grad_q[...], weight[:, :width])
        grad_act += nt(grad_k[...], weight[:, width : 2 * width])
        grad_act += nt(grad_v[...], weight[:, 2 * width :])
        normed, inverse = normalise(tokens[...].astype(F32))
        upstream = grad_after[...].reshape(patches, width).astype(F32)
        grad_tokens[...] = (
            upstream + norm_back(grad_act, normed, inverse, mods[1:2])
        ).astype(BF16)
        sums[0:1] += column_sum(grad_act)
        sums[1:2] += column_sum(grad_act * normed)

    def rows(columns):
        return pl.BlockSpec((patches, columns), lambda f: (f, 0))

    flat = jax.ShapeDtypeStruct((length, width), BF16)
    return pl.pallas_call(
        body,
        grid=(frames,),
        in_specs=[
            rows(3 * width),
            rows(width),
            pl.BlockSpec((1, pairs, 2, patches), lambda f: (f, 0, 0, 0)),
            pl.BlockSpec((1, pairs, 2, patches), lambda f: (f, 0, 0, 0)),
            whole(bias.shape),
            whole(weight.shape),
            rows(width),
            pl.BlockSpec((peers, 1, spots, width), lambda f: (0, f, 0, 0)),
            whole(mods.shape),
        ],
        out_specs=[rows(width)] * 4 + [whole_out((2, width))],
        out_shape=[flat, flat, flat, flat, jax.ShapeDtypeStruct((2, width), F32)],
        compiler_params=params(),
        cost_estimate=cost(24e9, 20 * MIB, 6e6),
        name="space_back",
    )(packed, grad_heads, totals, inner, bias, weight, tokens, grad_after, mods)


TILE = 16


def apart_bias():
    row = lax.broadcasted_iota(jnp.int32, (TILE, 128), 0)
    column = lax.broadcasted_iota(jnp.int32, (TILE, 128), 1)
    return jnp.where((row & (TILE - 1)) == (column & (TILE - 1)), 0.0, APART)


def part_cuts(pair, width):
    return [slice(p * width + 128 * pair, p * width + 128 * pair + 128) for p in range(3)]


def time_forward(after, mods, table, own, other):
    frames, spots, width = after.shape
    depth = own.shape[0] * own.shape[1] * 2
    block = frames * TILE
    length = frames * spots
    pairs = width // 128

    def body(table, after, mods, own, other, act, packed, heads, branch, totals, time_in, time_out):
        @pl.when(pl.program_id(0) == 0)
        def _():
            build(
                table, 0, own, other, [(0, 3 * width, time_in, 0), (3 * width, width, time_out, 0)]
            )

        apart = apart_bias()
        normed, _ = normalise(after[...].reshape(block, width).astype(F32))
        value = (normed * (1.0 + mods[4:5]) + mods[3:4]).astype(BF16)
        act[...] = value
        packed[...] = nn(value, time_in[...]).astype(BF16)
        parts = [[packed[:, cut] for cut in part_cuts(pair, width)] for pair in range(pairs)]
        for pair, (attended, logs) in enumerate(heads_forward(parts, apart)):
            heads[:, 128 * pair : 128 * pair + 128] = attended
            totals[0, pair] = logs
        branch[...] = nn(heads[...], time_out[...])

    def rows(columns):
        return pl.BlockSpec((block, columns), lambda i, t: (i, 0))

    return pl.pallas_call(
        body,
        grid_spec=pltpu.PrefetchScalarGridSpec(
            num_scalar_prefetch=1,
            grid=(spots // TILE,),
            in_specs=[pl.BlockSpec((frames, TILE, width), lambda i, t: (0, i, 0))]
            + [whole(a.shape) for a in (mods, own, other)],
            out_specs=[
                rows(width),
                rows(3 * width),
                rows(width),
                rows(width),
                pl.BlockSpec((1, pairs, 2, block), lambda i, t: (i, 0, 0, 0)),
                whole_out((depth, 3 * width)),
                whole_out((depth, width)),
            ],
        ),
        out_shape=[
            jax.ShapeDtypeStruct((length, width), BF16),
            jax.ShapeDtypeStruct((length, 3 * width), BF16),
            jax.ShapeDtypeStruct((length, width), BF16),
            jax.ShapeDtypeStruct((length, width), F32),
            jax.ShapeDtypeStruct((spots // TILE, pairs, 2, block), F32),
            jax.ShapeDtypeStruct((depth, 3 * width), BF16),
            jax.ShapeDtypeStruct((depth, width), BF16),
        ],
        compiler_params=params(),
        cost_estimate=cost(8e9, 24 * MIB, 3e6),
        name="time_forward",
    )(table, after, mods, own, other)


def middle(
    after, grad_out, packed, heads, time_branch, totals, mods, first_bias, second_bias, time_in,
    time_out, mlp_full, share,
):
    frames, spots, width = after.shape
    hidden_width = first_bias.shape[1]
    depth = mlp_full.shape[0]
    count = depth // share
    block = frames * TILE
    length = frames * spots
    pairs = width // 128
    chunks = hidden_width // width
    slope = math.sqrt(2.0 / math.pi)

    def body(
        after, grad_out, packed, heads, time_branch, totals,
        mods, first_bias, second_bias, time_in, time_out, first, shares,
        out, grad_after, mlp_act, hidden, grad_second, grad_pre, grad_branch, grad_packed,
        sums, bias_sums, derived, second,
    ):
        @pl.when(pl.program_id(0) == 0)
        def _():
            def unpack(i, carry):
                piece = shares[i].astype(F32)
                parts = [piece[:, c * width : (c + 1) * width] for c in range(chunks)]
                rows = pl.ds(pl.multiple_of(i * chunks * share, chunks * share), chunks * share)
                second[rows] = jnp.concatenate(parts, axis=0).astype(BF16)
                return carry

            lax.fori_loop(0, count, unpack, 0)
            sums[...] = jnp.zeros_like(sums)
            bias_sums[...] = jnp.zeros_like(bias_sums)

        current = after[...].reshape(block, width).astype(F32)
        after_time = current + mods[5:6] * time_branch[...]
        mlp_norm, mlp_inverse = normalise(after_time)
        act = (mlp_norm * (1.0 + mods[7:8]) + mods[6:7]).astype(BF16)
        mlp_act[...] = act
        mlp_branch = 0.0
        for chunk in range(chunks):
            cut = slice(width * chunk, width * chunk + width)
            pre = nn(act, first[:, cut]) + first_bias[:, cut]
            squared = pre * pre
            bent = jnp.tanh(slope * pre * (1.0 + 0.044715 * squared))
            half = 0.5 * (1.0 + bent)
            value = (pre * half).astype(BF16)
            hidden[:, cut] = value
            derived[:, cut] = half + 0.5 * slope * pre * (1.0 - bent * bent) * (
                1.0 + 3.0 * 0.044715 * squared
            )
            mlp_branch += nn(value, second[cut])
        mlp_branch += second_bias[...]
        out[...] = (after_time + mods[8:9] * mlp_branch).astype(BF16).reshape(frames, TILE, width)

        upstream = grad_out[...].reshape(block, width).astype(F32)
        sums[5:6] += column_sum(upstream * mlp_branch)
        grad_value = (upstream * mods[8:9]).astype(BF16)
        grad_second[...] = grad_value
        bias_sums[:, hidden_width:] += column_sum(grad_value.astype(F32))
        grad_act = 0.0
        for chunk in range(chunks):
            cut = slice(width * chunk, width * chunk + width)
            value = (nt(grad_value, second[cut]) * derived[:, cut]).astype(BF16)
            grad_pre[:, cut] = value
            bias_sums[:, cut] += column_sum(value.astype(F32))
            grad_act += nt(value, first[:, cut])
        sums[3:4] += column_sum(grad_act)
        sums[4:5] += column_sum(grad_act * mlp_norm)
        upstream = upstream + norm_back(grad_act, mlp_norm, mlp_inverse, mods[7:8])

        sums[2:3] += column_sum(upstream * time_branch[...])
        grad_value = (upstream * mods[5:6]).astype(BF16)
        grad_branch[...] = grad_value
        grad_heads = nt(grad_value, time_out[...]).astype(BF16)
        apart = apart_bias()
        inner = inner_sums(heads[...], grad_heads)
        parts = []
        for pair in range(pairs):
            cuts = part_cuts(pair, width)
            parts.append(
                [packed[:, cut] for cut in cuts]
                + [grad_heads[:, cuts[0]], totals[0, pair], inner[2 * pair : 2 * pair + 2]]
            )
        for pair, results in enumerate(heads_back(parts, apart)):
            for cut, part in zip(part_cuts(pair, width), results):
                grad_packed[:, cut] = part
        grad_act = nt(grad_packed[...], time_in[...]).astype(BF16).astype(F32)
        time_norm, time_inverse = normalise(current)
        sums[0:1] += column_sum(grad_act)
        sums[1:2] += column_sum(grad_act * time_norm)
        upstream = upstream + norm_back(grad_act, time_norm, time_inverse, mods[4:5])
        grad_after[...] = upstream.astype(BF16).reshape(frames, TILE, width)

    moving = pl.BlockSpec((frames, TILE, width), lambda i: (0, i, 0))

    def rows(columns):
        return pl.BlockSpec((block, columns), lambda i: (i, 0))

    def array(columns):
        return jax.ShapeDtypeStruct((length, columns), BF16)

    narrow, wide, triple = width, hidden_width, 3 * width
    kept = [narrow, wide, narrow, wide, narrow, triple]
    held = (mods, first_bias, second_bias, time_in, time_out)
    shares = mlp_full.reshape(count, share, 2 * hidden_width)
    return pl.pallas_call(
        body,
        grid=(spots // TILE,),
        in_specs=[moving, moving, rows(triple), rows(width), rows(width)]
        + [pl.BlockSpec((1, pairs, 2, block), lambda i: (i, 0, 0, 0))]
        + [whole(a.shape) for a in held]
        + [
            pl.BlockSpec((depth, hidden_width), lambda i: (0, 0), pipeline_mode=pl.Buffered(1)),
            pl.BlockSpec(
                (count, share, hidden_width), lambda i: (0, 0, 1), pipeline_mode=pl.Buffered(1)
            ),
        ],
        out_specs=[moving, moving]
        + [rows(c) for c in kept]
        + [whole_out((8, width)), whole_out((1, hidden_width + width))],
        out_shape=[jax.ShapeDtypeStruct(after.shape, BF16)] * 2
        + [array(c) for c in kept]
        + [
            jax.ShapeDtypeStruct((8, width), F32),
            jax.ShapeDtypeStruct((1, hidden_width + width), F32),
        ],
        scratch_shapes=[
            pltpu.VMEM((block, hidden_width), F32),
            pltpu.VMEM((hidden_width, width), BF16),
        ],
        compiler_params=params(60),
        cost_estimate=cost(40e9, 50 * MIB, 8e6),
        name="middle",
    )(after, grad_out, packed, heads, time_branch, totals, *held, mlp_full, shares)


def local(
    count,
    tokens,
    condition,
    patch_mask,
    grad_out,
    mod_weight,
    mod_bias,
    space_qkv,
    space_proj,
    time_qkv,
    time_proj,
    mlp_in,
    in_bias,
    mlp_out,
    out_bias,
):
    length, width = tokens.shape
    patches = patch_mask.shape[1]
    frame_dev = length // patches
    groups = condition.shape[0]
    clip_dev = FRAMES // frame_dev
    spots = patches // clip_dev
    sp_size = lax.axis_size("sp")
    shard = mod_weight.shape[0]
    mod_width = mod_weight.shape[1]
    hidden_width = mlp_in.shape[1]
    me = lax.axis_index("dp") * sp_size + lax.axis_index("sp")
    chip = me // 2
    core = me % 2
    clip_row = lax.axis_index("sp") // clip_dev
    order_a, order_b = chip_orders(count)
    teams = [list(range(s, s + clip_dev)) for s in range(0, sp_size, clip_dev)]

    def across(values):
        return lax.all_to_all(
            values, "sp", split_axis=0, concat_axis=0, tiled=True, axis_index_groups=teams
        )

    near = jnp.stack([condition[clip_row ^ s] for s in range(groups)])
    mask = sp_size
    while mask < count:
        near = jnp.concatenate([near, swap(near, mask, count)], axis=0)
        mask *= 2
    lifted = jax.nn.silu(near.astype(F32)).astype(BF16)
    lifted_rows = lax.dynamic_slice_in_dim(lifted, me * shard, shard, 1)
    part = jnp.dot(lifted_rows, mod_weight, preferred_element_type=F32)
    own = jnp.zeros((mod_width + hidden_width + width,), F32)
    own = lax.dynamic_update_slice(own, mod_bias.astype(F32), (me * mod_bias.shape[0],))
    own = lax.dynamic_update_slice(
        own, in_bias.astype(F32), (mod_width + me * in_bias.shape[0],)
    )
    own = lax.dynamic_update_slice(
        own, out_bias.astype(F32), (mod_width + hidden_width + me * out_bias.shape[0],)
    )
    row = jnp.pad(part, ((0, 0), (0, hidden_width + width))) + own[None]

    def row_halved(row, mask):
        half = row.shape[0] // 2
        return row[:half] + swap(row[half:], mask, count)

    def row_added(row, mask):
        return row + swap(row, mask, count)

    row_steps = []
    mask = count // 2
    while mask:
        row_steps.append(functools.partial(row_halved if mask >= clip_dev else row_added, mask=mask))
        mask //= 2

    hidden_share = mlp_out.shape[0] // shard
    if shard % 8:
        mlp_share = 8
        full = lax.all_gather(mlp_out, AXES, axis=0, tiled=True)
        full = full.reshape(-1, hidden_share, mlp_share, width)
        full = jnp.transpose(full, (0, 2, 1, 3)).reshape(-1, hidden_width)
        mlp_full = jnp.concatenate([lax.all_gather(mlp_in, AXES, axis=0, tiled=True), full], axis=1)
    else:
        mlp_share = shard
        packed_out = [mlp_out[i * shard : (i + 1) * shard] for i in range(hidden_share)]
        mlp_full = lax.all_gather(
            jnp.concatenate([mlp_in] + packed_out, axis=1), AXES, axis=0, tiled=True
        )
    cut = (space_qkv.shape[1] + width) // 2
    wanted = [
        space_qkv[:, :cut],
        jnp.concatenate([space_qkv[:, cut:], space_proj], axis=1),
        jnp.concatenate([time_qkv, time_proj], axis=1),
    ]
    if shard % 8:
        held = []
        for part in wanted:
            full = lax.all_gather(part, AXES, axis=0, tiled=True).reshape(-1, 2, 8, part.shape[1])
            held.append((full[:, 0], full[:, 1]))
        time_held = held.pop()
        spots_held = held[0][0].shape[0]
        table = jnp.stack(
            [jnp.arange(spots_held, dtype=jnp.int32)] * 2 + [jnp.zeros((spots_held,), jnp.int32)]
        )
        time_steps = []
    else:
        time_steps = list(order_a)
        time_own = wanted[2][None]

        def time_step(value):
            nonlocal time_own
            got = swap(time_own, time_steps.pop(0), count)
            value, got, time_own = lax.optimization_barrier((value, got, time_own))
            value, time_own = lax.optimization_barrier(
                (value, jnp.concatenate([time_own, got], axis=0))
            )
            return value

        one, two = wanted[0][None], wanted[1][None]
        for step, (mask_a, mask_b) in enumerate(zip(order_a, order_b)):
            if step >= 2 and len(time_steps) > 2:
                one = time_step(one)
            got = swap(one, mask_a, count), swap(two, mask_b, count)
            one = jnp.concatenate([one, got[0]], axis=0)
            two = jnp.concatenate([two, got[1]], axis=0)
            for _ in range(min(step, 2)):
                if len(row_steps) > 1:
                    row = row_steps.pop(0)(row)
            one, two, row = lax.optimization_barrier((one, two, row))
        held = [(one, swap(one, 1, count)), (two, swap(two, 1, count))]
        table = place_table((order_a, order_b), chip, core, count)

    while row_steps:
        row = row_steps.pop(0)(row)
    mods = row[0, :mod_width].reshape(9, width)
    first_bias = row[:, mod_width : mod_width + hidden_width]
    second_bias = row[:, mod_width + hidden_width :]

    mask_row = lax.dynamic_index_in_dim(patch_mask, clip_row, 0, keepdims=False)
    key_bias = jnp.where(mask_row == 1, 0.0, MASKED).astype(F32)[:, None]
    space_act, space_packed, space_full, space_out = space_project(tokens, mods, table, held)
    if time_steps:
        space_packed = time_step(space_packed)
    space_heads, space_total, space_branch, after_space = space_forward(
        space_packed, tokens, mods, key_bias, space_out, patches, clip_dev
    )
    if time_steps:
        after_space = time_step(after_space)
    after_here = across(after_space)
    if shard % 8 == 0:
        time_held = time_own, swap(time_own, 1, count)

    shape = (clip_dev, frame_dev, spots, width)
    flat_shape = (FRAMES, spots, width)
    grad_here = jnp.transpose(grad_out.reshape(frame_dev, clip_dev, spots, width), (1, 0, 2, 3))
    after_here, time_held, grad_here = lax.optimization_barrier((after_here, time_held, grad_here))
    after_here = after_here.reshape(flat_shape)
    grad_here = across(grad_here)
    times = time_forward(after_here, mods, table, *time_held)
    times, grad_here = lax.optimization_barrier((times, grad_here))
    time_act, time_packed, time_heads, time_branch, time_total, time_full, time_out = times
    (
        out_here,
        grad_here,
        mlp_act,
        hidden,
        grad_second,
        grad_pre,
        grad_time_branch,
        grad_time_packed,
        sums,
        bias_sums,
    ) = middle(
        after_here,
        grad_here.reshape(flat_shape),
        time_packed,
        time_heads,
        time_branch,
        time_total,
        mods,
        first_bias,
        second_bias,
        time_full,
        time_out,
        mlp_full,
        mlp_share,
    )

    turn_a, turn_b = order_a[::-1], order_b[::-1]
    turn_e = [turn_a[i] for i in (0, 2, 1)] + turn_a[3:]
    turn_t = [turn_a[i] for i in (2, 1, 0)] + turn_a[3:]

    def reduced(*sheets, deep=None):
        return weight_grads(sheets, chip, core, count, shard, width, deep)

    grad_after = across(grad_here.reshape(shape))
    wide = hidden_width // width
    shares = reduced(
        ([(mlp_act, grad_pre, 0, wide)], turn_b), deep=(hidden, grad_second, turn_e)
    )
    shares, grad_after, time_act = lax.optimization_barrier((shares, grad_after, time_act))
    fold_a, fold_e = Fold(shares[:2], turn_b, count), Fold(shares[2:], turn_e, count)
    shares = reduced(
        ([(time_act, grad_time_packed, 0, 3), (time_heads, grad_time_branch, 0, 1)], turn_t)
    )
    shares, grad_after = meet((shares, grad_after), fold_a, fold_e)
    fold_b = Fold(shares, turn_t, count)
    grad_space_branch, grad_space_heads, inner, grad_gate, out_here = meet(
        (
            *space_branch_back(grad_after, space_branch, space_heads, mods, space_out, patches),
            out_here,
        ),
        fold_b,
    )
    out_back = across(out_here.reshape(shape))
    grads = space_back(
        space_packed,
        grad_space_heads,
        space_total,
        inner,
        key_bias,
        space_full,
        tokens,
        grad_after,
        mods,
        patches,
    )
    grad_q, grad_k, grad_v, grad_tokens, space_sums, out_back, grad_gate = meet(
        (*grads, out_back, grad_gate), fold_a, fold_e, fold_b
    )
    out_tokens = jnp.transpose(out_back, (1, 0, 2, 3)).reshape(length, width)
    rows = jnp.concatenate(
        [space_sums.reshape(1, -1), grad_gate, sums[:6].reshape(1, -1), bias_sums], axis=1
    )
    mask = clip_dev // 2
    got = swap(rows, mask, count)
    shares = reduced(
        ([(space_heads, grad_space_branch, 0, 1), (space_act, grad_q, 0, 1)], turn_a),
        ([(space_act, grad_k, 0, 1), (space_act, grad_v, 0, 1)], turn_b),
    )
    shares, rows, got = meet((shares, rows, got), fold_a, fold_e, fold_b)
    fold_c, fold_d = Fold(shares[:2], turn_a, count), Fold(shares[2:], turn_b, count)
    rounds = [(fold_c, fold_d), (fold_a, fold_e, fold_b)]
    while mask:
        rows = rows + got
        mask //= 2
        if mask:
            got = swap(rows, mask, count)
            rows, got = meet((rows, got), *rounds.pop(0)) if rounds else (rows, got)
    mask = clip_dev
    while mask < count:
        got = swap(rows, mask, count)
        if mask == clip_dev:
            rows, got = meet((rows, got), fold_c, fold_d)
        rows = jnp.concatenate([rows, got], axis=0)
        mask *= 2
    while len(fold_a.masks) > 1:
        rows = meet(rows, fold_a, fold_e, fold_b)
    grad_a, grad_b, grad_mlp_out = fold_a.finish(), fold_b.finish(), fold_e.finish()
    grad_rows = rows[:, :mod_width]
    grad_lifted = lax.dot_general(
        grad_rows,
        mod_weight.astype(F32),
        (((1,), (1,)), ((), ())),
        precision=lax.Precision.HIGHEST,
        preferred_element_type=F32,
    )
    near_clips = jnp.arange(count // clip_dev) ^ (me // clip_dev)
    grad_lifted = jnp.take(grad_lifted, near_clips, axis=0)
    grad_lifted = jnp.repeat(
        grad_lifted.reshape(count // sp_size, 1, groups * shard), sp_size, axis=1
    ).reshape(count, groups * shard)
    grad_lifted = lax.all_to_all(grad_lifted, AXES, split_axis=0, concat_axis=0, tiled=True)
    while len(fold_d.masks) > 1:
        grad_a, grad_b = meet(
            (grad_a, grad_b), *[fold for fold in (fold_c, fold_d) if len(fold.masks) > 1]
        )
    grad_c, grad_d = fold_c.finish(), fold_d.finish()
    grad_mlp_in = grad_a
    grad_time_qkv = grad_b[:, : 3 * width]
    grad_time_proj = grad_b[:, 3 * width :]
    grad_space_proj = grad_c[:, :width]
    grad_space_qkv = jnp.concatenate([grad_c[:, width:], grad_d], axis=1)

    grad_mod_weight = lax.dot_general(
        lifted_rows.astype(F32),
        grad_rows,
        (((0,), (0,)), ((), ())),
        precision=lax.Precision.HIGHEST,
        preferred_element_type=F32,
    )
    totals = jnp.sum(rows, axis=0)
    grad_mod_bias = lax.dynamic_slice_in_dim(totals, me * mod_bias.shape[0], mod_bias.shape[0])
    grad_in_bias = lax.dynamic_slice_in_dim(
        totals, mod_width + me * in_bias.shape[0], in_bias.shape[0]
    )
    grad_out_bias = lax.dynamic_slice_in_dim(
        totals, mod_width + hidden_width + me * out_bias.shape[0], out_bias.shape[0]
    )
    grad_lifted = jnp.transpose(grad_lifted.reshape(count, groups, shard), (1, 0, 2))
    grad_lifted = grad_lifted.reshape(groups, width)
    _, silu_back = jax.vjp(jax.nn.silu, condition.astype(F32))
    grad_condition = silu_back(grad_lifted)[0]

    return (
        out_tokens,
        grad_tokens,
        grad_condition,
        grad_mod_weight,
        grad_mod_bias,
        grad_space_qkv,
        grad_space_proj,
        grad_time_qkv,
        grad_time_proj,
        grad_mlp_in,
        grad_in_bias,
        grad_mlp_out,
        grad_out_bias,
    )


def solution(mesh):
    count = mesh.shape["dp"] * mesh.shape["sp"]
    both = P(AXES, None)
    flat = P(AXES)
    clips = P("dp", None)
    return jax.shard_map(
        functools.partial(local, count),
        mesh=mesh,
        in_specs=(
            both, clips, clips, both, both, flat, both, both, both, both, both, flat, both, flat,
        ),
        out_specs=(
            both, both, clips, both, flat, both, both, both, both, both, flat, both, flat,
        ),
        check_vma=False,
    )
```

```python
import functools
import math

import jax
import jax.numpy as jnp
from jax import lax
from jax.experimental import pallas as pl
from jax.experimental.pallas import tpu as pltpu
from jax.sharding import PartitionSpec as P

HEADS = 12
HEAD_DIM = 64
FRAMES = 16
EPSILON = 1e-06
MASKED = -10000.0
APART = -1e30
AXES = ("dp", "sp")
F32 = jnp.float32
BF16 = jnp.bfloat16
MIB = 1 << 20


def swap(values, mask, count):
    return lax.ppermute(values, AXES, [(i, i ^ mask) for i in range(count)])


def chip_orders(count):
    bits = [1 << i for i in range(1, count.bit_length() - 1)]
    low, high, middle = bits[0], bits[-1], bits[1:-1][::-1]
    return (middle + [high, low], middle + [low, high])


def spread(shard, order, count):
    held = shard[None]
    for mask in order:
        held = jnp.concatenate([held, swap(held, mask, count)], axis=0)
    return held


def spread_places(order, count):
    places = []
    for distance in range(count // 2):
        places.append(sum(1 << s for s, mask in enumerate(order) if distance & (mask >> 1)))
    return places


def fold_places(order, count):
    steps = len(order)
    places = []
    for distance in range(count // 2):
        places.append(
            sum(1 << (steps - 1 - s) for s, mask in enumerate(order) if distance & (mask >> 1))
        )
    return places


class Fold:
    def __init__(self, shares, order, count):
        self.keep, self.send = shares
        self.masks = [1] + list(order)
        self.count = count
        self.got = swap(self.send, 1, count)

    def add(self):
        half = self.keep.shape[0] // 2
        low = self.keep[:half].astype(F32) + self.got[:half].astype(F32)
        high = self.keep[half:].astype(F32) + self.got[half:].astype(F32)
        self.keep, self.send = low.astype(BF16), high.astype(BF16)
        self.masks.pop(0)

    def go(self):
        self.got = swap(self.send, self.masks[0], self.count)

    def finish(self):
        while len(self.masks) > 1:
            self.add()
            self.go()
        return self.keep[0].astype(F32) + self.got[0].astype(F32)


def meet(values, *folds):
    values, states = lax.optimization_barrier(
        (values, [(f.keep, f.got) for f in folds])
    )
    for fold, (fold.keep, fold.got) in zip(folds, states):
        fold.add()
    values, states = lax.optimization_barrier((values, [(f.keep, f.send) for f in folds]))
    for fold, (fold.keep, fold.send) in zip(folds, states):
        fold.go()
    return values


def clip_total(row, mask, count):
    while mask:
        row = row + swap(row, mask, count)
        mask //= 2
    return row


def nn(a, b):
    return jnp.dot(a, b, preferred_element_type=F32)


def nt(a, b):
    return lax.dot_general(a, b, (((1,), (1,)), ((), ())), preferred_element_type=F32)


def tn(a, b):
    return lax.dot_general(a, b, (((0,), (0,)), ((), ())), preferred_element_type=F32)


def normalise(values):
    average = jnp.mean(values, axis=-1, keepdims=True)
    centred = values - average
    inverse = lax.rsqrt(jnp.mean(centred * centred, axis=-1, keepdims=True) + EPSILON)
    return centred * inverse, inverse


def norm_back(grad_mod, normed, inverse, scale):
    grad_normed = grad_mod * (1.0 + scale)
    inner = jnp.mean(grad_normed * normed, axis=-1, keepdims=True)
    average = jnp.mean(grad_normed, axis=-1, keepdims=True)
    return inverse * (grad_normed - average - normed * inner)


def column_sum(values):
    return jnp.sum(values, axis=0, keepdims=True)


def halves():
    lane = lax.broadcasted_iota(jnp.int32, (1, 2 * HEAD_DIM), 1)
    first = (lane < HEAD_DIM).astype(F32)
    return first.astype(BF16), (1.0 - first).astype(BF16)


def turned(values):
    return jnp.transpose(values.astype(F32), (1, 0))


def key_lanes(bias, half):
    lane = lax.broadcasted_iota(jnp.int32, (1, 2 * HEAD_DIM), 1) - (1 - half) * HEAD_DIM
    large = bias.astype(BF16).astype(F32)
    lanes = large * (lane == 0).astype(F32) + (bias - large) * (lane == 1).astype(F32)
    return lanes.astype(BF16)


def query_lanes(half):
    lane = lax.broadcasted_iota(jnp.int32, (1, 2 * HEAD_DIM), 1) - (1 - half) * HEAD_DIM
    return jnp.logical_or(lane == 0, lane == 1).astype(F32).astype(BF16)


def biased_scores(queries, keys, half, mask, lanes):
    if lanes is None:
        return nt(keys * (mask * 0.125), queries)
    return nt(keys * (mask * 0.125) + lanes[half], queries * mask + query_lanes(half))


def heads_forward(pairs, apart=None, lanes=None):
    masks = halves()

    def scores_of(item):
        queries, keys, _ = pairs[item // 2]
        return biased_scores(queries, keys, item % 2, masks[item % 2], lanes)

    coming = scores_of(0)
    results = []
    for item in range(2 * len(pairs)):
        scores = coming if apart is None else spaced(coming, apart)
        if item + 1 < 2 * len(pairs):
            coming = scores_of(item + 1)
        if item % 2 == 0:
            values_t = turned(pairs[item // 2][2]).astype(BF16)
            parts, totals = [], []
        largest = jnp.max(scores, axis=0, keepdims=True)
        exponent = jnp.exp(scores - largest)
        denominator = jnp.sum(exponent, axis=0, keepdims=True)
        half = item % 2
        attended = nn(values_t[half * HEAD_DIM : (half + 1) * HEAD_DIM], exponent.astype(BF16))
        parts.append(attended * (1.0 / denominator))
        totals.append(largest + jnp.log(denominator))
        if half == 1:
            attended = jnp.transpose(jnp.concatenate(parts, axis=0), (1, 0)).astype(BF16)
            results.append((attended, jnp.concatenate(totals, axis=0)))
    return results


def spaced(scores, apart):
    rows, lanes = apart.shape
    parts = []
    for start in range(0, scores.shape[1], lanes):
        part = scores[:, start : start + lanes].reshape(-1, rows, lanes) + apart[None]
        parts.append(part.reshape(-1, lanes))
    return jnp.concatenate(parts, axis=1)


def heads_back(pairs, apart=None, lanes=None):
    masks = halves()

    def products_of(item):
        queries, keys, values, grad, _, _ = pairs[item // 2]
        mask = masks[item % 2]
        scores = biased_scores(queries, keys, item % 2, mask, lanes)
        return scores, nt(values * mask, grad)

    coming = products_of(0)
    results = []
    for item in range(2 * len(pairs)):
        scores, grad_probs = coming
        if item + 1 < 2 * len(pairs):
            coming = products_of(item + 1)
        half = item % 2
        queries, keys, _, grad, totals, inner = pairs[item // 2]
        if half == 0:
            keys_t = turned(keys).astype(BF16)
            grad_queries, grad_keys, grad_values = [], 0.0, 0.0
        if apart is not None:
            scores = spaced(scores, apart)
        probable = jnp.exp(scores - totals[half : half + 1])
        grad_scores = (probable * (grad_probs - inner[half : half + 1])).astype(BF16)
        mask = masks[half]
        grad_values += nn(probable.astype(BF16), grad * mask)
        grad_keys += nn(grad_scores, queries * (mask * 0.125))
        grad_queries.append(nn(keys_t[half * HEAD_DIM : (half + 1) * HEAD_DIM], grad_scores))
        if half == 1:
            grad_queries = jnp.transpose(jnp.concatenate(grad_queries, axis=0), (1, 0)) * 0.125
            results.append(
                (grad_queries.astype(BF16), grad_keys.astype(BF16), grad_values.astype(BF16))
            )
    return results


def inner_sums(heads, grad_heads):
    width = heads.shape[1]
    head = lax.broadcasted_iota(jnp.int32, (16, width), 0)
    lane = lax.broadcasted_iota(jnp.int32, (16, width), 1)
    chosen = (lane // HEAD_DIM == head).astype(F32).astype(BF16)
    product = heads.astype(F32) * grad_heads.astype(F32)
    large = product.astype(BF16)
    return nt(chosen, large) + nt(chosen, (product - large.astype(F32)).astype(BF16))


def whole(shape):
    return pl.BlockSpec(shape, lambda *_: (0,) * len(shape), pipeline_mode=pl.Buffered(1))


def whole_out(shape):
    return pl.BlockSpec(shape, lambda *_: (0,) * len(shape))


def params(limit=56):
    return pltpu.CompilerParams(vmem_limit_bytes=limit * MIB)


def cost(flops, moved, special=0):
    return pl.CostEstimate(flops=int(flops) // 16, bytes_accessed=int(moved) // 16, transcendentals=0)


def place_table(orders, chip, core, count):
    chips = count // 2
    index = jnp.arange(chips) ^ chip
    return jnp.stack(
        [jnp.array(spread_places(order, count), jnp.int32)[index] for order in orders]
        + [jnp.full((chips,), core, jnp.int32)]
    )


def build(table, row, own, other, runs):
    chips, share, _ = own.shape
    odd = table[table.shape[0] - 1, 0] == 1

    def step(i, carry):
        place = table[row, i]
        one = own[place].astype(F32)
        two = other[place].astype(F32)
        joined = jnp.concatenate(
            [jnp.where(odd, two, one), jnp.where(odd, one, two)], axis=0
        ).astype(BF16)
        rows = pl.ds(pl.multiple_of(i * 2 * share, 2 * share), 2 * share)
        for column, width, target, start in runs:
            target[rows, start : start + width] = joined[:, column : column + width]
        return carry

    lax.fori_loop(0, chips, step, 0)


def weight_grads(sheets, chip, core, count, share, block, deep=None):
    chips = count // 2
    groups = [group for sheet, _ in sheets for group in sheet]
    length = groups[0][0].shape[0]
    depth = count * share
    steps = [group[3] for group in groups]
    starts = [sum(steps[:i]) for i in range(len(steps))]
    sizes = [sum(group[3] for group in sheet) for sheet, _ in sheets]
    sheet_starts = [sum(sizes[:i]) for i in range(len(sizes))]
    owners = [i for i, (sheet, _) in enumerate(sheets) for _ in sheet]
    total = sum(steps)
    extra = deep[0].shape[1] // block if deep else 0
    orders = [order for _, order in sheets] + ([deep[2]] if deep else [])
    distances = jnp.arange(chips) ^ chip
    table = jnp.concatenate(
        [jnp.array(fold_places(order, count), jnp.int32)[distances] for order in orders]
        + [jnp.full((1,), core, jnp.int32)]
    )

    def body(table, *refs):
        ins, outs = refs[: len(operands)], refs[len(operands) : -1]
        acts_t = refs[-1]
        j = pl.program_id(0)
        odd = table[chips * len(orders)] == 1
        for index, owner in enumerate(owners):
            acts, grads = ins[act_places[index]], ins[grad_places[index]]
            keep, send = outs[2 * owner : 2 * owner + 2]
            here = j - starts[index]

            if index == 0 or act_places[index] != act_places[index - 1]:

                @pl.when(here == 0)
                def _():
                    acts_t[...] = turned(acts[...]).astype(BF16)

            @pl.when(jnp.logical_and(here >= 0, here < steps[index]))
            def _():
                product = nn(acts_t[...], grads[...])
                for pair in range(chips):
                    place = table[owner * chips + pair]
                    start = 2 * pair * share
                    first = product[start : start + share]
                    second = product[start + share : start + 2 * share]
                    keep[place] = jnp.where(odd, second, first).astype(BF16)
                    send[place] = jnp.where(odd, first, second).astype(BF16)

        if deep:
            keep, send = outs[-2:]
            rows = keep.shape[1]
            pairs = block // (2 * rows)

            @pl.when(j >= total)
            def _():
                product = tn(ins[-2][...], ins[-1][...])
                for pair in range(pairs):
                    place = table[len(sheets) * chips + (j - total) * pairs + pair]
                    start = 2 * pair * rows
                    first = product[start : start + rows]
                    second = product[start + rows : start + 2 * rows]
                    keep[place] = jnp.where(odd, second, first).astype(BF16)
                    send[place] = jnp.where(odd, first, second).astype(BF16)

    in_specs = []
    operands = []
    act_places = []
    grad_places = []
    for index, (start, (acts, grads, g_first, blocks)) in enumerate(zip(starts, groups)):
        if index and acts is groups[index - 1][0]:
            act_places.append(act_places[-1])
        else:
            act_places.append(len(operands))
            operands.append(acts)
            in_specs.append(pl.BlockSpec((length, depth), lambda j, t: (0, 0)))
        follows = index and grads is groups[index - 1][1]
        if follows and g_first == groups[index - 1][2] + groups[index - 1][3]:
            grad_places.append(grad_places[-1])
            first, g_start, last = walks.pop()
            walks.append((first, g_start, last + blocks))
        else:
            if index == 0:
                walks = []
            grad_places.append(len(operands))
            operands.append(grads)
            in_specs.append(None)
            walks.append((start, g_first, blocks))
    for place, (start, g_first, blocks) in zip(sorted(set(grad_places)), walks):
        in_specs[place] = pl.BlockSpec(
            (length, block),
            lambda j, t, s=start, m=blocks, g=g_first: (0, g + jnp.clip(j - s, 0, m - 1)),
        )
    out_specs = []
    out_shape = []
    for start, size in zip(sheet_starts, sizes):
        out_specs += [
            pl.BlockSpec(
                (chips, share, block),
                lambda j, t, s=start, m=size: (0, 0, jnp.clip(j - s, 0, m - 1)),
            )
        ] * 2
        out_shape += [jax.ShapeDtypeStruct((chips, share, size * block), BF16)] * 2
    if deep:
        in_specs.append(
            pl.BlockSpec((length, block), lambda j, t: (0, jnp.clip(j - total, 0, extra - 1)))
        )
        in_specs.append(pl.BlockSpec(deep[1].shape, lambda j, t: (0, 0)))
        operands += list(deep[:2])
        shape = (chips, deep[0].shape[1] // count, deep[1].shape[1])
        out_specs += [whole_out(shape)] * 2
        out_shape += [jax.ShapeDtypeStruct(shape, BF16)] * 2
    return pl.pallas_call(
        body,
        grid_spec=pltpu.PrefetchScalarGridSpec(
            num_scalar_prefetch=1,
            grid=(total + extra,),
            in_specs=in_specs,
            out_specs=out_specs,
            scratch_shapes=[pltpu.VMEM((depth, length), BF16)],
        ),
        out_shape=out_shape,
        compiler_params=params(),
        cost_estimate=cost(2 * length * depth * total * block, 4 * depth * total * block),
        name="weight_grads",
    )(table, *operands)


def space_project(tokens, mods, table, held):
    length, width = tokens.shape
    depth = held[0][0].shape[0] * held[0][0].shape[1] * 2
    wide = 3 * width
    cut = held[0][0].shape[2]
    block = 256

    def body(table, tokens, mods, own_a, other_a, own_b, other_b, act, packed, weight, last):
        @pl.when(pl.program_id(0) == 0)
        def _():
            build(table, 0, own_a, other_a, [(0, cut, weight, 0)])
            build(
                table, 1, own_b, other_b, [(0, wide - cut, weight, cut), (wide - cut, width, last, 0)]
            )

        normed, _ = normalise(tokens[...].astype(F32))
        value = (normed * (1.0 + mods[1:2]) + mods[0:1]).astype(BF16)
        act[...] = value
        packed[...] = nn(value, weight[...]).astype(BF16)

    parts = [part for pair in held for part in pair]
    return pl.pallas_call(
        body,
        grid_spec=pltpu.PrefetchScalarGridSpec(
            num_scalar_prefetch=1,
            grid=(length // block,),
            in_specs=[pl.BlockSpec((block, width), lambda i, t: (i, 0)), whole(mods.shape)]
            + [whole(part.shape) for part in parts],
            out_specs=[
                pl.BlockSpec((block, width), lambda i, t: (i, 0)),
                pl.BlockSpec((block, wide), lambda i, t: (i, 0)),
                whole_out((depth, wide)),
                whole_out((depth, width)),
            ],
        ),
        out_shape=[
            jax.ShapeDtypeStruct((length, width), BF16),
            jax.ShapeDtypeStruct((length, wide), BF16),
            jax.ShapeDtypeStruct((depth, wide), BF16),
            jax.ShapeDtypeStruct((depth, width), BF16),
        ],
        compiler_params=params(),
        cost_estimate=cost(2 * length * width * wide, 16 * MIB),
        name="space_project",
    )(table, tokens, mods, *parts)


def space_forward(packed, tokens, mods, bias, weight, patches, peers):
    length, width = tokens.shape
    frames = length // patches
    pairs = width // 128
    spots = patches // peers

    def body(packed, tokens, mods, bias, weight, heads, totals, branch, after):
        lanes = [key_lanes(bias[...], half) for half in range(2)]

        def step(pair, carry):
            at = pl.multiple_of(pair * 128, 128)
            parts = [packed[:, pl.ds(part * width + at, 128)] for part in range(3)]
            ((attended, logs),) = heads_forward([parts], lanes=lanes)
            heads[:, pl.ds(at, 128)] = attended
            totals[0, pair] = logs
            return carry

        lax.fori_loop(0, pairs, step, 0)
        product = nn(heads[...], weight[...])
        branch[...] = product.astype(BF16)
        result = (tokens[...].astype(F32) + mods[2:3] * product).astype(BF16)
        for peer in range(peers):
            after[peer, 0] = result[peer * spots : (peer + 1) * spots]

    def rows(columns):
        return pl.BlockSpec((patches, columns), lambda f: (f, 0))

    return pl.pallas_call(
        body,
        grid=(frames,),
        in_specs=[rows(3 * width), rows(width)]
        + [whole(a.shape) for a in (mods, bias, weight)],
        out_specs=[
            rows(width),
            pl.BlockSpec((1, pairs, 2, patches), lambda f: (f, 0, 0, 0)),
            rows(width),
            pl.BlockSpec((peers, 1, spots, width), lambda f: (0, f, 0, 0)),
        ],
        out_shape=[
            jax.ShapeDtypeStruct((length, width), BF16),
            jax.ShapeDtypeStruct((frames, pairs, 2, patches), F32),
            jax.ShapeDtypeStruct((length, width), BF16),
            jax.ShapeDtypeStruct((peers, frames, spots, width), BF16),
        ],
        compiler_params=params(),
        cost_estimate=cost(10e9, 10 * MIB, 6e6),
        name="space_forward",
    )(packed, tokens, mods, bias, weight)


def space_branch_back(grad_after, branch, heads, mods, weight, patches):
    peers, frames, spots, width = grad_after.shape
    length = frames * patches

    def body(grad_after, branch, heads, mods, weight, grad_branch, grad_heads, inner, grad_gate):
        upstream = grad_after[...].reshape(patches, width).astype(F32)
        value = (upstream * mods[2:3]).astype(BF16)
        grad_branch[...] = value
        grads = nt(value, weight[...]).astype(BF16)
        grad_heads[...] = grads
        rows = inner_sums(heads[...], grads)
        for pair in range(inner.shape[1]):
            inner[0, pair] = rows[2 * pair : 2 * pair + 2]

        @pl.when(pl.program_id(0) == 0)
        def _():
            grad_gate[...] = jnp.zeros_like(grad_gate)

        grad_gate[...] += column_sum(upstream * branch[...].astype(F32))

    return pl.pallas_call(
        body,
        grid=(frames,),
        in_specs=[
            pl.BlockSpec((peers, 1, spots, width), lambda f: (0, f, 0, 0)),
            pl.BlockSpec((patches, width), lambda f: (f, 0)),
            pl.BlockSpec((patches, width), lambda f: (f, 0)),
            whole(mods.shape),
            whole(weight.shape),
        ],
        out_specs=[
            pl.BlockSpec((patches, width), lambda f: (f, 0)),
            pl.BlockSpec((patches, width), lambda f: (f, 0)),
            pl.BlockSpec((1, width // 128, 2, patches), lambda f: (f, 0, 0, 0)),
            whole_out((1, width)),
        ],
        out_shape=[
            jax.ShapeDtypeStruct((length, width), BF16),
            jax.ShapeDtypeStruct((length, width), BF16),
            jax.ShapeDtypeStruct((frames, width // 128, 2, patches), F32),
            jax.ShapeDtypeStruct((1, width), F32),
        ],
        compiler_params=params(),
        cost_estimate=cost(2 * length * width * width, 8 * MIB),
        name="space_branch_back",
    )(grad_after, branch, heads, mods, weight)


def space_back(packed, grad_heads, totals, inner, bias, weight, tokens, grad_after, mods, patches):
    peers, frames, spots, width = grad_after.shape
    length = frames * patches
    pairs = width // 128

    def body(
        packed, grad_heads, totals, inner, bias, weight, tokens, grad_after, mods,
        grad_packed, grad_tokens, sums,
    ):
        lanes = [key_lanes(bias[...], half) for half in range(2)]

        def step(pair, carry):
            at = pl.multiple_of(pair * 128, 128)
            parts = [packed[:, pl.ds(part * width + at, 128)] for part in range(3)]
            rest = [grad_heads[:, pl.ds(at, 128)], totals[0, pair], inner[0, pair]]
            (results,) = heads_back([parts + rest], lanes=lanes)
            for part, result in enumerate(results):
                grad_packed[:, pl.ds(part * width + at, 128)] = result
            return carry

        lax.fori_loop(0, pairs, step, 0)

        @pl.when(pl.program_id(0) == 0)
        def _():
            sums[...] = jnp.zeros_like(sums)

        grad_act = nt(grad_packed[...], weight[...])
        normed, inverse = normalise(tokens[...].astype(F32))
        upstream = grad_after[...].reshape(patches, width).astype(F32)
        grad_tokens[...] = (
            upstream + norm_back(grad_act, normed, inverse, mods[1:2])
        ).astype(BF16)
        sums[0:1] += column_sum(grad_act)
        sums[1:2] += column_sum(grad_act * normed)

    def rows(columns):
        return pl.BlockSpec((patches, columns), lambda f: (f, 0))

    flat = jax.ShapeDtypeStruct((length, width), BF16)
    return pl.pallas_call(
        body,
        grid=(frames,),
        in_specs=[
            rows(3 * width),
            rows(width),
            pl.BlockSpec((1, pairs, 2, patches), lambda f: (f, 0, 0, 0)),
            pl.BlockSpec((1, pairs, 2, patches), lambda f: (f, 0, 0, 0)),
            whole(bias.shape),
            whole(weight.shape),
            rows(width),
            pl.BlockSpec((peers, 1, spots, width), lambda f: (0, f, 0, 0)),
            whole(mods.shape),
        ],
        out_specs=[rows(3 * width), rows(width), whole_out((2, width))],
        out_shape=[
            jax.ShapeDtypeStruct((length, 3 * width), BF16),
            flat,
            jax.ShapeDtypeStruct((2, width), F32),
        ],
        compiler_params=params(),
        cost_estimate=cost(24e9, 20 * MIB, 6e6),
        name="space_back",
    )(packed, grad_heads, totals, inner, bias, weight, tokens, grad_after, mods)


TILE = 16


def apart_bias():
    row = lax.broadcasted_iota(jnp.int32, (TILE, 128), 0)
    column = lax.broadcasted_iota(jnp.int32, (TILE, 128), 1)
    return jnp.where((row & (TILE - 1)) == (column & (TILE - 1)), 0.0, APART)


def part_cuts(pair, width):
    return [slice(p * width + 128 * pair, p * width + 128 * pair + 128) for p in range(3)]


def time_forward(after, mods, table, own, other):
    frames, spots, width = after.shape
    depth = own.shape[0] * own.shape[1] * 2
    block = frames * TILE
    length = frames * spots
    pairs = width // 128

    def body(table, after, mods, own, other, act, packed, heads, branch, totals, time_in, time_out):
        @pl.when(pl.program_id(0) == 0)
        def _():
            build(
                table, 0, own, other, [(0, 3 * width, time_in, 0), (3 * width, width, time_out, 0)]
            )

        apart = apart_bias()
        normed, _ = normalise(after[...].reshape(block, width).astype(F32))
        value = (normed * (1.0 + mods[4:5]) + mods[3:4]).astype(BF16)
        act[...] = value
        packed[...] = nn(value, time_in[...]).astype(BF16)
        parts = [[packed[:, cut] for cut in part_cuts(pair, width)] for pair in range(pairs)]
        for pair, (attended, logs) in enumerate(heads_forward(parts, apart)):
            heads[:, 128 * pair : 128 * pair + 128] = attended
            totals[0, pair] = logs
        branch[...] = nn(heads[...], time_out[...])

    def rows(columns):
        return pl.BlockSpec((block, columns), lambda i, t: (i, 0))

    return pl.pallas_call(
        body,
        grid_spec=pltpu.PrefetchScalarGridSpec(
            num_scalar_prefetch=1,
            grid=(spots // TILE,),
            in_specs=[pl.BlockSpec((frames, TILE, width), lambda i, t: (0, i, 0))]
            + [whole(a.shape) for a in (mods, own, other)],
            out_specs=[
                rows(width),
                rows(3 * width),
                rows(width),
                rows(width),
                pl.BlockSpec((1, pairs, 2, block), lambda i, t: (i, 0, 0, 0)),
                whole_out((depth, 3 * width)),
                whole_out((depth, width)),
            ],
        ),
        out_shape=[
            jax.ShapeDtypeStruct((length, width), BF16),
            jax.ShapeDtypeStruct((length, 3 * width), BF16),
            jax.ShapeDtypeStruct((length, width), BF16),
            jax.ShapeDtypeStruct((length, width), F32),
            jax.ShapeDtypeStruct((spots // TILE, pairs, 2, block), F32),
            jax.ShapeDtypeStruct((depth, 3 * width), BF16),
            jax.ShapeDtypeStruct((depth, width), BF16),
        ],
        compiler_params=params(),
        cost_estimate=cost(8e9, 24 * MIB, 3e6),
        name="time_forward",
    )(table, after, mods, own, other)


def middle(
    after, grad_out, packed, heads, time_branch, totals, mods, first_bias, second_bias, time_in,
    time_out, mlp_full, share,
):
    frames, spots, width = after.shape
    hidden_width = first_bias.shape[1]
    depth = mlp_full.shape[0]
    count = depth // share
    block = frames * TILE
    length = frames * spots
    pairs = width // 128
    chunks = hidden_width // width
    slope = math.sqrt(2.0 / math.pi)

    def body(
        after, grad_out, packed, heads, time_branch, totals,
        mods, first_bias, second_bias, time_in, time_out, first, shares,
        out, grad_after, mlp_act, hidden, grad_second, grad_pre, grad_branch, grad_packed,
        sums, bias_sums, derived, second,
    ):
        @pl.when(pl.program_id(0) == 0)
        def _():
            def unpack(i, carry):
                piece = shares[i].astype(F32)
                parts = [piece[:, c * width : (c + 1) * width] for c in range(chunks)]
                rows = pl.ds(pl.multiple_of(i * chunks * share, chunks * share), chunks * share)
                second[rows] = jnp.concatenate(parts, axis=0).astype(BF16)
                return carry

            lax.fori_loop(0, count, unpack, 0)
            sums[...] = jnp.zeros_like(sums)
            bias_sums[...] = jnp.zeros_like(bias_sums)

        current = after[...].reshape(block, width).astype(F32)
        after_time = current + mods[5:6] * time_branch[...]
        mlp_norm, mlp_inverse = normalise(after_time)
        act = (mlp_norm * (1.0 + mods[7:8]) + mods[6:7]).astype(BF16)
        mlp_act[...] = act
        mlp_branch = 0.0
        for chunk in range(chunks):
            cut = slice(width * chunk, width * chunk + width)
            pre = nn(act, first[:, cut]) + first_bias[:, cut]
            squared = pre * pre
            bent = jnp.tanh(slope * pre * (1.0 + 0.044715 * squared))
            half = 0.5 * (1.0 + bent)
            value = (pre * half).astype(BF16)
            hidden[:, cut] = value
            derived[:, cut] = half + 0.5 * slope * pre * (1.0 - bent * bent) * (
                1.0 + 3.0 * 0.044715 * squared
            )
            mlp_branch += nn(value, second[cut])
        mlp_branch += second_bias[...]
        out[...] = (after_time + mods[8:9] * mlp_branch).astype(BF16).reshape(frames, TILE, width)

        upstream = grad_out[...].reshape(block, width).astype(F32)
        sums[5:6] += column_sum(upstream * mlp_branch)
        grad_value = (upstream * mods[8:9]).astype(BF16)
        grad_second[...] = grad_value
        bias_sums[:, hidden_width:] += column_sum(grad_value.astype(F32))
        grad_act = 0.0
        for chunk in range(chunks):
            cut = slice(width * chunk, width * chunk + width)
            value = (nt(grad_value, second[cut]) * derived[:, cut]).astype(BF16)
            grad_pre[:, cut] = value
            bias_sums[:, cut] += column_sum(value.astype(F32))
            grad_act += nt(value, first[:, cut])
        sums[3:4] += column_sum(grad_act)
        sums[4:5] += column_sum(grad_act * mlp_norm)
        upstream = upstream + norm_back(grad_act, mlp_norm, mlp_inverse, mods[7:8])

        sums[2:3] += column_sum(upstream * time_branch[...])
        grad_value = (upstream * mods[5:6]).astype(BF16)
        grad_branch[...] = grad_value
        grad_heads = nt(grad_value, time_out[...]).astype(BF16)
        apart = apart_bias()
        inner = inner_sums(heads[...], grad_heads)
        parts = []
        for pair in range(pairs):
            cuts = part_cuts(pair, width)
            parts.append(
                [packed[:, cut] for cut in cuts]
                + [grad_heads[:, cuts[0]], totals[0, pair], inner[2 * pair : 2 * pair + 2]]
            )
        for pair, results in enumerate(heads_back(parts, apart)):
            for cut, part in zip(part_cuts(pair, width), results):
                grad_packed[:, cut] = part
        grad_act = nt(grad_packed[...], time_in[...]).astype(BF16).astype(F32)
        time_norm, time_inverse = normalise(current)
        sums[0:1] += column_sum(grad_act)
        sums[1:2] += column_sum(grad_act * time_norm)
        upstream = upstream + norm_back(grad_act, time_norm, time_inverse, mods[4:5])
        grad_after[...] = upstream.astype(BF16).reshape(frames, TILE, width)

    moving = pl.BlockSpec((frames, TILE, width), lambda i: (0, i, 0))

    def rows(columns):
        return pl.BlockSpec((block, columns), lambda i: (i, 0))

    def array(columns):
        return jax.ShapeDtypeStruct((length, columns), BF16)

    narrow, wide, triple = width, hidden_width, 3 * width
    kept = [narrow, wide, narrow, wide, narrow, triple]
    held = (mods, first_bias, second_bias, time_in, time_out)
    shares = mlp_full.reshape(count, share, 2 * hidden_width)
    return pl.pallas_call(
        body,
        grid=(spots // TILE,),
        in_specs=[moving, moving, rows(triple), rows(width), rows(width)]
        + [pl.BlockSpec((1, pairs, 2, block), lambda i: (i, 0, 0, 0))]
        + [whole(a.shape) for a in held]
        + [
            pl.BlockSpec((depth, hidden_width), lambda i: (0, 0), pipeline_mode=pl.Buffered(1)),
            pl.BlockSpec(
                (count, share, hidden_width), lambda i: (0, 0, 1), pipeline_mode=pl.Buffered(1)
            ),
        ],
        out_specs=[moving, moving]
        + [rows(c) for c in kept]
        + [whole_out((8, width)), whole_out((1, hidden_width + width))],
        out_shape=[jax.ShapeDtypeStruct(after.shape, BF16)] * 2
        + [array(c) for c in kept]
        + [
            jax.ShapeDtypeStruct((8, width), F32),
            jax.ShapeDtypeStruct((1, hidden_width + width), F32),
        ],
        scratch_shapes=[
            pltpu.VMEM((block, hidden_width), F32),
            pltpu.VMEM((hidden_width, width), BF16),
        ],
        compiler_params=params(60),
        cost_estimate=cost(40e9, 50 * MIB, 8e6),
        name="middle",
    )(after, grad_out, packed, heads, time_branch, totals, *held, mlp_full, shares)


def local(
    count,
    tokens,
    condition,
    patch_mask,
    grad_out,
    mod_weight,
    mod_bias,
    space_qkv,
    space_proj,
    time_qkv,
    time_proj,
    mlp_in,
    in_bias,
    mlp_out,
    out_bias,
):
    length, width = tokens.shape
    patches = patch_mask.shape[1]
    frame_dev = length // patches
    groups = condition.shape[0]
    clip_dev = FRAMES // frame_dev
    spots = patches // clip_dev
    sp_size = lax.axis_size("sp")
    shard = mod_weight.shape[0]
    mod_width = mod_weight.shape[1]
    hidden_width = mlp_in.shape[1]
    me = lax.axis_index("dp") * sp_size + lax.axis_index("sp")
    chip = me // 2
    core = me % 2
    clip_row = lax.axis_index("sp") // clip_dev
    order_a, order_b = chip_orders(count)
    teams = [list(range(s, s + clip_dev)) for s in range(0, sp_size, clip_dev)]

    def across(values):
        return lax.all_to_all(
            values, "sp", split_axis=0, concat_axis=0, tiled=True, axis_index_groups=teams
        )

    near = jnp.stack([condition[clip_row ^ s] for s in range(groups)])
    mask = sp_size
    while mask < count:
        near = jnp.concatenate([near, swap(near, mask, count)], axis=0)
        mask *= 2
    lifted = jax.nn.silu(near.astype(F32)).astype(BF16)
    lifted_rows = lax.dynamic_slice_in_dim(lifted, me * shard, shard, 1)
    part = jnp.dot(lifted_rows, mod_weight, preferred_element_type=F32)
    own = jnp.zeros((mod_width + hidden_width + width,), F32)
    own = lax.dynamic_update_slice(own, mod_bias.astype(F32), (me * mod_bias.shape[0],))
    own = lax.dynamic_update_slice(
        own, in_bias.astype(F32), (mod_width + me * in_bias.shape[0],)
    )
    own = lax.dynamic_update_slice(
        own, out_bias.astype(F32), (mod_width + hidden_width + me * out_bias.shape[0],)
    )
    row = jnp.pad(part, ((0, 0), (0, hidden_width + width))) + own[None]

    def row_halved(row, mask):
        half = row.shape[0] // 2
        return row[:half] + swap(row[half:], mask, count)

    def row_added(row, mask):
        return row + swap(row, mask, count)

    row_steps = []
    mask = count // 2
    while mask:
        row_steps.append(functools.partial(row_halved if mask >= clip_dev else row_added, mask=mask))
        mask //= 2

    hidden_share = mlp_out.shape[0] // shard
    if shard % 8:
        mlp_share = 8
        full = lax.all_gather(mlp_out, AXES, axis=0, tiled=True)
        full = full.reshape(-1, hidden_share, mlp_share, width)
        full = jnp.transpose(full, (0, 2, 1, 3)).reshape(-1, hidden_width)
        mlp_full = jnp.concatenate([lax.all_gather(mlp_in, AXES, axis=0, tiled=True), full], axis=1)
    else:
        mlp_share = shard
        packed_out = [mlp_out[i * shard : (i + 1) * shard] for i in range(hidden_share)]
        mlp_full = lax.all_gather(
            jnp.concatenate([mlp_in] + packed_out, axis=1), AXES, axis=0, tiled=True
        )
    cut = (space_qkv.shape[1] + width) // 2
    wanted = [
        space_qkv[:, :cut],
        jnp.concatenate([space_qkv[:, cut:], space_proj], axis=1),
        jnp.concatenate([time_qkv, time_proj], axis=1),
    ]
    if shard % 8:
        held = []
        for part in wanted:
            full = lax.all_gather(part, AXES, axis=0, tiled=True).reshape(-1, 2, 8, part.shape[1])
            held.append((full[:, 0], full[:, 1]))
        time_held = held.pop()
        spots_held = held[0][0].shape[0]
        table = jnp.stack(
            [jnp.arange(spots_held, dtype=jnp.int32)] * 2 + [jnp.zeros((spots_held,), jnp.int32)]
        )
        time_steps = []
    else:
        time_steps = list(order_a)
        time_own = wanted[2][None]

        def time_step(value):
            nonlocal time_own
            got = swap(time_own, time_steps.pop(0), count)
            value, got, time_own = lax.optimization_barrier((value, got, time_own))
            value, time_own = lax.optimization_barrier(
                (value, jnp.concatenate([time_own, got], axis=0))
            )
            return value

        one, two = wanted[0][None], wanted[1][None]
        for step, (mask_a, mask_b) in enumerate(zip(order_a, order_b)):
            if step >= 2 and len(time_steps) > 2:
                one = time_step(one)
            got = swap(one, mask_a, count), swap(two, mask_b, count)
            one = jnp.concatenate([one, got[0]], axis=0)
            two = jnp.concatenate([two, got[1]], axis=0)
            for _ in range(min(step, 2)):
                if len(row_steps) > 1:
                    row = row_steps.pop(0)(row)
            one, two, row = lax.optimization_barrier((one, two, row))
        held = [(one, swap(one, 1, count)), (two, swap(two, 1, count))]
        table = place_table((order_a, order_b), chip, core, count)

    while row_steps:
        row = row_steps.pop(0)(row)
    mods = row[0, :mod_width].reshape(9, width)
    first_bias = row[:, mod_width : mod_width + hidden_width]
    second_bias = row[:, mod_width + hidden_width :]

    mask_row = lax.dynamic_index_in_dim(patch_mask, clip_row, 0, keepdims=False)
    key_bias = jnp.where(mask_row == 1, 0.0, MASKED).astype(F32)[:, None]
    space_act, space_packed, space_full, space_out = space_project(tokens, mods, table, held)
    if time_steps:
        space_packed = time_step(space_packed)
    space_heads, space_total, space_branch, after_space = space_forward(
        space_packed, tokens, mods, key_bias, space_out, patches, clip_dev
    )
    if time_steps:
        after_space = time_step(after_space)
    after_here = across(after_space)
    if shard % 8 == 0:
        time_held = time_own, swap(time_own, 1, count)

    shape = (clip_dev, frame_dev, spots, width)
    flat_shape = (FRAMES, spots, width)
    grad_here = jnp.transpose(grad_out.reshape(frame_dev, clip_dev, spots, width), (1, 0, 2, 3))
    after_here, time_held, grad_here = lax.optimization_barrier((after_here, time_held, grad_here))
    after_here = after_here.reshape(flat_shape)
    grad_here = across(grad_here)
    times = time_forward(after_here, mods, table, *time_held)
    times, grad_here = lax.optimization_barrier((times, grad_here))
    time_act, time_packed, time_heads, time_branch, time_total, time_full, time_out = times
    (
        out_here,
        grad_here,
        mlp_act,
        hidden,
        grad_second,
        grad_pre,
        grad_time_branch,
        grad_time_packed,
        sums,
        bias_sums,
    ) = middle(
        after_here,
        grad_here.reshape(flat_shape),
        time_packed,
        time_heads,
        time_branch,
        time_total,
        mods,
        first_bias,
        second_bias,
        time_full,
        time_out,
        mlp_full,
        mlp_share,
    )

    turn_a, turn_b = order_a[::-1], order_b[::-1]
    turn_e = [turn_a[i] for i in (0, 2, 1)] + turn_a[3:]
    turn_t = [turn_a[i] for i in (2, 1, 0)] + turn_a[3:]

    def reduced(*sheets, deep=None):
        return weight_grads(sheets, chip, core, count, shard, width, deep)

    grad_after = across(grad_here.reshape(shape))
    wide = hidden_width // width
    shares = reduced(
        ([(mlp_act, grad_pre, 0, wide)], turn_b), deep=(hidden, grad_second, turn_e)
    )
    shares, grad_after, time_act, out_here = lax.optimization_barrier(
        (shares, grad_after, time_act, out_here)
    )
    out_back = across(out_here.reshape(shape))
    fold_a, fold_e = Fold(shares[:2], turn_b, count), Fold(shares[2:], turn_e, count)
    shares = reduced(
        ([(time_act, grad_time_packed, 0, 3), (time_heads, grad_time_branch, 0, 1)], turn_t)
    )
    shares, grad_after, out_back = meet((shares, grad_after, out_back), fold_a, fold_e)
    fold_b = Fold(shares, turn_t, count)
    grad_space_branch, grad_space_heads, inner, grad_gate = meet(
        space_branch_back(grad_after, space_branch, space_heads, mods, space_out, patches), fold_b
    )
    grads = space_back(
        space_packed,
        grad_space_heads,
        space_total,
        inner,
        key_bias,
        space_full,
        tokens,
        grad_after,
        mods,
        patches,
    )
    grad_space_packed, grad_tokens, space_sums, grad_gate = meet(
        (*grads, grad_gate), fold_a, fold_e, fold_b
    )
    out_tokens = jnp.transpose(out_back, (1, 0, 2, 3)).reshape(length, width)
    rows = jnp.concatenate(
        [space_sums.reshape(1, -1), grad_gate, sums[:6].reshape(1, -1), bias_sums], axis=1
    )
    mask = clip_dev // 2
    got = swap(rows, mask, count)
    shares = reduced(
        ([(space_heads, grad_space_branch, 0, 1), (space_act, grad_space_packed, 0, 1)], turn_a),
        ([(space_act, grad_space_packed, 1, 2)], turn_b),
    )
    shares, rows, got = meet((shares, rows, got), fold_a, fold_e, fold_b)
    fold_c, fold_d = Fold(shares[:2], turn_a, count), Fold(shares[2:], turn_b, count)
    rounds = [(fold_c, fold_d), (fold_a, fold_e, fold_b)]
    while mask:
        rows = rows + got
        mask //= 2
        if mask:
            got = swap(rows, mask, count)
            rows, got = meet((rows, got), *rounds.pop(0)) if rounds else (rows, got)
    mask = clip_dev
    while mask < count:
        got = swap(rows, mask, count)
        if mask == clip_dev:
            rows, got = meet((rows, got), fold_c, fold_d)
        rows = jnp.concatenate([rows, got], axis=0)
        mask *= 2
    while len(fold_a.masks) > 1:
        rows = meet(rows, fold_a, fold_e, fold_b)
    grad_a, grad_b, grad_mlp_out = fold_a.finish(), fold_b.finish(), fold_e.finish()
    grad_rows = rows[:, :mod_width]
    grad_lifted = lax.dot_general(
        grad_rows,
        mod_weight.astype(F32),
        (((1,), (1,)), ((), ())),
        precision=lax.Precision.HIGHEST,
        preferred_element_type=F32,
    )
    near_clips = jnp.arange(count // clip_dev) ^ (me // clip_dev)
    grad_lifted = jnp.take(grad_lifted, near_clips, axis=0)
    grad_lifted = jnp.repeat(
        grad_lifted.reshape(count // sp_size, 1, groups * shard), sp_size, axis=1
    ).reshape(count, groups * shard)
    grad_lifted = lax.all_to_all(grad_lifted, AXES, split_axis=0, concat_axis=0, tiled=True)
    while len(fold_d.masks) > 1:
        grad_a, grad_b = meet(
            (grad_a, grad_b), *[fold for fold in (fold_c, fold_d) if len(fold.masks) > 1]
        )
    grad_c, grad_d = fold_c.finish(), fold_d.finish()
    grad_mlp_in = grad_a
    grad_time_qkv = grad_b[:, : 3 * width]
    grad_time_proj = grad_b[:, 3 * width :]
    grad_space_proj = grad_c[:, :width]
    grad_space_qkv = jnp.concatenate([grad_c[:, width:], grad_d], axis=1)

    grad_mod_weight = lax.dot_general(
        lifted_rows.astype(F32),
        grad_rows,
        (((0,), (0,)), ((), ())),
        precision=lax.Precision.HIGHEST,
        preferred_element_type=F32,
    )
    totals = jnp.sum(rows, axis=0)
    grad_mod_bias = lax.dynamic_slice_in_dim(totals, me * mod_bias.shape[0], mod_bias.shape[0])
    grad_in_bias = lax.dynamic_slice_in_dim(
        totals, mod_width + me * in_bias.shape[0], in_bias.shape[0]
    )
    grad_out_bias = lax.dynamic_slice_in_dim(
        totals, mod_width + hidden_width + me * out_bias.shape[0], out_bias.shape[0]
    )
    grad_lifted = jnp.transpose(grad_lifted.reshape(count, groups, shard), (1, 0, 2))
    grad_lifted = grad_lifted.reshape(groups, width)
    _, silu_back = jax.vjp(jax.nn.silu, condition.astype(F32))
    grad_condition = silu_back(grad_lifted)[0]

    return (
        out_tokens,
        grad_tokens,
        grad_condition,
        grad_mod_weight,
        grad_mod_bias,
        grad_space_qkv,
        grad_space_proj,
        grad_time_qkv,
        grad_time_proj,
        grad_mlp_in,
        grad_in_bias,
        grad_mlp_out,
        grad_out_bias,
    )


def solution(mesh):
    count = mesh.shape["dp"] * mesh.shape["sp"]
    both = P(AXES, None)
    flat = P(AXES)
    clips = P("dp", None)
    return jax.shard_map(
        functools.partial(local, count),
        mesh=mesh,
        in_specs=(
            both, clips, clips, both, both, flat, both, both, both, both, both, flat, both, flat,
        ),
        out_specs=(
            both, both, clips, both, flat, both, both, both, both, both, flat, both, flat,
        ),
        check_vma=False,
    )
```

```python
import functools
import math

import jax
import jax.numpy as jnp
from jax import lax
from jax.experimental import pallas as pl
from jax.experimental.pallas import tpu as pltpu
from jax.sharding import PartitionSpec as P

HEADS = 12
HEAD_DIM = 64
FRAMES = 16
EPSILON = 1e-06
MASKED = -10000.0
APART = -1e30
AXES = ("dp", "sp")
F32 = jnp.float32
BF16 = jnp.bfloat16
MIB = 1 << 20


def swap(values, mask, count):
    return lax.ppermute(values, AXES, [(i, i ^ mask) for i in range(count)])


def chip_orders(count):
    bits = [1 << i for i in range(1, count.bit_length() - 1)]
    low, high, middle = bits[0], bits[-1], bits[1:-1][::-1]
    return (middle + [high, low], middle + [low, high])


def spread(shard, order, count):
    held = shard[None]
    for mask in order:
        held = jnp.concatenate([held, swap(held, mask, count)], axis=0)
    return held


def spread_places(order, count):
    places = []
    for distance in range(count // 2):
        places.append(sum(1 << s for s, mask in enumerate(order) if distance & (mask >> 1)))
    return places


def fold_places(order, count):
    steps = len(order)
    places = []
    for distance in range(count // 2):
        places.append(
            sum(1 << (steps - 1 - s) for s, mask in enumerate(order) if distance & (mask >> 1))
        )
    return places


class Fold:
    def __init__(self, shares, order, count):
        self.keep, self.send = shares
        self.masks = [1] + list(order)
        self.count = count
        self.got = swap(self.send, 1, count)

    def add(self):
        half = self.keep.shape[0] // 2
        low = self.keep[:half].astype(F32) + self.got[:half].astype(F32)
        high = self.keep[half:].astype(F32) + self.got[half:].astype(F32)
        self.keep, self.send = low.astype(BF16), high.astype(BF16)
        self.masks.pop(0)

    def go(self):
        self.got = swap(self.send, self.masks[0], self.count)

    def finish(self):
        while len(self.masks) > 1:
            self.add()
            self.go()
        return self.keep[0].astype(F32) + self.got[0].astype(F32)


def meet(values, *folds):
    values, states = lax.optimization_barrier(
        (values, [(f.keep, f.got) for f in folds])
    )
    for fold, (fold.keep, fold.got) in zip(folds, states):
        fold.add()
    values, states = lax.optimization_barrier((values, [(f.keep, f.send) for f in folds]))
    for fold, (fold.keep, fold.send) in zip(folds, states):
        fold.go()
    return values


def clip_total(row, mask, count):
    while mask:
        row = row + swap(row, mask, count)
        mask //= 2
    return row


def nn(a, b):
    return jnp.dot(a, b, preferred_element_type=F32)


def nt(a, b):
    return lax.dot_general(a, b, (((1,), (1,)), ((), ())), preferred_element_type=F32)


def tn(a, b):
    return lax.dot_general(a, b, (((0,), (0,)), ((), ())), preferred_element_type=F32)


def normalise(values):
    average = jnp.mean(values, axis=-1, keepdims=True)
    centred = values - average
    inverse = lax.rsqrt(jnp.mean(centred * centred, axis=-1, keepdims=True) + EPSILON)
    return centred * inverse, inverse


def norm_back(grad_mod, normed, inverse, scale):
    grad_normed = grad_mod * (1.0 + scale)
    inner = jnp.mean(grad_normed * normed, axis=-1, keepdims=True)
    average = jnp.mean(grad_normed, axis=-1, keepdims=True)
    return inverse * (grad_normed - average - normed * inner)


def column_sum(values):
    return jnp.sum(values, axis=0, keepdims=True)


def halves():
    lane = lax.broadcasted_iota(jnp.int32, (1, 2 * HEAD_DIM), 1)
    first = (lane < HEAD_DIM).astype(F32)
    return first.astype(BF16), (1.0 - first).astype(BF16)


def turned(values):
    return jnp.transpose(values.astype(F32), (1, 0))


def key_lanes(bias, half):
    lane = lax.broadcasted_iota(jnp.int32, (1, 2 * HEAD_DIM), 1) - (1 - half) * HEAD_DIM
    large = bias.astype(BF16).astype(F32)
    lanes = large * (lane == 0).astype(F32) + (bias - large) * (lane == 1).astype(F32)
    return lanes.astype(BF16)


def query_lanes(half):
    lane = lax.broadcasted_iota(jnp.int32, (1, 2 * HEAD_DIM), 1) - (1 - half) * HEAD_DIM
    return jnp.logical_or(lane == 0, lane == 1).astype(F32).astype(BF16)


def biased_scores(queries, keys, half, mask, lanes):
    if lanes is None:
        return nt(keys * (mask * 0.125), queries)
    return nt(keys * (mask * 0.125) + lanes[half], queries * mask + query_lanes(half))


def heads_forward(pairs, apart=None, lanes=None):
    masks = halves()

    def scores_of(item):
        queries, keys, _ = pairs[item // 2]
        return biased_scores(queries, keys, item % 2, masks[item % 2], lanes)

    coming = scores_of(0)
    results = []
    for item in range(2 * len(pairs)):
        scores = coming if apart is None else spaced(coming, apart)
        if item + 1 < 2 * len(pairs):
            coming = scores_of(item + 1)
        if item % 2 == 0:
            values_t = turned(pairs[item // 2][2]).astype(BF16)
            parts, totals = [], []
        largest = jnp.max(scores, axis=0, keepdims=True)
        exponent = jnp.exp(scores - largest)
        denominator = jnp.sum(exponent, axis=0, keepdims=True)
        half = item % 2
        attended = nn(values_t[half * HEAD_DIM : (half + 1) * HEAD_DIM], exponent.astype(BF16))
        parts.append(attended * (1.0 / denominator))
        totals.append(largest + jnp.log(denominator))
        if half == 1:
            attended = jnp.transpose(jnp.concatenate(parts, axis=0), (1, 0)).astype(BF16)
            results.append((attended, jnp.concatenate(totals, axis=0)))
    return results


def spaced(scores, apart):
    rows, lanes = apart.shape
    parts = []
    for start in range(0, scores.shape[1], lanes):
        part = scores[:, start : start + lanes].reshape(-1, rows, lanes) + apart[None]
        parts.append(part.reshape(-1, lanes))
    return jnp.concatenate(parts, axis=1)


def heads_back(pairs, apart=None, lanes=None):
    masks = halves()

    def products_of(item):
        queries, keys, values, grad, _, _ = pairs[item // 2]
        mask = masks[item % 2]
        scores = biased_scores(queries, keys, item % 2, mask, lanes)
        return scores, nt(values * mask, grad)

    coming = products_of(0)
    results = []
    for item in range(2 * len(pairs)):
        scores, grad_probs = coming
        if item + 1 < 2 * len(pairs):
            coming = products_of(item + 1)
        half = item % 2
        queries, keys, _, grad, totals, inner = pairs[item // 2]
        if half == 0:
            keys_t = turned(keys).astype(BF16)
            grad_queries, grad_keys, grad_values = [], 0.0, 0.0
        if apart is not None:
            scores = spaced(scores, apart)
        probable = jnp.exp(scores - totals[half : half + 1])
        grad_scores = (probable * (grad_probs - inner[half : half + 1])).astype(BF16)
        mask = masks[half]
        grad_values += nn(probable.astype(BF16), grad * mask)
        grad_keys += nn(grad_scores, queries * (mask * 0.125))
        grad_queries.append(nn(keys_t[half * HEAD_DIM : (half + 1) * HEAD_DIM], grad_scores))
        if half == 1:
            grad_queries = jnp.transpose(jnp.concatenate(grad_queries, axis=0), (1, 0)) * 0.125
            results.append(
                (grad_queries.astype(BF16), grad_keys.astype(BF16), grad_values.astype(BF16))
            )
    return results


def inner_sums(heads, grad_heads):
    width = heads.shape[1]
    head = lax.broadcasted_iota(jnp.int32, (16, width), 0)
    lane = lax.broadcasted_iota(jnp.int32, (16, width), 1)
    chosen = (lane // HEAD_DIM == head).astype(F32).astype(BF16)
    product = heads.astype(F32) * grad_heads.astype(F32)
    large = product.astype(BF16)
    return nt(chosen, large) + nt(chosen, (product - large.astype(F32)).astype(BF16))


def whole(shape):
    return pl.BlockSpec(shape, lambda *_: (0,) * len(shape), pipeline_mode=pl.Buffered(1))


def whole_out(shape):
    return pl.BlockSpec(shape, lambda *_: (0,) * len(shape))


def params(limit=56):
    return pltpu.CompilerParams(vmem_limit_bytes=limit * MIB)


def cost(flops, moved, special=0):
    return pl.CostEstimate(flops=int(flops) // 16, bytes_accessed=int(moved) // 16, transcendentals=0)


def place_table(orders, chip, core, count):
    chips = count // 2
    index = jnp.arange(chips) ^ chip
    return jnp.stack(
        [jnp.array(spread_places(order, count), jnp.int32)[index] for order in orders]
        + [jnp.full((chips,), core, jnp.int32)]
    )


def build(table, row, own, other, runs):
    chips, share, _ = own.shape
    odd = table[table.shape[0] - 1, 0] == 1

    def step(i, carry):
        place = table[row, i]
        one = own[place].astype(F32)
        two = other[place].astype(F32)
        joined = jnp.concatenate(
            [jnp.where(odd, two, one), jnp.where(odd, one, two)], axis=0
        ).astype(BF16)
        rows = pl.ds(pl.multiple_of(i * 2 * share, 2 * share), 2 * share)
        for column, width, target, start in runs:
            target[rows, start : start + width] = joined[:, column : column + width]
        return carry

    lax.fori_loop(0, chips, step, 0)


def weight_grads(sheets, chip, core, count, share, block, deep=None):
    chips = count // 2
    groups = [group for sheet, _ in sheets for group in sheet]
    length = groups[0][0].shape[0]
    depth = count * share
    steps = [group[3] for group in groups]
    starts = [sum(steps[:i]) for i in range(len(steps))]
    sizes = [sum(group[3] for group in sheet) for sheet, _ in sheets]
    sheet_starts = [sum(sizes[:i]) for i in range(len(sizes))]
    owners = [i for i, (sheet, _) in enumerate(sheets) for _ in sheet]
    total = sum(steps)
    extra = deep[0].shape[1] // block if deep else 0
    orders = [order for _, order in sheets] + ([deep[2]] if deep else [])
    distances = jnp.arange(chips) ^ chip
    table = jnp.concatenate(
        [jnp.array(fold_places(order, count), jnp.int32)[distances] for order in orders]
        + [jnp.full((1,), core, jnp.int32)]
    )

    def body(table, *refs):
        ins, outs = refs[: len(operands)], refs[len(operands) : -1]
        acts_t = refs[-1]
        j = pl.program_id(0)
        odd = table[chips * len(orders)] == 1
        for index, owner in enumerate(owners):
            acts, grads = ins[act_places[index]], ins[grad_places[index]]
            keep, send = outs[2 * owner : 2 * owner + 2]
            here = j - starts[index]

            if index == 0 or act_places[index] != act_places[index - 1]:

                @pl.when(here == 0)
                def _():
                    acts_t[...] = turned(acts[...]).astype(BF16)

            @pl.when(jnp.logical_and(here >= 0, here < steps[index]))
            def _():
                product = nn(acts_t[...], grads[...])
                for pair in range(chips):
                    place = table[owner * chips + pair]
                    start = 2 * pair * share
                    first = product[start : start + share]
                    second = product[start + share : start + 2 * share]
                    keep[place] = jnp.where(odd, second, first).astype(BF16)
                    send[place] = jnp.where(odd, first, second).astype(BF16)

        if deep:
            keep, send = outs[-2:]
            rows = keep.shape[1]
            pairs = block // (2 * rows)

            @pl.when(j >= total)
            def _():
                product = tn(ins[-2][...], ins[-1][...])
                for pair in range(pairs):
                    place = table[len(sheets) * chips + (j - total) * pairs + pair]
                    start = 2 * pair * rows
                    first = product[start : start + rows]
                    second = product[start + rows : start + 2 * rows]
                    keep[place] = jnp.where(odd, second, first).astype(BF16)
                    send[place] = jnp.where(odd, first, second).astype(BF16)

    in_specs = []
    operands = []
    act_places = []
    grad_places = []
    for index, (start, (acts, grads, g_first, blocks)) in enumerate(zip(starts, groups)):
        if index and acts is groups[index - 1][0]:
            act_places.append(act_places[-1])
        else:
            act_places.append(len(operands))
            operands.append(acts)
            in_specs.append(pl.BlockSpec((length, depth), lambda j, t: (0, 0)))
        follows = index and grads is groups[index - 1][1]
        if follows and g_first == groups[index - 1][2] + groups[index - 1][3]:
            grad_places.append(grad_places[-1])
            first, g_start, last = walks.pop()
            walks.append((first, g_start, last + blocks))
        else:
            if index == 0:
                walks = []
            grad_places.append(len(operands))
            operands.append(grads)
            in_specs.append(None)
            walks.append((start, g_first, blocks))
    for place, (start, g_first, blocks) in zip(sorted(set(grad_places)), walks):
        in_specs[place] = pl.BlockSpec(
            (length, block),
            lambda j, t, s=start, m=blocks, g=g_first: (0, g + jnp.clip(j - s, 0, m - 1)),
        )
    out_specs = []
    out_shape = []
    for start, size in zip(sheet_starts, sizes):
        out_specs += [
            pl.BlockSpec(
                (chips, share, block),
                lambda j, t, s=start, m=size: (0, 0, jnp.clip(j - s, 0, m - 1)),
            )
        ] * 2
        out_shape += [jax.ShapeDtypeStruct((chips, share, size * block), BF16)] * 2
    if deep:
        in_specs.append(
            pl.BlockSpec((length, block), lambda j, t: (0, jnp.clip(j - total, 0, extra - 1)))
        )
        in_specs.append(pl.BlockSpec(deep[1].shape, lambda j, t: (0, 0)))
        operands += list(deep[:2])
        shape = (chips, deep[0].shape[1] // count, deep[1].shape[1])
        out_specs += [whole_out(shape)] * 2
        out_shape += [jax.ShapeDtypeStruct(shape, BF16)] * 2
    return pl.pallas_call(
        body,
        grid_spec=pltpu.PrefetchScalarGridSpec(
            num_scalar_prefetch=1,
            grid=(total + extra,),
            in_specs=in_specs,
            out_specs=out_specs,
            scratch_shapes=[pltpu.VMEM((depth, length), BF16)],
        ),
        out_shape=out_shape,
        compiler_params=params(),
        cost_estimate=cost(2 * length * depth * total * block, 4 * depth * total * block),
        name="weight_grads",
    )(table, *operands)


def space_project(tokens, mods, table, held):
    length, width = tokens.shape
    depth = held[0][0].shape[0] * held[0][0].shape[1] * 2
    wide = 3 * width
    cut = held[0][0].shape[2]
    block = 256

    def body(table, tokens, mods, own_a, other_a, own_b, other_b, act, packed, weight, last):
        @pl.when(pl.program_id(0) == 0)
        def _():
            build(table, 0, own_a, other_a, [(0, cut, weight, 0)])
            build(
                table, 1, own_b, other_b, [(0, wide - cut, weight, cut), (wide - cut, width, last, 0)]
            )

        normed, _ = normalise(tokens[...].astype(F32))
        value = (normed * (1.0 + mods[1:2]) + mods[0:1]).astype(BF16)
        act[...] = value
        packed[...] = nn(value, weight[...]).astype(BF16)

    parts = [part for pair in held for part in pair]
    return pl.pallas_call(
        body,
        grid_spec=pltpu.PrefetchScalarGridSpec(
            num_scalar_prefetch=1,
            grid=(length // block,),
            in_specs=[pl.BlockSpec((block, width), lambda i, t: (i, 0)), whole(mods.shape)]
            + [whole(part.shape) for part in parts],
            out_specs=[
                pl.BlockSpec((block, width), lambda i, t: (i, 0)),
                pl.BlockSpec((block, wide), lambda i, t: (i, 0)),
                whole_out((depth, wide)),
                whole_out((depth, width)),
            ],
        ),
        out_shape=[
            jax.ShapeDtypeStruct((length, width), BF16),
            jax.ShapeDtypeStruct((length, wide), BF16),
            jax.ShapeDtypeStruct((depth, wide), BF16),
            jax.ShapeDtypeStruct((depth, width), BF16),
        ],
        compiler_params=params(),
        cost_estimate=cost(2 * length * width * wide, 16 * MIB),
        name="space_project",
    )(table, tokens, mods, *parts)


def space_forward(packed, tokens, mods, bias, weight, patches, peers):
    length, width = tokens.shape
    frames = length // patches
    pairs = width // 128
    spots = patches // peers

    def body(packed, tokens, mods, bias, weight, heads, totals, branch, after):
        lanes = [key_lanes(bias[...], half) for half in range(2)]

        def step(pair, carry):
            at = pl.multiple_of(pair * 128, 128)
            parts = [packed[:, pl.ds(part * width + at, 128)] for part in range(3)]
            ((attended, logs),) = heads_forward([parts], lanes=lanes)
            heads[:, pl.ds(at, 128)] = attended
            totals[0, pair] = logs
            return carry

        lax.fori_loop(0, pairs, step, 0)
        product = nn(heads[...], weight[...])
        branch[...] = product.astype(BF16)
        result = (tokens[...].astype(F32) + mods[2:3] * product).astype(BF16)
        for peer in range(peers):
            after[peer, 0] = result[peer * spots : (peer + 1) * spots]

    def rows(columns):
        return pl.BlockSpec((patches, columns), lambda f: (f, 0))

    return pl.pallas_call(
        body,
        grid=(frames,),
        in_specs=[rows(3 * width), rows(width)]
        + [whole(a.shape) for a in (mods, bias, weight)],
        out_specs=[
            rows(width),
            pl.BlockSpec((1, pairs, 2, patches), lambda f: (f, 0, 0, 0)),
            rows(width),
            pl.BlockSpec((peers, 1, spots, width), lambda f: (0, f, 0, 0)),
        ],
        out_shape=[
            jax.ShapeDtypeStruct((length, width), BF16),
            jax.ShapeDtypeStruct((frames, pairs, 2, patches), F32),
            jax.ShapeDtypeStruct((length, width), BF16),
            jax.ShapeDtypeStruct((peers, frames, spots, width), BF16),
        ],
        compiler_params=params(),
        cost_estimate=cost(10e9, 10 * MIB, 6e6),
        name="space_forward",
    )(packed, tokens, mods, bias, weight)


def space_branch_back(grad_after, branch, heads, mods, weight, patches):
    peers, frames, spots, width = grad_after.shape
    length = frames * patches

    def body(grad_after, branch, heads, mods, weight, grad_branch, grad_heads, inner, grad_gate):
        upstream = grad_after[...].reshape(patches, width).astype(F32)
        value = (upstream * mods[2:3]).astype(BF16)
        grad_branch[...] = value
        grads = nt(value, weight[...]).astype(BF16)
        grad_heads[...] = grads
        rows = inner_sums(heads[...], grads)
        for pair in range(inner.shape[1]):
            inner[0, pair] = rows[2 * pair : 2 * pair + 2]

        @pl.when(pl.program_id(0) == 0)
        def _():
            grad_gate[...] = jnp.zeros_like(grad_gate)

        grad_gate[...] += column_sum(upstream * branch[...].astype(F32))

    return pl.pallas_call(
        body,
        grid=(frames,),
        in_specs=[
            pl.BlockSpec((peers, 1, spots, width), lambda f: (0, f, 0, 0)),
            pl.BlockSpec((patches, width), lambda f: (f, 0)),
            pl.BlockSpec((patches, width), lambda f: (f, 0)),
            whole(mods.shape),
            whole(weight.shape),
        ],
        out_specs=[
            pl.BlockSpec((patches, width), lambda f: (f, 0)),
            pl.BlockSpec((patches, width), lambda f: (f, 0)),
            pl.BlockSpec((1, width // 128, 2, patches), lambda f: (f, 0, 0, 0)),
            whole_out((1, width)),
        ],
        out_shape=[
            jax.ShapeDtypeStruct((length, width), BF16),
            jax.ShapeDtypeStruct((length, width), BF16),
            jax.ShapeDtypeStruct((frames, width // 128, 2, patches), F32),
            jax.ShapeDtypeStruct((1, width), F32),
        ],
        compiler_params=params(),
        cost_estimate=cost(2 * length * width * width, 8 * MIB),
        name="space_branch_back",
    )(grad_after, branch, heads, mods, weight)


def space_back(packed, grad_heads, totals, inner, bias, weight, tokens, grad_after, mods, patches):
    peers, frames, spots, width = grad_after.shape
    length = frames * patches
    pairs = width // 128

    def body(
        packed, grad_heads, totals, inner, bias, weight, tokens, grad_after, mods,
        grad_packed, grad_tokens, sums,
    ):
        lanes = [key_lanes(bias[...], half) for half in range(2)]

        def step(pair, carry):
            at = pl.multiple_of(pair * 128, 128)
            parts = [packed[:, pl.ds(part * width + at, 128)] for part in range(3)]
            rest = [grad_heads[:, pl.ds(at, 128)], totals[0, pair], inner[0, pair]]
            (results,) = heads_back([parts + rest], lanes=lanes)
            for part, result in enumerate(results):
                grad_packed[:, pl.ds(part * width + at, 128)] = result
            return carry

        lax.fori_loop(0, pairs, step, 0)

        @pl.when(pl.program_id(0) == 0)
        def _():
            sums[...] = jnp.zeros_like(sums)

        grad_act = nt(grad_packed[...], weight[...])
        normed, inverse = normalise(tokens[...].astype(F32))
        upstream = grad_after[...].reshape(patches, width).astype(F32)
        grad_tokens[...] = (
            upstream + norm_back(grad_act, normed, inverse, mods[1:2])
        ).astype(BF16)
        sums[0:1] += column_sum(grad_act)
        sums[1:2] += column_sum(grad_act * normed)

    def rows(columns):
        return pl.BlockSpec((patches, columns), lambda f: (f, 0))

    flat = jax.ShapeDtypeStruct((length, width), BF16)
    return pl.pallas_call(
        body,
        grid=(frames,),
        in_specs=[
            rows(3 * width),
            rows(width),
            pl.BlockSpec((1, pairs, 2, patches), lambda f: (f, 0, 0, 0)),
            pl.BlockSpec((1, pairs, 2, patches), lambda f: (f, 0, 0, 0)),
            whole(bias.shape),
            whole(weight.shape),
            rows(width),
            pl.BlockSpec((peers, 1, spots, width), lambda f: (0, f, 0, 0)),
            whole(mods.shape),
        ],
        out_specs=[rows(3 * width), rows(width), whole_out((2, width))],
        out_shape=[
            jax.ShapeDtypeStruct((length, 3 * width), BF16),
            flat,
            jax.ShapeDtypeStruct((2, width), F32),
        ],
        compiler_params=params(),
        cost_estimate=cost(24e9, 20 * MIB, 6e6),
        name="space_back",
    )(packed, grad_heads, totals, inner, bias, weight, tokens, grad_after, mods)


TILE = 16


def apart_bias():
    row = lax.broadcasted_iota(jnp.int32, (TILE, 128), 0)
    column = lax.broadcasted_iota(jnp.int32, (TILE, 128), 1)
    return jnp.where((row & (TILE - 1)) == (column & (TILE - 1)), 0.0, APART)


def part_cuts(pair, width):
    return [slice(p * width + 128 * pair, p * width + 128 * pair + 128) for p in range(3)]


def time_forward(after, mods, table, own, other):
    frames, spots, width = after.shape
    depth = own.shape[0] * own.shape[1] * 2
    block = frames * TILE
    length = frames * spots
    pairs = width // 128

    def body(table, after, mods, own, other, act, packed, heads, branch, totals, time_in, time_out):
        @pl.when(pl.program_id(0) == 0)
        def _():
            build(
                table, 0, own, other, [(0, 3 * width, time_in, 0), (3 * width, width, time_out, 0)]
            )

        apart = apart_bias()
        normed, _ = normalise(after[...].reshape(block, width).astype(F32))
        value = (normed * (1.0 + mods[4:5]) + mods[3:4]).astype(BF16)
        act[...] = value
        packed[...] = nn(value, time_in[...]).astype(BF16)
        parts = [[packed[:, cut] for cut in part_cuts(pair, width)] for pair in range(pairs)]
        for pair, (attended, logs) in enumerate(heads_forward(parts, apart)):
            heads[:, 128 * pair : 128 * pair + 128] = attended
            totals[0, pair] = logs
        branch[...] = nn(heads[...], time_out[...])

    def rows(columns):
        return pl.BlockSpec((block, columns), lambda i, t: (i, 0))

    return pl.pallas_call(
        body,
        grid_spec=pltpu.PrefetchScalarGridSpec(
            num_scalar_prefetch=1,
            grid=(spots // TILE,),
            in_specs=[pl.BlockSpec((frames, TILE, width), lambda i, t: (0, i, 0))]
            + [whole(a.shape) for a in (mods, own, other)],
            out_specs=[
                rows(width),
                rows(3 * width),
                rows(width),
                rows(width),
                pl.BlockSpec((1, pairs, 2, block), lambda i, t: (i, 0, 0, 0)),
                whole_out((depth, 3 * width)),
                whole_out((depth, width)),
            ],
        ),
        out_shape=[
            jax.ShapeDtypeStruct((length, width), BF16),
            jax.ShapeDtypeStruct((length, 3 * width), BF16),
            jax.ShapeDtypeStruct((length, width), BF16),
            jax.ShapeDtypeStruct((length, width), F32),
            jax.ShapeDtypeStruct((spots // TILE, pairs, 2, block), F32),
            jax.ShapeDtypeStruct((depth, 3 * width), BF16),
            jax.ShapeDtypeStruct((depth, width), BF16),
        ],
        compiler_params=params(),
        cost_estimate=cost(8e9, 24 * MIB, 3e6),
        name="time_forward",
    )(table, after, mods, own, other)


def middle(
    after, grad_out, packed, heads, time_branch, totals, mods, first_bias, second_bias, time_in,
    time_out, mlp_full, share,
):
    frames, spots, width = after.shape
    hidden_width = first_bias.shape[1]
    depth = mlp_full.shape[0]
    count = depth // share
    block = frames * TILE
    length = frames * spots
    pairs = width // 128
    chunks = hidden_width // width
    slope = math.sqrt(2.0 / math.pi)

    def body(
        after, grad_out, packed, heads, time_branch, totals,
        mods, first_bias, second_bias, time_in, time_out, first, shares,
        out, grad_after, mlp_act, hidden, grad_second, grad_pre, grad_branch, grad_packed,
        sums, bias_sums, derived, second,
    ):
        @pl.when(pl.program_id(0) == 0)
        def _():
            def unpack(i, carry):
                piece = shares[i].astype(F32)
                parts = [piece[:, c * width : (c + 1) * width] for c in range(chunks)]
                rows = pl.ds(pl.multiple_of(i * chunks * share, chunks * share), chunks * share)
                second[rows] = jnp.concatenate(parts, axis=0).astype(BF16)
                return carry

            lax.fori_loop(0, count, unpack, 0)
            sums[...] = jnp.zeros_like(sums)
            bias_sums[...] = jnp.zeros_like(bias_sums)

        current = after[...].reshape(block, width).astype(F32)
        after_time = current + mods[5:6] * time_branch[...]
        mlp_norm, mlp_inverse = normalise(after_time)
        act = (mlp_norm * (1.0 + mods[7:8]) + mods[6:7]).astype(BF16)
        mlp_act[...] = act
        mlp_branch = 0.0
        for chunk in range(chunks):
            cut = slice(width * chunk, width * chunk + width)
            pre = nn(act, first[:, cut]) + first_bias[:, cut]
            squared = pre * pre
            bent = jnp.tanh(slope * pre * (1.0 + 0.044715 * squared))
            half = 0.5 * (1.0 + bent)
            value = (pre * half).astype(BF16)
            hidden[:, cut] = value
            derived[:, cut] = half + 0.5 * slope * pre * (1.0 - bent * bent) * (
                1.0 + 3.0 * 0.044715 * squared
            )
            mlp_branch += nn(value, second[cut])
        mlp_branch += second_bias[...]
        out[...] = (after_time + mods[8:9] * mlp_branch).astype(BF16).reshape(frames, TILE, width)

        upstream = grad_out[...].reshape(block, width).astype(F32)
        sums[5:6] += column_sum(upstream * mlp_branch)
        grad_value = (upstream * mods[8:9]).astype(BF16)
        grad_second[...] = grad_value
        bias_sums[:, hidden_width:] += column_sum(grad_value.astype(F32))
        grad_act = 0.0
        for chunk in range(chunks):
            cut = slice(width * chunk, width * chunk + width)
            value = (nt(grad_value, second[cut]) * derived[:, cut]).astype(BF16)
            grad_pre[:, cut] = value
            bias_sums[:, cut] += column_sum(value.astype(F32))
            grad_act += nt(value, first[:, cut])
        sums[3:4] += column_sum(grad_act)
        sums[4:5] += column_sum(grad_act * mlp_norm)
        upstream = upstream + norm_back(grad_act, mlp_norm, mlp_inverse, mods[7:8])

        sums[2:3] += column_sum(upstream * time_branch[...])
        grad_value = (upstream * mods[5:6]).astype(BF16)
        grad_branch[...] = grad_value
        grad_heads = nt(grad_value, time_out[...]).astype(BF16)
        apart = apart_bias()
        inner = inner_sums(heads[...], grad_heads)
        parts = []
        for pair in range(pairs):
            cuts = part_cuts(pair, width)
            parts.append(
                [packed[:, cut] for cut in cuts]
                + [grad_heads[:, cuts[0]], totals[0, pair], inner[2 * pair : 2 * pair + 2]]
            )
        for pair, results in enumerate(heads_back(parts, apart)):
            for cut, part in zip(part_cuts(pair, width), results):
                grad_packed[:, cut] = part
        grad_act = nt(grad_packed[...], time_in[...]).astype(BF16).astype(F32)
        time_norm, time_inverse = normalise(current)
        sums[0:1] += column_sum(grad_act)
        sums[1:2] += column_sum(grad_act * time_norm)
        upstream = upstream + norm_back(grad_act, time_norm, time_inverse, mods[4:5])
        grad_after[...] = upstream.astype(BF16).reshape(frames, TILE, width)

    moving = pl.BlockSpec((frames, TILE, width), lambda i: (0, i, 0))

    def rows(columns):
        return pl.BlockSpec((block, columns), lambda i: (i, 0))

    def array(columns):
        return jax.ShapeDtypeStruct((length, columns), BF16)

    narrow, wide, triple = width, hidden_width, 3 * width
    kept = [narrow, wide, narrow, wide, narrow, triple]
    held = (mods, first_bias, second_bias, time_in, time_out)
    shares = mlp_full.reshape(count, share, 2 * hidden_width)
    return pl.pallas_call(
        body,
        grid=(spots // TILE,),
        in_specs=[moving, moving, rows(triple), rows(width), rows(width)]
        + [pl.BlockSpec((1, pairs, 2, block), lambda i: (i, 0, 0, 0))]
        + [whole(a.shape) for a in held]
        + [
            pl.BlockSpec((depth, hidden_width), lambda i: (0, 0), pipeline_mode=pl.Buffered(1)),
            pl.BlockSpec(
                (count, share, hidden_width), lambda i: (0, 0, 1), pipeline_mode=pl.Buffered(1)
            ),
        ],
        out_specs=[moving, moving]
        + [rows(c) for c in kept]
        + [whole_out((8, width)), whole_out((1, hidden_width + width))],
        out_shape=[jax.ShapeDtypeStruct(after.shape, BF16)] * 2
        + [array(c) for c in kept]
        + [
            jax.ShapeDtypeStruct((8, width), F32),
            jax.ShapeDtypeStruct((1, hidden_width + width), F32),
        ],
        scratch_shapes=[
            pltpu.VMEM((block, hidden_width), F32),
            pltpu.VMEM((hidden_width, width), BF16),
        ],
        compiler_params=params(60),
        cost_estimate=cost(40e9, 50 * MIB, 8e6),
        name="middle",
    )(after, grad_out, packed, heads, time_branch, totals, *held, mlp_full, shares)


def local(
    count,
    tokens,
    condition,
    patch_mask,
    grad_out,
    mod_weight,
    mod_bias,
    space_qkv,
    space_proj,
    time_qkv,
    time_proj,
    mlp_in,
    in_bias,
    mlp_out,
    out_bias,
):
    length, width = tokens.shape
    patches = patch_mask.shape[1]
    frame_dev = length // patches
    groups = condition.shape[0]
    clip_dev = FRAMES // frame_dev
    spots = patches // clip_dev
    sp_size = lax.axis_size("sp")
    shard = mod_weight.shape[0]
    mod_width = mod_weight.shape[1]
    hidden_width = mlp_in.shape[1]
    me = lax.axis_index("dp") * sp_size + lax.axis_index("sp")
    chip = me // 2
    core = me % 2
    clip_row = lax.axis_index("sp") // clip_dev
    order_a, order_b = chip_orders(count)
    teams = [list(range(s, s + clip_dev)) for s in range(0, sp_size, clip_dev)]

    def across(values):
        return lax.all_to_all(
            values, "sp", split_axis=0, concat_axis=0, tiled=True, axis_index_groups=teams
        )

    near = jnp.stack([condition[clip_row ^ s] for s in range(groups)])
    mask = sp_size
    while mask < count:
        near = jnp.concatenate([near, swap(near, mask, count)], axis=0)
        mask *= 2
    lifted = jax.nn.silu(near.astype(F32)).astype(BF16)
    lifted_rows = lax.dynamic_slice_in_dim(lifted, me * shard, shard, 1)
    part = jnp.dot(lifted_rows, mod_weight, preferred_element_type=F32)
    own = jnp.zeros((mod_width + hidden_width + width,), F32)
    own = lax.dynamic_update_slice(own, mod_bias.astype(F32), (me * mod_bias.shape[0],))
    own = lax.dynamic_update_slice(
        own, in_bias.astype(F32), (mod_width + me * in_bias.shape[0],)
    )
    own = lax.dynamic_update_slice(
        own, out_bias.astype(F32), (mod_width + hidden_width + me * out_bias.shape[0],)
    )
    row = jnp.pad(part, ((0, 0), (0, hidden_width + width))) + own[None]

    def row_halved(row, mask):
        half = row.shape[0] // 2
        return row[:half] + swap(row[half:], mask, count)

    def row_added(row, mask):
        return row + swap(row, mask, count)

    row_steps = []
    mask = count // 2
    while mask:
        row_steps.append(functools.partial(row_halved if mask >= clip_dev else row_added, mask=mask))
        mask //= 2

    hidden_share = mlp_out.shape[0] // shard
    if shard % 8:
        mlp_share = 8
        full = lax.all_gather(mlp_out, AXES, axis=0, tiled=True)
        full = full.reshape(-1, hidden_share, mlp_share, width)
        full = jnp.transpose(full, (0, 2, 1, 3)).reshape(-1, hidden_width)
        mlp_full = jnp.concatenate([lax.all_gather(mlp_in, AXES, axis=0, tiled=True), full], axis=1)
    else:
        mlp_share = shard
        packed_out = [mlp_out[i * shard : (i + 1) * shard] for i in range(hidden_share)]
        mlp_full = lax.all_gather(
            jnp.concatenate([mlp_in] + packed_out, axis=1), AXES, axis=0, tiled=True
        )
    cut = (space_qkv.shape[1] + width) // 2
    wanted = [
        space_qkv[:, :cut],
        jnp.concatenate([space_qkv[:, cut:], space_proj], axis=1),
        jnp.concatenate([time_qkv, time_proj], axis=1),
    ]
    if shard % 8:
        held = []
        for part in wanted:
            full = lax.all_gather(part, AXES, axis=0, tiled=True).reshape(-1, 2, 8, part.shape[1])
            held.append((full[:, 0], full[:, 1]))
        time_held = held.pop()
        spots_held = held[0][0].shape[0]
        table = jnp.stack(
            [jnp.arange(spots_held, dtype=jnp.int32)] * 2 + [jnp.zeros((spots_held,), jnp.int32)]
        )
        time_steps = []
    else:
        time_steps = list(order_a)
        time_own = wanted[2][None]

        def time_step(value):
            nonlocal time_own
            got = swap(time_own, time_steps.pop(0), count)
            value, got, time_own = lax.optimization_barrier((value, got, time_own))
            value, time_own = lax.optimization_barrier(
                (value, jnp.concatenate([time_own, got], axis=0))
            )
            return value

        one, two = wanted[0][None], wanted[1][None]
        for step, (mask_a, mask_b) in enumerate(zip(order_a, order_b)):
            if step >= 2 and len(time_steps) > 2:
                one = time_step(one)
            got = swap(one, mask_a, count), swap(two, mask_b, count)
            one = jnp.concatenate([one, got[0]], axis=0)
            two = jnp.concatenate([two, got[1]], axis=0)
            for _ in range(min(step, 2)):
                if len(row_steps) > 1:
                    row = row_steps.pop(0)(row)
            one, two, row = lax.optimization_barrier((one, two, row))
        held = [(one, swap(one, 1, count)), (two, swap(two, 1, count))]
        table = place_table((order_a, order_b), chip, core, count)

    while row_steps:
        row = row_steps.pop(0)(row)
    mods = row[0, :mod_width].reshape(9, width)
    first_bias = row[:, mod_width : mod_width + hidden_width]
    second_bias = row[:, mod_width + hidden_width :]

    mask_row = lax.dynamic_index_in_dim(patch_mask, clip_row, 0, keepdims=False)
    key_bias = jnp.where(mask_row == 1, 0.0, MASKED).astype(F32)[:, None]
    space_act, space_packed, space_full, space_out = space_project(tokens, mods, table, held)
    if time_steps:
        space_packed = time_step(space_packed)
    space_heads, space_total, space_branch, after_space = space_forward(
        space_packed, tokens, mods, key_bias, space_out, patches, clip_dev
    )
    if time_steps:
        after_space = time_step(after_space)
    after_here = across(after_space)
    if shard % 8 == 0:
        time_held = time_own, swap(time_own, 1, count)

    shape = (clip_dev, frame_dev, spots, width)
    flat_shape = (FRAMES, spots, width)
    grad_here = jnp.transpose(grad_out.reshape(frame_dev, clip_dev, spots, width), (1, 0, 2, 3))
    after_here, time_held, grad_here = lax.optimization_barrier((after_here, time_held, grad_here))
    after_here = after_here.reshape(flat_shape)
    grad_here = across(grad_here)
    times = time_forward(after_here, mods, table, *time_held)
    times, grad_here = lax.optimization_barrier((times, grad_here))
    time_act, time_packed, time_heads, time_branch, time_total, time_full, time_out = times
    (
        out_here,
        grad_here,
        mlp_act,
        hidden,
        grad_second,
        grad_pre,
        grad_time_branch,
        grad_time_packed,
        sums,
        bias_sums,
    ) = middle(
        after_here,
        grad_here.reshape(flat_shape),
        time_packed,
        time_heads,
        time_branch,
        time_total,
        mods,
        first_bias,
        second_bias,
        time_full,
        time_out,
        mlp_full,
        mlp_share,
    )

    turn_a, turn_b = order_a[::-1], order_b[::-1]
    turn_e = [turn_a[i] for i in (0, 2, 1)] + turn_a[3:]
    turn_t = [turn_a[i] for i in (2, 1, 0)] + turn_a[3:]

    def reduced(*sheets, deep=None):
        return weight_grads(sheets, chip, core, count, shard, width, deep)

    grad_after = across(grad_here.reshape(shape))
    wide = hidden_width // width
    shares = reduced(
        ([(mlp_act, grad_pre, 0, wide)], turn_b), deep=(hidden, grad_second, turn_e)
    )
    shares, grad_after, time_act, out_here = lax.optimization_barrier(
        (shares, grad_after, time_act, out_here)
    )
    out_back = across(out_here.reshape(shape))
    fold_a, fold_e = Fold(shares[:2], turn_b, count), Fold(shares[2:], turn_e, count)
    shares = reduced(
        ([(time_act, grad_time_packed, 0, 3), (time_heads, grad_time_branch, 0, 1)], turn_t)
    )
    shares, grad_after, out_back = meet((shares, grad_after, out_back), fold_a, fold_e)
    fold_b = Fold(shares, turn_t, count)
    grad_space_branch, grad_space_heads, inner, grad_gate = meet(
        space_branch_back(grad_after, space_branch, space_heads, mods, space_out, patches), fold_b
    )
    grads = space_back(
        space_packed,
        grad_space_heads,
        space_total,
        inner,
        key_bias,
        space_full,
        tokens,
        grad_after,
        mods,
        patches,
    )
    grad_space_packed, grad_tokens, space_sums, grad_gate = meet(
        (*grads, grad_gate), fold_a, fold_e, fold_b
    )
    out_tokens = jnp.transpose(out_back, (1, 0, 2, 3)).reshape(length, width)
    rows = jnp.concatenate(
        [space_sums.reshape(1, -1), grad_gate, sums[:6].reshape(1, -1), bias_sums], axis=1
    )
    mask = clip_dev // 2
    got = swap(rows, mask, count)
    shares = reduced(
        ([(space_heads, grad_space_branch, 0, 1), (space_act, grad_space_packed, 0, 1)], turn_a),
        ([(space_act, grad_space_packed, 1, 2)], turn_b),
    )
    shares, rows, got = meet((shares, rows, got), fold_a, fold_e, fold_b)
    fold_c, fold_d = Fold(shares[:2], turn_a, count), Fold(shares[2:], turn_b, count)
    rounds = [(fold_c, fold_d), (fold_a, fold_e, fold_b)]
    while mask:
        rows = rows + got
        mask //= 2
        if mask:
            got = swap(rows, mask, count)
            rows, got = meet((rows, got), *rounds.pop(0)) if rounds else (rows, got)
    mask = clip_dev
    while mask < count:
        got = swap(rows, mask, count)
        if mask == clip_dev:
            rows, got = meet((rows, got), fold_c, fold_d)
        rows = jnp.concatenate([rows, got], axis=0)
        mask *= 2
    while len(fold_a.masks) > 1:
        rows = meet(rows, fold_a, fold_e, fold_b)
    grad_a, grad_b, grad_mlp_out = fold_a.finish(), fold_b.finish(), fold_e.finish()
    if len(fold_c.masks) > 1:
        rows = meet(rows, fold_c, fold_d)
    grad_rows = rows[:, :mod_width]
    grad_lifted = lax.dot_general(
        grad_rows,
        mod_weight.astype(F32),
        (((1,), (1,)), ((), ())),
        precision=lax.Precision.HIGHEST,
        preferred_element_type=F32,
    )
    near_clips = jnp.arange(count // clip_dev) ^ (me // clip_dev)
    grad_lifted = jnp.take(grad_lifted, near_clips, axis=0)
    grad_lifted = jnp.repeat(
        grad_lifted.reshape(count // sp_size, 1, groups * shard), sp_size, axis=1
    ).reshape(count, groups * shard)
    if len(fold_c.masks) > 1:
        grad_lifted = meet(grad_lifted, fold_c, fold_d)
    grad_lifted = lax.all_to_all(grad_lifted, AXES, split_axis=0, concat_axis=0, tiled=True)
    while len(fold_d.masks) > 1:
        grad_a, grad_b = meet(
            (grad_a, grad_b), *[fold for fold in (fold_c, fold_d) if len(fold.masks) > 1]
        )
    grad_c, grad_d = fold_c.finish(), fold_d.finish()
    grad_mlp_in = grad_a
    grad_time_qkv = grad_b[:, : 3 * width]
    grad_time_proj = grad_b[:, 3 * width :]
    grad_space_proj = grad_c[:, :width]
    grad_space_qkv = jnp.concatenate([grad_c[:, width:], grad_d], axis=1)

    grad_mod_weight = lax.dot_general(
        lifted_rows.astype(F32),
        grad_rows,
        (((0,), (0,)), ((), ())),
        precision=lax.Precision.HIGHEST,
        preferred_element_type=F32,
    )
    totals = jnp.sum(rows, axis=0)
    grad_mod_bias = lax.dynamic_slice_in_dim(totals, me * mod_bias.shape[0], mod_bias.shape[0])
    grad_in_bias = lax.dynamic_slice_in_dim(
        totals, mod_width + me * in_bias.shape[0], in_bias.shape[0]
    )
    grad_out_bias = lax.dynamic_slice_in_dim(
        totals, mod_width + hidden_width + me * out_bias.shape[0], out_bias.shape[0]
    )
    grad_lifted = jnp.transpose(grad_lifted.reshape(count, groups, shard), (1, 0, 2))
    grad_lifted = grad_lifted.reshape(groups, width)
    _, silu_back = jax.vjp(jax.nn.silu, condition.astype(F32))
    grad_condition = silu_back(grad_lifted)[0]

    return (
        out_tokens,
        grad_tokens,
        grad_condition,
        grad_mod_weight,
        grad_mod_bias,
        grad_space_qkv,
        grad_space_proj,
        grad_time_qkv,
        grad_time_proj,
        grad_mlp_in,
        grad_in_bias,
        grad_mlp_out,
        grad_out_bias,
    )


def solution(mesh):
    count = mesh.shape["dp"] * mesh.shape["sp"]
    both = P(AXES, None)
    flat = P(AXES)
    clips = P("dp", None)
    return jax.shard_map(
        functools.partial(local, count),
        mesh=mesh,
        in_specs=(
            both, clips, clips, both, both, flat, both, both, both, both, both, flat, both, flat,
        ),
        out_specs=(
            both, both, clips, both, flat, both, both, both, both, both, flat, both, flat,
        ),
        check_vma=False,
    )
```

```python
import functools
import math

import jax
import jax.numpy as jnp
from jax import lax
from jax.experimental import pallas as pl
from jax.experimental.pallas import tpu as pltpu
from jax.sharding import PartitionSpec as P

HEADS = 12
HEAD_DIM = 64
FRAMES = 16
EPSILON = 1e-06
MASKED = -10000.0
APART = -1e30
AXES = ("dp", "sp")
F32 = jnp.float32
BF16 = jnp.bfloat16
MIB = 1 << 20


def swap(values, mask, count):
    return lax.ppermute(values, AXES, [(i, i ^ mask) for i in range(count)])


def chip_orders(count):
    bits = [1 << i for i in range(1, count.bit_length() - 1)]
    low, high, middle = bits[0], bits[-1], bits[1:-1][::-1]
    return (middle + [high, low], middle + [low, high])


def spread(shard, order, count):
    held = shard[None]
    for mask in order:
        held = jnp.concatenate([held, swap(held, mask, count)], axis=0)
    return held


def spread_places(order, count):
    places = []
    for distance in range(count // 2):
        places.append(sum(1 << s for s, mask in enumerate(order) if distance & (mask >> 1)))
    return places


def fold_places(order, count):
    steps = len(order)
    places = []
    for distance in range(count // 2):
        places.append(
            sum(1 << (steps - 1 - s) for s, mask in enumerate(order) if distance & (mask >> 1))
        )
    return places


class Fold:
    def __init__(self, shares, order, count):
        self.keep, self.send = shares
        self.masks = [1] + list(order)
        self.count = count
        self.got = swap(self.send, 1, count)

    def add(self):
        half = self.keep.shape[0] // 2
        low = self.keep[:half].astype(F32) + self.got[:half].astype(F32)
        high = self.keep[half:].astype(F32) + self.got[half:].astype(F32)
        self.keep, self.send = low.astype(BF16), high.astype(BF16)
        self.masks.pop(0)

    def go(self):
        self.got = swap(self.send, self.masks[0], self.count)

    def finish(self):
        while len(self.masks) > 1:
            self.add()
            self.go()
        return self.keep[0].astype(F32) + self.got[0].astype(F32)


def meet(values, *folds):
    values, states = lax.optimization_barrier(
        (values, [(f.keep, f.got) for f in folds])
    )
    for fold, (fold.keep, fold.got) in zip(folds, states):
        fold.add()
    values, states = lax.optimization_barrier((values, [(f.keep, f.send) for f in folds]))
    for fold, (fold.keep, fold.send) in zip(folds, states):
        fold.go()
    return values


def clip_total(row, mask, count):
    while mask:
        row = row + swap(row, mask, count)
        mask //= 2
    return row


def nn(a, b):
    return jnp.dot(a, b, preferred_element_type=F32)


def nt(a, b):
    return lax.dot_general(a, b, (((1,), (1,)), ((), ())), preferred_element_type=F32)


def tn(a, b):
    return lax.dot_general(a, b, (((0,), (0,)), ((), ())), preferred_element_type=F32)


def normalise(values):
    average = jnp.mean(values, axis=-1, keepdims=True)
    centred = values - average
    inverse = lax.rsqrt(jnp.mean(centred * centred, axis=-1, keepdims=True) + EPSILON)
    return centred * inverse, inverse


def norm_back(grad_mod, normed, inverse, scale):
    grad_normed = grad_mod * (1.0 + scale)
    inner = jnp.mean(grad_normed * normed, axis=-1, keepdims=True)
    average = jnp.mean(grad_normed, axis=-1, keepdims=True)
    return inverse * (grad_normed - average - normed * inner)


def column_sum(values):
    return jnp.sum(values, axis=0, keepdims=True)


def halves():
    lane = lax.broadcasted_iota(jnp.int32, (1, 2 * HEAD_DIM), 1)
    first = (lane < HEAD_DIM).astype(F32)
    return first.astype(BF16), (1.0 - first).astype(BF16)


def turned(values):
    return jnp.transpose(values.astype(F32), (1, 0))


def key_lanes(bias, half):
    lane = lax.broadcasted_iota(jnp.int32, (1, 2 * HEAD_DIM), 1) - (1 - half) * HEAD_DIM
    large = bias.astype(BF16).astype(F32)
    lanes = large * (lane == 0).astype(F32) + (bias - large) * (lane == 1).astype(F32)
    return lanes.astype(BF16)


def query_lanes(half):
    lane = lax.broadcasted_iota(jnp.int32, (1, 2 * HEAD_DIM), 1) - (1 - half) * HEAD_DIM
    return jnp.logical_or(lane == 0, lane == 1).astype(F32).astype(BF16)


def biased_scores(queries, keys, half, mask, lanes):
    if lanes is None:
        return nt(keys * (mask * 0.125), queries)
    return nt(keys * (mask * 0.125) + lanes[half], queries * mask + query_lanes(half))


def heads_forward(pairs, apart=None, lanes=None):
    masks = halves()

    def scores_of(item):
        queries, keys, _ = pairs[item // 2]
        return biased_scores(queries, keys, item % 2, masks[item % 2], lanes)

    coming = scores_of(0)
    results = []
    for item in range(2 * len(pairs)):
        scores = coming if apart is None else spaced(coming, apart)
        if item + 1 < 2 * len(pairs):
            coming = scores_of(item + 1)
        if item % 2 == 0:
            values_t = turned(pairs[item // 2][2]).astype(BF16)
            parts, totals = [], []
        largest = jnp.max(scores, axis=0, keepdims=True)
        exponent = jnp.exp(scores - largest)
        denominator = jnp.sum(exponent, axis=0, keepdims=True)
        half = item % 2
        attended = nn(values_t[half * HEAD_DIM : (half + 1) * HEAD_DIM], exponent.astype(BF16))
        parts.append(attended * (1.0 / denominator))
        totals.append(largest + jnp.log(denominator))
        if half == 1:
            attended = jnp.transpose(jnp.concatenate(parts, axis=0), (1, 0)).astype(BF16)
            results.append((attended, jnp.concatenate(totals, axis=0)))
    return results


def spaced(scores, apart):
    rows, lanes = apart.shape
    parts = []
    for start in range(0, scores.shape[1], lanes):
        part = scores[:, start : start + lanes].reshape(-1, rows, lanes) + apart[None]
        parts.append(part.reshape(-1, lanes))
    return jnp.concatenate(parts, axis=1)


def heads_back(pairs, apart=None, lanes=None):
    masks = halves()

    def products_of(item):
        queries, keys, values, grad, _, _ = pairs[item // 2]
        mask = masks[item % 2]
        scores = biased_scores(queries, keys, item % 2, mask, lanes)
        return scores, nt(values * mask, grad)

    coming = products_of(0)
    results = []
    for item in range(2 * len(pairs)):
        scores, grad_probs = coming
        if item + 1 < 2 * len(pairs):
            coming = products_of(item + 1)
        half = item % 2
        queries, keys, _, grad, totals, inner = pairs[item // 2]
        if half == 0:
            keys_t = turned(keys).astype(BF16)
            grad_queries, grad_keys, grad_values = [], 0.0, 0.0
        if apart is not None:
            scores = spaced(scores, apart)
        probable = jnp.exp(scores - totals[half : half + 1])
        grad_scores = (probable * (grad_probs - inner[half : half + 1])).astype(BF16)
        mask = masks[half]
        grad_values += nn(probable.astype(BF16), grad * mask)
        grad_keys += nn(grad_scores, queries * (mask * 0.125))
        grad_queries.append(nn(keys_t[half * HEAD_DIM : (half + 1) * HEAD_DIM], grad_scores))
        if half == 1:
            grad_queries = jnp.transpose(jnp.concatenate(grad_queries, axis=0), (1, 0)) * 0.125
            results.append(
                (grad_queries.astype(BF16), grad_keys.astype(BF16), grad_values.astype(BF16))
            )
    return results


def inner_sums(heads, grad_heads):
    width = heads.shape[1]
    head = lax.broadcasted_iota(jnp.int32, (16, width), 0)
    lane = lax.broadcasted_iota(jnp.int32, (16, width), 1)
    chosen = (lane // HEAD_DIM == head).astype(F32).astype(BF16)
    product = heads.astype(F32) * grad_heads.astype(F32)
    large = product.astype(BF16)
    return nt(chosen, large) + nt(chosen, (product - large.astype(F32)).astype(BF16))


def whole(shape):
    return pl.BlockSpec(shape, lambda *_: (0,) * len(shape), pipeline_mode=pl.Buffered(1))


def whole_out(shape):
    return pl.BlockSpec(shape, lambda *_: (0,) * len(shape))


def params(limit=56):
    return pltpu.CompilerParams(vmem_limit_bytes=limit * MIB)


def cost(flops, moved, special=0):
    return pl.CostEstimate(flops=int(flops) // 16, bytes_accessed=int(moved) // 16, transcendentals=0)


def place_table(orders, chip, core, count):
    chips = count // 2
    index = jnp.arange(chips) ^ chip
    return jnp.stack(
        [jnp.array(spread_places(order, count), jnp.int32)[index] for order in orders]
        + [jnp.full((chips,), core, jnp.int32)]
    )


def build(table, row, own, other, runs):
    chips, share, _ = own.shape
    odd = table[table.shape[0] - 1, 0] == 1

    def step(i, carry):
        place = table[row, i]
        one = own[place].astype(F32)
        two = other[place].astype(F32)
        joined = jnp.concatenate(
            [jnp.where(odd, two, one), jnp.where(odd, one, two)], axis=0
        ).astype(BF16)
        rows = pl.ds(pl.multiple_of(i * 2 * share, 2 * share), 2 * share)
        for column, width, target, start in runs:
            target[rows, start : start + width] = joined[:, column : column + width]
        return carry

    lax.fori_loop(0, chips, step, 0)


def weight_grads(sheets, chip, core, count, share, block, deep=None):
    chips = count // 2
    groups = [group for sheet, _ in sheets for group in sheet]
    length = groups[0][0].shape[0]
    depth = count * share
    steps = [group[3] for group in groups]
    starts = [sum(steps[:i]) for i in range(len(steps))]
    sizes = [sum(group[3] for group in sheet) for sheet, _ in sheets]
    sheet_starts = [sum(sizes[:i]) for i in range(len(sizes))]
    owners = [i for i, (sheet, _) in enumerate(sheets) for _ in sheet]
    total = sum(steps)
    extra = deep[0].shape[1] // block if deep else 0
    orders = [order for _, order in sheets] + ([deep[2]] if deep else [])
    distances = jnp.arange(chips) ^ chip
    table = jnp.concatenate(
        [jnp.array(fold_places(order, count), jnp.int32)[distances] for order in orders]
        + [jnp.full((1,), core, jnp.int32)]
    )

    def body(table, *refs):
        ins, outs = refs[: len(operands)], refs[len(operands) : -1]
        acts_t = refs[-1]
        j = pl.program_id(0)
        odd = table[chips * len(orders)] == 1
        for index, owner in enumerate(owners):
            acts, grads = ins[act_places[index]], ins[grad_places[index]]
            keep, send = outs[2 * owner : 2 * owner + 2]
            here = j - starts[index]

            if index == 0 or act_places[index] != act_places[index - 1]:

                @pl.when(here == 0)
                def _():
                    acts_t[...] = turned(acts[...]).astype(BF16)

            @pl.when(jnp.logical_and(here >= 0, here < steps[index]))
            def _():
                product = nn(acts_t[...], grads[...])
                for pair in range(chips):
                    place = table[owner * chips + pair]
                    start = 2 * pair * share
                    first = product[start : start + share]
                    second = product[start + share : start + 2 * share]
                    keep[place] = jnp.where(odd, second, first).astype(BF16)
                    send[place] = jnp.where(odd, first, second).astype(BF16)

        if deep:
            keep, send = outs[-2:]
            rows = keep.shape[1]
            pairs = block // (2 * rows)

            @pl.when(j >= total)
            def _():
                product = tn(ins[-2][...], ins[-1][...])
                for pair in range(pairs):
                    place = table[len(sheets) * chips + (j - total) * pairs + pair]
                    start = 2 * pair * rows
                    first = product[start : start + rows]
                    second = product[start + rows : start + 2 * rows]
                    keep[place] = jnp.where(odd, second, first).astype(BF16)
                    send[place] = jnp.where(odd, first, second).astype(BF16)

    in_specs = []
    operands = []
    act_places = []
    grad_places = []
    for index, (start, (acts, grads, g_first, blocks)) in enumerate(zip(starts, groups)):
        if index and acts is groups[index - 1][0]:
            act_places.append(act_places[-1])
        else:
            act_places.append(len(operands))
            operands.append(acts)
            in_specs.append(pl.BlockSpec((length, depth), lambda j, t: (0, 0)))
        follows = index and grads is groups[index - 1][1]
        if follows and g_first == groups[index - 1][2] + groups[index - 1][3]:
            grad_places.append(grad_places[-1])
            first, g_start, last = walks.pop()
            walks.append((first, g_start, last + blocks))
        else:
            if index == 0:
                walks = []
            grad_places.append(len(operands))
            operands.append(grads)
            in_specs.append(None)
            walks.append((start, g_first, blocks))
    for place, (start, g_first, blocks) in zip(sorted(set(grad_places)), walks):
        in_specs[place] = pl.BlockSpec(
            (length, block),
            lambda j, t, s=start, m=blocks, g=g_first: (0, g + jnp.clip(j - s, 0, m - 1)),
        )
    out_specs = []
    out_shape = []
    for start, size in zip(sheet_starts, sizes):
        out_specs += [
            pl.BlockSpec(
                (chips, share, block),
                lambda j, t, s=start, m=size: (0, 0, jnp.clip(j - s, 0, m - 1)),
            )
        ] * 2
        out_shape += [jax.ShapeDtypeStruct((chips, share, size * block), BF16)] * 2
    if deep:
        in_specs.append(
            pl.BlockSpec((length, block), lambda j, t: (0, jnp.clip(j - total, 0, extra - 1)))
        )
        in_specs.append(pl.BlockSpec(deep[1].shape, lambda j, t: (0, 0)))
        operands += list(deep[:2])
        shape = (chips, deep[0].shape[1] // count, deep[1].shape[1])
        out_specs += [whole_out(shape)] * 2
        out_shape += [jax.ShapeDtypeStruct(shape, BF16)] * 2
    return pl.pallas_call(
        body,
        grid_spec=pltpu.PrefetchScalarGridSpec(
            num_scalar_prefetch=1,
            grid=(total + extra,),
            in_specs=in_specs,
            out_specs=out_specs,
            scratch_shapes=[pltpu.VMEM((depth, length), BF16)],
        ),
        out_shape=out_shape,
        compiler_params=params(),
        cost_estimate=cost(2 * length * depth * total * block, 4 * depth * total * block),
        name="weight_grads",
    )(table, *operands)


def space_project(tokens, mods, table, held):
    length, width = tokens.shape
    depth = held[0][0].shape[0] * held[0][0].shape[1] * 2
    wide = 3 * width
    cut = held[0][0].shape[2]
    block = 256

    def body(table, tokens, mods, own_a, other_a, own_b, other_b, act, packed, weight, last):
        @pl.when(pl.program_id(0) == 0)
        def _():
            build(table, 0, own_a, other_a, [(0, cut, weight, 0)])
            build(
                table, 1, own_b, other_b, [(0, wide - cut, weight, cut), (wide - cut, width, last, 0)]
            )

        normed, _ = normalise(tokens[...].astype(F32))
        value = (normed * (1.0 + mods[1:2]) + mods[0:1]).astype(BF16)
        act[...] = value
        packed[...] = nn(value, weight[...]).astype(BF16)

    parts = [part for pair in held for part in pair]
    return pl.pallas_call(
        body,
        grid_spec=pltpu.PrefetchScalarGridSpec(
            num_scalar_prefetch=1,
            grid=(length // block,),
            in_specs=[pl.BlockSpec((block, width), lambda i, t: (i, 0)), whole(mods.shape)]
            + [whole(part.shape) for part in parts],
            out_specs=[
                pl.BlockSpec((block, width), lambda i, t: (i, 0)),
                pl.BlockSpec((block, wide), lambda i, t: (i, 0)),
                whole_out((depth, wide)),
                whole_out((depth, width)),
            ],
        ),
        out_shape=[
            jax.ShapeDtypeStruct((length, width), BF16),
            jax.ShapeDtypeStruct((length, wide), BF16),
            jax.ShapeDtypeStruct((depth, wide), BF16),
            jax.ShapeDtypeStruct((depth, width), BF16),
        ],
        compiler_params=params(),
        cost_estimate=cost(2 * length * width * wide, 16 * MIB),
        name="space_project",
    )(table, tokens, mods, *parts)


def space_forward(packed, tokens, mods, bias, weight, patches, peers):
    length, width = tokens.shape
    frames = length // patches
    pairs = width // 128
    spots = patches // peers

    def body(packed, tokens, mods, bias, weight, heads, totals, branch, after):
        lanes = [key_lanes(bias[...], half) for half in range(2)]

        def step(pair, carry):
            at = pl.multiple_of(pair * 128, 128)
            parts = [packed[:, pl.ds(part * width + at, 128)] for part in range(3)]
            ((attended, logs),) = heads_forward([parts], lanes=lanes)
            heads[:, pl.ds(at, 128)] = attended
            totals[0, pair] = logs
            return carry

        lax.fori_loop(0, pairs, step, 0, unroll=2)
        product = nn(heads[...], weight[...])
        branch[...] = product.astype(BF16)
        result = (tokens[...].astype(F32) + mods[2:3] * product).astype(BF16)
        for peer in range(peers):
            after[peer, 0] = result[peer * spots : (peer + 1) * spots]

    def rows(columns):
        return pl.BlockSpec((patches, columns), lambda f: (f, 0))

    return pl.pallas_call(
        body,
        grid=(frames,),
        in_specs=[rows(3 * width), rows(width)]
        + [whole(a.shape) for a in (mods, bias, weight)],
        out_specs=[
            rows(width),
            pl.BlockSpec((1, pairs, 2, patches), lambda f: (f, 0, 0, 0)),
            rows(width),
            pl.BlockSpec((peers, 1, spots, width), lambda f: (0, f, 0, 0)),
        ],
        out_shape=[
            jax.ShapeDtypeStruct((length, width), BF16),
            jax.ShapeDtypeStruct((frames, pairs, 2, patches), F32),
            jax.ShapeDtypeStruct((length, width), BF16),
            jax.ShapeDtypeStruct((peers, frames, spots, width), BF16),
        ],
        compiler_params=params(),
        cost_estimate=cost(10e9, 10 * MIB, 6e6),
        name="space_forward",
    )(packed, tokens, mods, bias, weight)


def space_branch_back(grad_after, branch, heads, mods, weight, patches):
    peers, frames, spots, width = grad_after.shape
    length = frames * patches

    def body(grad_after, branch, heads, mods, weight, grad_branch, grad_heads, inner, grad_gate):
        upstream = grad_after[...].reshape(patches, width).astype(F32)
        value = (upstream * mods[2:3]).astype(BF16)
        grad_branch[...] = value
        grads = nt(value, weight[...]).astype(BF16)
        grad_heads[...] = grads
        rows = inner_sums(heads[...], grads)
        for pair in range(inner.shape[1]):
            inner[0, pair] = rows[2 * pair : 2 * pair + 2]

        @pl.when(pl.program_id(0) == 0)
        def _():
            grad_gate[...] = jnp.zeros_like(grad_gate)

        grad_gate[...] += column_sum(upstream * branch[...].astype(F32))

    return pl.pallas_call(
        body,
        grid=(frames,),
        in_specs=[
            pl.BlockSpec((peers, 1, spots, width), lambda f: (0, f, 0, 0)),
            pl.BlockSpec((patches, width), lambda f: (f, 0)),
            pl.BlockSpec((patches, width), lambda f: (f, 0)),
            whole(mods.shape),
            whole(weight.shape),
        ],
        out_specs=[
            pl.BlockSpec((patches, width), lambda f: (f, 0)),
            pl.BlockSpec((patches, width), lambda f: (f, 0)),
            pl.BlockSpec((1, width // 128, 2, patches), lambda f: (f, 0, 0, 0)),
            whole_out((1, width)),
        ],
        out_shape=[
            jax.ShapeDtypeStruct((length, width), BF16),
            jax.ShapeDtypeStruct((length, width), BF16),
            jax.ShapeDtypeStruct((frames, width // 128, 2, patches), F32),
            jax.ShapeDtypeStruct((1, width), F32),
        ],
        compiler_params=params(),
        cost_estimate=cost(2 * length * width * width, 8 * MIB),
        name="space_branch_back",
    )(grad_after, branch, heads, mods, weight)


def space_back(packed, grad_heads, totals, inner, bias, weight, tokens, grad_after, mods, patches):
    peers, frames, spots, width = grad_after.shape
    length = frames * patches
    pairs = width // 128

    def body(
        packed, grad_heads, totals, inner, bias, weight, tokens, grad_after, mods,
        grad_packed, grad_tokens, sums,
    ):
        lanes = [key_lanes(bias[...], half) for half in range(2)]

        def step(pair, carry):
            at = pl.multiple_of(pair * 128, 128)
            parts = [packed[:, pl.ds(part * width + at, 128)] for part in range(3)]
            rest = [grad_heads[:, pl.ds(at, 128)], totals[0, pair], inner[0, pair]]
            (results,) = heads_back([parts + rest], lanes=lanes)
            for part, result in enumerate(results):
                grad_packed[:, pl.ds(part * width + at, 128)] = result
            return carry

        lax.fori_loop(0, pairs, step, 0)

        @pl.when(pl.program_id(0) == 0)
        def _():
            sums[...] = jnp.zeros_like(sums)

        grad_act = nt(grad_packed[...], weight[...])
        normed, inverse = normalise(tokens[...].astype(F32))
        upstream = grad_after[...].reshape(patches, width).astype(F32)
        grad_tokens[...] = (
            upstream + norm_back(grad_act, normed, inverse, mods[1:2])
        ).astype(BF16)
        sums[0:1] += column_sum(grad_act)
        sums[1:2] += column_sum(grad_act * normed)

    def rows(columns):
        return pl.BlockSpec((patches, columns), lambda f: (f, 0))

    flat = jax.ShapeDtypeStruct((length, width), BF16)
    return pl.pallas_call(
        body,
        grid=(frames,),
        in_specs=[
            rows(3 * width),
            rows(width),
            pl.BlockSpec((1, pairs, 2, patches), lambda f: (f, 0, 0, 0)),
            pl.BlockSpec((1, pairs, 2, patches), lambda f: (f, 0, 0, 0)),
            whole(bias.shape),
            whole(weight.shape),
            rows(width),
            pl.BlockSpec((peers, 1, spots, width), lambda f: (0, f, 0, 0)),
            whole(mods.shape),
        ],
        out_specs=[rows(3 * width), rows(width), whole_out((2, width))],
        out_shape=[
            jax.ShapeDtypeStruct((length, 3 * width), BF16),
            flat,
            jax.ShapeDtypeStruct((2, width), F32),
        ],
        compiler_params=params(),
        cost_estimate=cost(24e9, 20 * MIB, 6e6),
        name="space_back",
    )(packed, grad_heads, totals, inner, bias, weight, tokens, grad_after, mods)


TILE = 16


def apart_bias():
    row = lax.broadcasted_iota(jnp.int32, (TILE, 128), 0)
    column = lax.broadcasted_iota(jnp.int32, (TILE, 128), 1)
    return jnp.where((row & (TILE - 1)) == (column & (TILE - 1)), 0.0, APART)


def part_cuts(pair, width):
    return [slice(p * width + 128 * pair, p * width + 128 * pair + 128) for p in range(3)]


def time_forward(after, mods, table, own, other):
    frames, spots, width = after.shape
    depth = own.shape[0] * own.shape[1] * 2
    block = frames * TILE
    length = frames * spots
    pairs = width // 128

    def body(table, after, mods, own, other, act, packed, heads, branch, totals, time_in, time_out):
        @pl.when(pl.program_id(0) == 0)
        def _():
            build(
                table, 0, own, other, [(0, 3 * width, time_in, 0), (3 * width, width, time_out, 0)]
            )

        apart = apart_bias()
        normed, _ = normalise(after[...].reshape(block, width).astype(F32))
        value = (normed * (1.0 + mods[4:5]) + mods[3:4]).astype(BF16)
        act[...] = value
        packed[...] = nn(value, time_in[...]).astype(BF16)
        parts = [[packed[:, cut] for cut in part_cuts(pair, width)] for pair in range(pairs)]
        for pair, (attended, logs) in enumerate(heads_forward(parts, apart)):
            heads[:, 128 * pair : 128 * pair + 128] = attended
            totals[0, pair] = logs
        branch[...] = nn(heads[...], time_out[...])

    def rows(columns):
        return pl.BlockSpec((block, columns), lambda i, t: (i, 0))

    return pl.pallas_call(
        body,
        grid_spec=pltpu.PrefetchScalarGridSpec(
            num_scalar_prefetch=1,
            grid=(spots // TILE,),
            in_specs=[pl.BlockSpec((frames, TILE, width), lambda i, t: (0, i, 0))]
            + [whole(a.shape) for a in (mods, own, other)],
            out_specs=[
                rows(width),
                rows(3 * width),
                rows(width),
                rows(width),
                pl.BlockSpec((1, pairs, 2, block), lambda i, t: (i, 0, 0, 0)),
                whole_out((depth, 3 * width)),
                whole_out((depth, width)),
            ],
        ),
        out_shape=[
            jax.ShapeDtypeStruct((length, width), BF16),
            jax.ShapeDtypeStruct((length, 3 * width), BF16),
            jax.ShapeDtypeStruct((length, width), BF16),
            jax.ShapeDtypeStruct((length, width), F32),
            jax.ShapeDtypeStruct((spots // TILE, pairs, 2, block), F32),
            jax.ShapeDtypeStruct((depth, 3 * width), BF16),
            jax.ShapeDtypeStruct((depth, width), BF16),
        ],
        compiler_params=params(),
        cost_estimate=cost(8e9, 24 * MIB, 3e6),
        name="time_forward",
    )(table, after, mods, own, other)


def middle(
    after, grad_out, packed, heads, time_branch, totals, mods, first_bias, second_bias, time_in,
    time_out, mlp_full, share,
):
    frames, spots, width = after.shape
    hidden_width = first_bias.shape[1]
    depth = mlp_full.shape[0]
    count = depth // share
    block = frames * TILE
    length = frames * spots
    pairs = width // 128
    chunks = hidden_width // width
    slope = math.sqrt(2.0 / math.pi)

    def body(
        after, grad_out, packed, heads, time_branch, totals,
        mods, first_bias, second_bias, time_in, time_out, first, shares,
        out, grad_after, mlp_act, hidden, grad_second, grad_pre, grad_branch, grad_packed,
        sums, bias_sums, derived, second,
    ):
        @pl.when(pl.program_id(0) == 0)
        def _():
            def unpack(i, carry):
                piece = shares[i].astype(F32)
                parts = [piece[:, c * width : (c + 1) * width] for c in range(chunks)]
                rows = pl.ds(pl.multiple_of(i * chunks * share, chunks * share), chunks * share)
                second[rows] = jnp.concatenate(parts, axis=0).astype(BF16)
                return carry

            lax.fori_loop(0, count, unpack, 0)
            sums[...] = jnp.zeros_like(sums)
            bias_sums[...] = jnp.zeros_like(bias_sums)

        current = after[...].reshape(block, width).astype(F32)
        after_time = current + mods[5:6] * time_branch[...]
        mlp_norm, mlp_inverse = normalise(after_time)
        act = (mlp_norm * (1.0 + mods[7:8]) + mods[6:7]).astype(BF16)
        mlp_act[...] = act
        mlp_branch = 0.0
        for chunk in range(chunks):
            cut = slice(width * chunk, width * chunk + width)
            pre = nn(act, first[:, cut]) + first_bias[:, cut]
            squared = pre * pre
            bent = jnp.tanh(slope * pre * (1.0 + 0.044715 * squared))
            half = 0.5 * (1.0 + bent)
            value = (pre * half).astype(BF16)
            hidden[:, cut] = value
            derived[:, cut] = half + 0.5 * slope * pre * (1.0 - bent * bent) * (
                1.0 + 3.0 * 0.044715 * squared
            )
            mlp_branch += nn(value, second[cut])
        mlp_branch += second_bias[...]
        out[...] = (after_time + mods[8:9] * mlp_branch).astype(BF16).reshape(frames, TILE, width)

        upstream = grad_out[...].reshape(block, width).astype(F32)
        sums[5:6] += column_sum(upstream * mlp_branch)
        grad_value = (upstream * mods[8:9]).astype(BF16)
        grad_second[...] = grad_value
        bias_sums[:, hidden_width:] += column_sum(grad_value.astype(F32))
        grad_act = 0.0
        for chunk in range(chunks):
            cut = slice(width * chunk, width * chunk + width)
            value = (nt(grad_value, second[cut]) * derived[:, cut]).astype(BF16)
            grad_pre[:, cut] = value
            bias_sums[:, cut] += column_sum(value.astype(F32))
            grad_act += nt(value, first[:, cut])
        sums[3:4] += column_sum(grad_act)
        sums[4:5] += column_sum(grad_act * mlp_norm)
        upstream = upstream + norm_back(grad_act, mlp_norm, mlp_inverse, mods[7:8])

        sums[2:3] += column_sum(upstream * time_branch[...])
        grad_value = (upstream * mods[5:6]).astype(BF16)
        grad_branch[...] = grad_value
        grad_heads = nt(grad_value, time_out[...]).astype(BF16)
        apart = apart_bias()
        inner = inner_sums(heads[...], grad_heads)
        parts = []
        for pair in range(pairs):
            cuts = part_cuts(pair, width)
            parts.append(
                [packed[:, cut] for cut in cuts]
                + [grad_heads[:, cuts[0]], totals[0, pair], inner[2 * pair : 2 * pair + 2]]
            )
        for pair, results in enumerate(heads_back(parts, apart)):
            for cut, part in zip(part_cuts(pair, width), results):
                grad_packed[:, cut] = part
        grad_act = nt(grad_packed[...], time_in[...]).astype(BF16).astype(F32)
        time_norm, time_inverse = normalise(current)
        sums[0:1] += column_sum(grad_act)
        sums[1:2] += column_sum(grad_act * time_norm)
        upstream = upstream + norm_back(grad_act, time_norm, time_inverse, mods[4:5])
        grad_after[...] = upstream.astype(BF16).reshape(frames, TILE, width)

    moving = pl.BlockSpec((frames, TILE, width), lambda i: (0, i, 0))

    def rows(columns):
        return pl.BlockSpec((block, columns), lambda i: (i, 0))

    def array(columns):
        return jax.ShapeDtypeStruct((length, columns), BF16)

    narrow, wide, triple = width, hidden_width, 3 * width
    kept = [narrow, wide, narrow, wide, narrow, triple]
    held = (mods, first_bias, second_bias, time_in, time_out)
    shares = mlp_full.reshape(count, share, 2 * hidden_width)
    return pl.pallas_call(
        body,
        grid=(spots // TILE,),
        in_specs=[moving, moving, rows(triple), rows(width), rows(width)]
        + [pl.BlockSpec((1, pairs, 2, block), lambda i: (i, 0, 0, 0))]
        + [whole(a.shape) for a in held]
        + [
            pl.BlockSpec((depth, hidden_width), lambda i: (0, 0), pipeline_mode=pl.Buffered(1)),
            pl.BlockSpec(
                (count, share, hidden_width), lambda i: (0, 0, 1), pipeline_mode=pl.Buffered(1)
            ),
        ],
        out_specs=[moving, moving]
        + [rows(c) for c in kept]
        + [whole_out((8, width)), whole_out((1, hidden_width + width))],
        out_shape=[jax.ShapeDtypeStruct(after.shape, BF16)] * 2
        + [array(c) for c in kept]
        + [
            jax.ShapeDtypeStruct((8, width), F32),
            jax.ShapeDtypeStruct((1, hidden_width + width), F32),
        ],
        scratch_shapes=[
            pltpu.VMEM((block, hidden_width), F32),
            pltpu.VMEM((hidden_width, width), BF16),
        ],
        compiler_params=params(60),
        cost_estimate=cost(40e9, 50 * MIB, 8e6),
        name="middle",
    )(after, grad_out, packed, heads, time_branch, totals, *held, mlp_full, shares)


def local(
    count,
    tokens,
    condition,
    patch_mask,
    grad_out,
    mod_weight,
    mod_bias,
    space_qkv,
    space_proj,
    time_qkv,
    time_proj,
    mlp_in,
    in_bias,
    mlp_out,
    out_bias,
):
    length, width = tokens.shape
    patches = patch_mask.shape[1]
    frame_dev = length // patches
    groups = condition.shape[0]
    clip_dev = FRAMES // frame_dev
    spots = patches // clip_dev
    sp_size = lax.axis_size("sp")
    shard = mod_weight.shape[0]
    mod_width = mod_weight.shape[1]
    hidden_width = mlp_in.shape[1]
    me = lax.axis_index("dp") * sp_size + lax.axis_index("sp")
    chip = me // 2
    core = me % 2
    clip_row = lax.axis_index("sp") // clip_dev
    order_a, order_b = chip_orders(count)
    teams = [list(range(s, s + clip_dev)) for s in range(0, sp_size, clip_dev)]

    def across(values):
        return lax.all_to_all(
            values, "sp", split_axis=0, concat_axis=0, tiled=True, axis_index_groups=teams
        )

    near = jnp.stack([condition[clip_row ^ s] for s in range(groups)])
    mask = sp_size
    while mask < count:
        near = jnp.concatenate([near, swap(near, mask, count)], axis=0)
        mask *= 2
    lifted = jax.nn.silu(near.astype(F32)).astype(BF16)
    lifted_rows = lax.dynamic_slice_in_dim(lifted, me * shard, shard, 1)
    part = jnp.dot(lifted_rows, mod_weight, preferred_element_type=F32)
    own = jnp.zeros((mod_width + hidden_width + width,), F32)
    own = lax.dynamic_update_slice(own, mod_bias.astype(F32), (me * mod_bias.shape[0],))
    own = lax.dynamic_update_slice(
        own, in_bias.astype(F32), (mod_width + me * in_bias.shape[0],)
    )
    own = lax.dynamic_update_slice(
        own, out_bias.astype(F32), (mod_width + hidden_width + me * out_bias.shape[0],)
    )
    row = jnp.pad(part, ((0, 0), (0, hidden_width + width))) + own[None]

    def row_halved(row, mask):
        half = row.shape[0] // 2
        return row[:half] + swap(row[half:], mask, count)

    def row_added(row, mask):
        return row + swap(row, mask, count)

    row_steps = []
    mask = count // 2
    while mask:
        row_steps.append(functools.partial(row_halved if mask >= clip_dev else row_added, mask=mask))
        mask //= 2

    hidden_share = mlp_out.shape[0] // shard
    if shard % 8:
        mlp_share = 8
        full = lax.all_gather(mlp_out, AXES, axis=0, tiled=True)
        full = full.reshape(-1, hidden_share, mlp_share, width)
        full = jnp.transpose(full, (0, 2, 1, 3)).reshape(-1, hidden_width)
        mlp_full = jnp.concatenate([lax.all_gather(mlp_in, AXES, axis=0, tiled=True), full], axis=1)
    else:
        mlp_share = shard
        packed_out = [mlp_out[i * shard : (i + 1) * shard] for i in range(hidden_share)]
        mlp_full = lax.all_gather(
            jnp.concatenate([mlp_in] + packed_out, axis=1), AXES, axis=0, tiled=True
        )
    cut = (space_qkv.shape[1] + width) // 2
    wanted = [
        space_qkv[:, :cut],
        jnp.concatenate([space_qkv[:, cut:], space_proj], axis=1),
        jnp.concatenate([time_qkv, time_proj], axis=1),
    ]
    if shard % 8:
        held = []
        for part in wanted:
            full = lax.all_gather(part, AXES, axis=0, tiled=True).reshape(-1, 2, 8, part.shape[1])
            held.append((full[:, 0], full[:, 1]))
        time_held = held.pop()
        spots_held = held[0][0].shape[0]
        table = jnp.stack(
            [jnp.arange(spots_held, dtype=jnp.int32)] * 2 + [jnp.zeros((spots_held,), jnp.int32)]
        )
        time_steps = []
    else:
        time_steps = list(order_a)
        time_own = wanted[2][None]

        def time_step(value):
            nonlocal time_own
            got = swap(time_own, time_steps.pop(0), count)
            value, got, time_own = lax.optimization_barrier((value, got, time_own))
            value, time_own = lax.optimization_barrier(
                (value, jnp.concatenate([time_own, got], axis=0))
            )
            return value

        one, two = wanted[0][None], wanted[1][None]
        for step, (mask_a, mask_b) in enumerate(zip(order_a, order_b)):
            if step >= 2 and len(time_steps) > 2:
                one = time_step(one)
            got = swap(one, mask_a, count), swap(two, mask_b, count)
            one = jnp.concatenate([one, got[0]], axis=0)
            two = jnp.concatenate([two, got[1]], axis=0)
            for _ in range(min(step, 2)):
                if len(row_steps) > 1:
                    row = row_steps.pop(0)(row)
            one, two, row = lax.optimization_barrier((one, two, row))
        held = [(one, swap(one, 1, count)), (two, swap(two, 1, count))]
        table = place_table((order_a, order_b), chip, core, count)

    while row_steps:
        row = row_steps.pop(0)(row)
    mods = row[0, :mod_width].reshape(9, width)
    first_bias = row[:, mod_width : mod_width + hidden_width]
    second_bias = row[:, mod_width + hidden_width :]

    mask_row = lax.dynamic_index_in_dim(patch_mask, clip_row, 0, keepdims=False)
    key_bias = jnp.where(mask_row == 1, 0.0, MASKED).astype(F32)[:, None]
    space_act, space_packed, space_full, space_out = space_project(tokens, mods, table, held)
    if time_steps:
        space_packed = time_step(space_packed)
    space_heads, space_total, space_branch, after_space = space_forward(
        space_packed, tokens, mods, key_bias, space_out, patches, clip_dev
    )
    if time_steps:
        after_space = time_step(after_space)
    after_here = across(after_space)
    if shard % 8 == 0:
        time_held = time_own, swap(time_own, 1, count)

    shape = (clip_dev, frame_dev, spots, width)
    flat_shape = (FRAMES, spots, width)
    grad_here = jnp.transpose(grad_out.reshape(frame_dev, clip_dev, spots, width), (1, 0, 2, 3))
    after_here, time_held, grad_here = lax.optimization_barrier((after_here, time_held, grad_here))
    after_here = after_here.reshape(flat_shape)
    grad_here = across(grad_here)
    times = time_forward(after_here, mods, table, *time_held)
    times, grad_here = lax.optimization_barrier((times, grad_here))
    time_act, time_packed, time_heads, time_branch, time_total, time_full, time_out = times
    (
        out_here,
        grad_here,
        mlp_act,
        hidden,
        grad_second,
        grad_pre,
        grad_time_branch,
        grad_time_packed,
        sums,
        bias_sums,
    ) = middle(
        after_here,
        grad_here.reshape(flat_shape),
        time_packed,
        time_heads,
        time_branch,
        time_total,
        mods,
        first_bias,
        second_bias,
        time_full,
        time_out,
        mlp_full,
        mlp_share,
    )

    turn_a, turn_b = order_a[::-1], order_b[::-1]
    turn_e = [turn_a[i] for i in (0, 2, 1)] + turn_a[3:]
    turn_t = [turn_a[i] for i in (2, 1, 0)] + turn_a[3:]

    def reduced(*sheets, deep=None):
        return weight_grads(sheets, chip, core, count, shard, width, deep)

    grad_after = across(grad_here.reshape(shape))
    wide = hidden_width // width
    shares = reduced(
        ([(mlp_act, grad_pre, 0, wide)], turn_b), deep=(hidden, grad_second, turn_e)
    )
    shares, grad_after, time_act, out_here = lax.optimization_barrier(
        (shares, grad_after, time_act, out_here)
    )
    out_back = across(out_here.reshape(shape))
    fold_a, fold_e = Fold(shares[:2], turn_b, count), Fold(shares[2:], turn_e, count)
    shares = reduced(
        ([(time_act, grad_time_packed, 0, 3), (time_heads, grad_time_branch, 0, 1)], turn_t)
    )
    shares, grad_after, out_back = meet((shares, grad_after, out_back), fold_a, fold_e)
    fold_b = Fold(shares, turn_t, count)
    grad_space_branch, grad_space_heads, inner, grad_gate = meet(
        space_branch_back(grad_after, space_branch, space_heads, mods, space_out, patches), fold_b
    )
    grads = space_back(
        space_packed,
        grad_space_heads,
        space_total,
        inner,
        key_bias,
        space_full,
        tokens,
        grad_after,
        mods,
        patches,
    )
    grad_space_packed, grad_tokens, space_sums, grad_gate = meet(
        (*grads, grad_gate), fold_a, fold_e, fold_b
    )
    out_tokens = jnp.transpose(out_back, (1, 0, 2, 3)).reshape(length, width)
    rows = jnp.concatenate(
        [space_sums.reshape(1, -1), grad_gate, sums[:6].reshape(1, -1), bias_sums], axis=1
    )
    mask = clip_dev // 2
    got = swap(rows, mask, count)
    shares = reduced(
        ([(space_heads, grad_space_branch, 0, 1), (space_act, grad_space_packed, 0, 1)], turn_a),
        ([(space_act, grad_space_packed, 1, 2)], turn_b),
    )
    shares, rows, got = meet((shares, rows, got), fold_a, fold_e, fold_b)
    fold_c, fold_d = Fold(shares[:2], turn_a, count), Fold(shares[2:], turn_b, count)
    rounds = [(fold_c, fold_d), (fold_a, fold_e, fold_b)]
    while mask:
        rows = rows + got
        mask //= 2
        if mask:
            got = swap(rows, mask, count)
            rows, got = meet((rows, got), *rounds.pop(0)) if rounds else (rows, got)
    mask = clip_dev
    while mask < count:
        got = swap(rows, mask, count)
        if mask == clip_dev:
            rows, got = meet((rows, got), fold_c, fold_d)
        rows = jnp.concatenate([rows, got], axis=0)
        mask *= 2
    while len(fold_a.masks) > 1:
        rows = meet(rows, fold_a, fold_e, fold_b)
    grad_a, grad_b, grad_mlp_out = fold_a.finish(), fold_b.finish(), fold_e.finish()
    if len(fold_c.masks) > 1:
        rows = meet(rows, fold_c, fold_d)
    grad_rows = rows[:, :mod_width]
    grad_lifted = lax.dot_general(
        grad_rows,
        mod_weight.astype(F32),
        (((1,), (1,)), ((), ())),
        precision=lax.Precision.HIGHEST,
        preferred_element_type=F32,
    )
    near_clips = jnp.arange(count // clip_dev) ^ (me // clip_dev)
    grad_lifted = jnp.take(grad_lifted, near_clips, axis=0)
    grad_lifted = jnp.repeat(
        grad_lifted.reshape(count // sp_size, 1, groups * shard), sp_size, axis=1
    ).reshape(count, groups * shard)
    if len(fold_c.masks) > 1:
        grad_lifted = meet(grad_lifted, fold_c, fold_d)
    grad_lifted = lax.all_to_all(grad_lifted, AXES, split_axis=0, concat_axis=0, tiled=True)
    while len(fold_d.masks) > 1:
        grad_a, grad_b = meet(
            (grad_a, grad_b), *[fold for fold in (fold_c, fold_d) if len(fold.masks) > 1]
        )
    grad_c, grad_d = fold_c.finish(), fold_d.finish()
    grad_mlp_in = grad_a
    grad_time_qkv = grad_b[:, : 3 * width]
    grad_time_proj = grad_b[:, 3 * width :]
    grad_space_proj = grad_c[:, :width]
    grad_space_qkv = jnp.concatenate([grad_c[:, width:], grad_d], axis=1)

    grad_mod_weight = lax.dot_general(
        lifted_rows.astype(F32),
        grad_rows,
        (((0,), (0,)), ((), ())),
        precision=lax.Precision.HIGHEST,
        preferred_element_type=F32,
    )
    totals = jnp.sum(rows, axis=0)
    grad_mod_bias = lax.dynamic_slice_in_dim(totals, me * mod_bias.shape[0], mod_bias.shape[0])
    grad_in_bias = lax.dynamic_slice_in_dim(
        totals, mod_width + me * in_bias.shape[0], in_bias.shape[0]
    )
    grad_out_bias = lax.dynamic_slice_in_dim(
        totals, mod_width + hidden_width + me * out_bias.shape[0], out_bias.shape[0]
    )
    grad_lifted = jnp.transpose(grad_lifted.reshape(count, groups, shard), (1, 0, 2))
    grad_lifted = grad_lifted.reshape(groups, width)
    _, silu_back = jax.vjp(jax.nn.silu, condition.astype(F32))
    grad_condition = silu_back(grad_lifted)[0]

    return (
        out_tokens,
        grad_tokens,
        grad_condition,
        grad_mod_weight,
        grad_mod_bias,
        grad_space_qkv,
        grad_space_proj,
        grad_time_qkv,
        grad_time_proj,
        grad_mlp_in,
        grad_in_bias,
        grad_mlp_out,
        grad_out_bias,
    )


def solution(mesh):
    count = mesh.shape["dp"] * mesh.shape["sp"]
    both = P(AXES, None)
    flat = P(AXES)
    clips = P("dp", None)
    return jax.shard_map(
        functools.partial(local, count),
        mesh=mesh,
        in_specs=(
            both, clips, clips, both, both, flat, both, both, both, both, both, flat, both, flat,
        ),
        out_specs=(
            both, both, clips, both, flat, both, both, both, both, both, flat, both, flat,
        ),
        check_vma=False,
    )
```
